128 devices in a mesh: seq: 64 (over z, x, y), tp: 2 (over core).
Axes of the slice: x: 4, y: 4, z: 4, core: 2. Of those that a mesh axis runs over, the one named last changes fastest.
Arguments:
- hidden_in: bfloat16 [16384, 1536], P('seq'), may hold values from -6 to 6
- gate_proj: float32 [1536, 3072], P(('seq', 'tp')), may hold values from -0.15625 to 0.15625
- inner_proj: float32 [1536, 3072], P(('seq', 'tp')), may hold values from -0.15625 to 0.15625
- small_proj: float32 [1536, 304], P(('seq', 'tp')), may hold values from -0.15625 to 0.15625
- row_layout: int32 [128], replicated, may hold values from 0 to 127, each once
- conv_inner: float32 [4, 3072], P(None, 'tp'), may hold values from -3 to 3
- conv_shared: float32 [4, 256], replicated, may hold values from -3 to 3
- bias_inner: float32 [3072], P('tp'), may hold values from -3 to 3
- bias_shared: float32 [256], replicated, may hold values from -3 to 3
- dt_bias: float32 [48], P('tp'), may hold values from -4 to -1
- decay_log: float32 [48], P('tp'), may hold values from -8 to 0
- skip_gain: float32 [48], P('tp'), may hold values from 0.5 to 2
- norm_gain: float32 [3072], P('tp'), may hold values from 0.1 to 1.9
- out_proj: float32 [3072, 1536], P('tp', 'seq'), may hold values from -0.109375 to 0.109375
- prompt_lengths: int32 [8], replicated, may hold values from 1 to 8192, 16384 in all
- group_map: int32 [8], replicated, may hold values from 0 to 3
- init_states: float32 [4, 48, 64, 128], P(None, 'tp'), may hold values from -12 to 12
- page_table: int32 [128], P('seq'), may hold values from 0 to 127, as said below
Outputs:
- mixed_out: bfloat16 [16384, 1536], P(('seq', 'tp'))
- state_pages: float32 [128, 48, 64, 128], P('seq', 'tp')
The draws below stay inside these ranges and needn't reach their ends.
Inputs may be any that keep to these rules, and one draw needn't show every extreme that they name: `prompt_lengths`: the lengths sum to 16384; the longest prompt has exactly 8192 tokens. `row_layout`: a permutation. `page_table`: no two snapshots share a slot; snapshot k goes to one of the 2 slots of the aligned block of 2 snapshots that holds k.
All inputs are finite; a program needn't handle non-finite values.
Results may differ from the reference program's by a relative error of at most 0.018.
Values may be sent and summed in bfloat16 or wider, within the bound.
A program may use at most 192 MiB of HBM per device.

```python
import math
import jax
import jax.numpy as jnp
import numpy as np
from jax import lax

D = 1536
H = 48
P_SIZE = 64
N = 128
CONV = 4
PAGE = 128
GROUPS = 4
PROMPTS = 8
DI = 3072
TOKENS = 16384
MOST = 8192
PAGE_DEV = 2
PAGES = 128
BLOCKS = 128


def draw_page_table(key, part):
    block_count = PAGES // PAGE_DEV
    keys = jax.random.split(jax.random.fold_in(key, 17), block_count)
    orders = jax.vmap(lambda one_key: jax.random.permutation(one_key, PAGE_DEV))(keys)
    base = jnp.arange(block_count, dtype=jnp.int32)[:, None] * PAGE_DEV
    return (orders.astype(jnp.int32) + base).reshape(PAGES).astype(jnp.int32)


def set_ends(array, rng, smallest, top_value):
    spot = [jax.random.randint(jax.random.fold_in(rng, axis), (), 0, length) for axis, length in enumerate(array.shape)]
    main_axis = array.shape.index(max(array.shape))
    neighbour = spot[:main_axis] + [(spot[main_axis] + 1) % array.shape[main_axis]] + spot[main_axis + 1:]
    return array.at[tuple(spot)].set(smallest).at[tuple(neighbour)].set(top_value)


def levels(key, extent, cuts, least, largest):
    factor_of = 1.0
    for dim, blocks in cuts:
        draws = jax.random.uniform(jax.random.fold_in(jax.random.fold_in(key, 6), dim), (blocks,), jnp.float32, least / len(cuts), largest / len(cuts))
        factor_of = factor_of * jnp.repeat(jnp.exp(draws), extent[dim] // blocks).reshape((-1,) + (1,) * (len(extent) - 1 - dim))
    return factor_of


def split_up(count, total, bound, skew):
    portions = [(1 << 20) // math.isqrt(rank ** skew) + 1 for rank in range(2, count + 1)]
    rest, given = total - bound - (count - 1), [1] * (count - 1)
    while rest > 0:
        free = [i for i in range(count - 1) if given[i] < bound]
        whole, budget = sum([portions[i] for i in free]), rest
        for i in free:
            extra = min(bound - given[i], max(1, budget * portions[i] // whole), rest)
            given[i] = given[i] + extra
            rest = rest - extra
    return np.array([bound] + given)


def ragged(stream_key, number_of, total, reach, lean):
    if number_of == 2:
        one = jax.random.randint(stream_key, (), max(1, total - reach), min(reach, total - 1) + 1)
        return jnp.stack([one, total - one])
    sizes = jnp.asarray(split_up(number_of, total, reach, lean), jnp.int32)
    pairs = (number_of - 1) // 2
    giver, taker = sizes[1:1 + 2 * pairs:2], sizes[2:2 + 2 * pairs:2]
    room = jnp.minimum(giver - 1, reach - taker)
    shifted = jax.random.randint(jax.random.fold_in(stream_key, 1), (pairs,), 0, 1 << 20) % (room + 1)
    sizes = sizes.at[1:1 + 2 * pairs:2].set(giver - shifted).at[2:2 + 2 * pairs:2].set(taker + shifted)
    return sizes[jax.random.permutation(jax.random.fold_in(stream_key, 2), number_of)]


def centred(key, dims, scale, most, cuts=(), held_as=jnp.bfloat16):
    array = jax.random.normal(key, dims, jnp.float32) * scale
    if len(cuts) > 0:
        array = levels(key, dims, cuts, -0.22, 0.18) * array
    return jnp.clip(array, min=-most, max=most).astype(held_as)


def setup_inputs(seed: int = 0) -> dict:
    seeds = jax.random.split(jax.random.key(seed), 19)
    return {
        "hidden_in": centred(seeds[0], (TOKENS, D), 1.0, 6.0, ((0, 64),)),
        "gate_proj": centred(seeds[1], (D, DI), D ** -0.5, 0.15625, ((0, 128),), jnp.float32),
        "inner_proj": centred(seeds[2], (D, DI), D ** -0.5, 0.15625, ((0, 128),), jnp.float32),
        "small_proj": centred(seeds[3], (D, 2 * N + H), D ** -0.5, 0.15625, ((0, 128),), jnp.float32),
        "row_layout": jax.random.permutation(seeds[4], BLOCKS).astype(jnp.int32),
        "conv_inner": centred(seeds[5], (CONV, DI), CONV ** -0.5, 3.0, ((1, 2),), jnp.float32),
        "conv_shared": centred(seeds[6], (CONV, 2 * N), CONV ** -0.5, 3.0, (), jnp.float32),
        "bias_inner": centred(seeds[7], (DI,), 0.5, 3.0, ((0, 2),), jnp.float32),
        "bias_shared": centred(seeds[8], (2 * N,), 0.5, 3.0, (), jnp.float32),
        "dt_bias": jnp.clip(-4.0 + 3.0 * jax.random.uniform(seeds[9], (H,), jnp.float32) ** levels(seeds[9], (H,), ((0, 2),), -0.2, 0.2), -4.0, -1.0),
        "decay_log": jnp.clip(-8.0 + 8.0 * jax.random.uniform(seeds[10], (H,), jnp.float32) ** levels(seeds[10], (H,), ((0, 2),), -0.2, 0.2), -8.0, 0.0),
        "skip_gain": jnp.clip(0.5 + 1.5 * jax.random.uniform(seeds[11], (H,), jnp.float32) ** levels(seeds[11], (H,), ((0, 2),), -0.2, 0.2), 0.5, 2.0),
        "norm_gain": jnp.clip(1.0 + 0.18 * jax.random.normal(seeds[12], (DI,), jnp.float32), 0.1, 1.9),
        "out_proj": centred(seeds[13], (DI, D), DI ** -0.5, 0.109375, ((0, 2), (1, 64)), jnp.float32),
        "prompt_lengths": ragged(seeds[14], PROMPTS, TOKENS, MOST, 2).astype(jnp.int32),
        "group_map": set_ends(jax.random.randint(seeds[15], (PROMPTS,), 0, GROUPS), jax.random.fold_in(seeds[15], 1), 0, GROUPS - 1).astype(jnp.int32),
        "init_states": centred(seeds[16], (GROUPS, H, P_SIZE, N), 2.0, 12.0, ((1, 2),), jnp.float32),
        "page_table": draw_page_table(jax.random.fold_in(seeds[18], 71), 0),
    }


epsilon = 1e-05

def token_meta(positions, lengths, groups, group_count):
    starts = jnp.cumsum(lengths) - lengths
    prompt_id = lax.optimization_barrier(jnp.sum((starts[None, :] <= positions[:, None]).astype(jnp.int32), axis=1)) - 1
    prompt_hot = prompt_id[:, None] == jnp.arange(lengths.shape[0], dtype=jnp.int32)[None, :]
    first_pos = lax.optimization_barrier(jnp.sum(jnp.where(prompt_hot, starts[None, :], 0), axis=1))
    group_id = lax.optimization_barrier(jnp.sum(jnp.where(prompt_hot, groups[None, :], 0), axis=1))
    group_hot = (group_id[:, None] == jnp.arange(group_count, dtype=jnp.int32)[None, :]).astype(jnp.float32)
    offset = positions - first_pos
    is_start = (offset == 0).astype(jnp.float32)
    return (prompt_id, offset, is_start, group_hot)

def conv_apply(source, edges, taps, conv_bias, offset):
    padded = jnp.concatenate([edges, source], axis=0).astype(jnp.float32)
    total_rows = source.shape[0]
    width = taps.shape[0]
    result = conv_bias[None, :] + jnp.zeros((total_rows, source.shape[1]), jnp.float32)
    for lag_index in range(width):
        within = (offset >= lag_index).astype(jnp.float32)[:, None]
        lo_row = width - 1 - lag_index
        result = result + taps[lag_index][None, :] * padded[lo_row:lo_row + total_rows] * within
    return jax.nn.silu(result)

def span_terms(x_span, b_span, c_span, dt_span, log_span, pid_span, start_span, group_span, init_states, skip_gain):
    highest = lax.Precision.HIGHEST
    length = x_span.shape[0]
    cumulative = jnp.cumsum(log_span, axis=0)
    before_log = cumulative - log_span
    slots = jnp.arange(length, dtype=jnp.int32)
    causal = (slots[:, None] >= slots[None, :]) & (pid_span[:, None] == pid_span[None, :])
    within = causal[:, :, None]
    decays = jnp.where(within, jnp.exp(jnp.where(within, cumulative[:, None, :] - cumulative[None, :, :], 0.0)), 0.0)
    scores = jnp.dot(c_span, b_span.T, precision=highest)
    mixing = decays * dt_span[None, :, :] * scores[:, :, None]
    y_part = jnp.einsum('tsh,shp->thp', mixing, x_span, precision=highest)
    opening = jnp.where(within, jnp.exp(jnp.where(within, cumulative[:, None, :] - before_log[None, :, :], 0.0)), 0.0)
    opening = lax.optimization_barrier(jnp.sum(opening * start_span[None, :, None], axis=1))
    read_init = jnp.einsum('tn,ghpn->tghp', c_span, init_states, precision=highest)
    read_init = jnp.einsum('tg,tghp->thp', group_span, read_init, precision=highest)
    y_part = y_part + opening[:, :, None] * read_init + skip_gain[None, :, None] * x_span
    weights_last = decays[length - 1] * dt_span
    summary = jnp.einsum('sh,shp,sn->hpn', weights_last, x_span, b_span, precision=highest)
    init_last = jnp.einsum('g,ghpn->hpn', group_span[length - 1], init_states, precision=highest)
    summary = summary + opening[length - 1][:, None, None] * init_last
    alive_mask = (pid_span == pid_span[0]).astype(jnp.float32) * (1.0 - start_span[0])
    carried = alive_mask[:, None] * jnp.exp(cumulative)
    return (y_part, summary, carried[length - 1], carried)

def unpermute(stored, row_layout):
    block_count = row_layout.shape[0]
    block_rows = stored.shape[0] // block_count
    blocks = stored.astype(jnp.bfloat16).reshape(block_count, block_rows, stored.shape[1])
    return jnp.zeros_like(blocks).at[row_layout].set(blocks).reshape(stored.shape)

def reference(hidden_in, gate_proj, inner_proj, small_proj, row_layout, conv_inner, conv_shared, bias_inner, bias_shared, dt_bias, decay_log, skip_gain, norm_gain, out_proj, prompt_lengths, group_map, init_states, page_table):
    highest = lax.Precision.HIGHEST
    gate_val = jnp.dot(hidden_in, unpermute(gate_proj, row_layout), preferred_element_type=jnp.float32).astype(jnp.bfloat16)
    inner_val = jnp.dot(hidden_in, unpermute(inner_proj, row_layout), preferred_element_type=jnp.float32).astype(jnp.bfloat16)
    shared_val = jnp.dot(hidden_in, unpermute(small_proj, row_layout), preferred_element_type=jnp.float32).astype(jnp.bfloat16)
    shared_bc = shared_val[:, :2 * N]
    dt_raw = shared_val[:, 2 * N:]
    positions = jnp.arange(TOKENS, dtype=jnp.int32)
    prompt_id, offset, is_start, group_hot = token_meta(positions, prompt_lengths, group_map, GROUPS)
    x_conv = conv_apply(inner_val, jnp.zeros((CONV - 1, DI), jnp.bfloat16), conv_inner, bias_inner, offset)
    bc_conv = conv_apply(shared_bc, jnp.zeros((CONV - 1, 2 * N), jnp.bfloat16), conv_shared, bias_shared, offset)
    dt_val = jax.nn.softplus(dt_raw.astype(jnp.float32) + dt_bias[None, :])
    log_rate = -jnp.exp(decay_log)[None, :] * dt_val
    spans = TOKENS // PAGE
    items = (x_conv.reshape(spans, PAGE, H, P_SIZE), bc_conv[:, :N].reshape(spans, PAGE, N), bc_conv[:, N:].reshape(spans, PAGE, N), dt_val.reshape(spans, PAGE, H), log_rate.reshape(spans, PAGE, H), prompt_id.reshape(spans, PAGE), is_start.reshape(spans, PAGE), group_hot.reshape(spans, PAGE, GROUPS))

    def advance(running, span_items):
        y_part, summary, decays, carried = span_terms(*span_items, init_states, skip_gain)
        y_part = y_part + carried[:, :, None] * jnp.einsum('tn,hpn->thp', span_items[2], running, precision=highest)
        ending = decays[:, None, None] * running + summary
        return (ending, (y_part, ending))
    _, (y_parts, endings) = lax.scan(advance, jnp.zeros((H, P_SIZE, N), jnp.float32), items)
    state_pages = jnp.zeros_like(endings).at[page_table].set(endings)
    gated = y_parts.reshape(TOKENS, DI) * jax.nn.silu(gate_val.astype(jnp.float32))
    squares = lax.optimization_barrier(jnp.sum(gated * gated, axis=1))
    normed = (gated * lax.rsqrt(squares / DI + epsilon)[:, None] * norm_gain[None, :]).astype(jnp.bfloat16)
    mixed_out = jnp.dot(normed, out_proj.astype(jnp.bfloat16), preferred_element_type=jnp.float32).astype(jnp.bfloat16)
    return (mixed_out, state_pages)
```

```python
import jax
import jax.numpy as jnp
from jax import lax
from jax.experimental import pallas as pl
from jax.experimental.pallas import tpu as pltpu
from jax.sharding import Mesh
from jax.sharding import PartitionSpec as P

N = 128
CONV = 4
PAGE = 128
DI = 3072
HEAD = 64
MINE = 6
CH = MINE * HEAD
EPS = 1e-05
BF = jnp.bfloat16
F32 = jnp.float32
NEG = -1e30


def dot(a, b):
    return jnp.dot(a, b, preferred_element_type=F32)


def dot_nt(a, b):
    return lax.dot_general(a, b, (((1,), (1,)), ((), ())), preferred_element_type=F32)


def dot_tn(a, b):
    return lax.dot_general(a, b, (((0,), (0,)), ((), ())), preferred_element_type=F32)


def silu(v):
    return v / (1.0 + jnp.exp(-v))


def softplus(v):
    return jnp.maximum(v, 0.0) + jnp.log1p(jnp.exp(-jnp.abs(v)))


def three(v):
    hi = v.astype(BF)
    rest = v - hi.astype(F32)
    mid = rest.astype(BF)
    return hi, mid, (rest - mid.astype(F32)).astype(BF)


def expand(v, hot):
    hi = v.astype(BF)
    lo = (v - hi.astype(F32)).astype(BF)
    return dot(hi, hot) + dot(lo, hot)


def head_hot():
    row = lax.broadcasted_iota(jnp.int32, (128, CH), 0)
    col = lax.broadcasted_iota(jnp.int32, (128, CH), 1)
    return (row == col // HEAD).astype(F32).astype(BF)


def wide(m):
    return jnp.concatenate([m, m, m], axis=1)


def local_kernel(
    where, lens, grps, hid, edge, w, ws, chan, cshared, heads, init,
    gate_o, y_o, c_o, fac_o, end_o, dp_o,
    xs, state, dp, dprow, read,
):
    step = pl.program_id(0)
    base = where[0] * 1024 + step * 256
    starts = []
    total = jnp.int32(0)
    for k in range(8):
        starts.append(total)
        total = total + lens[k]
    hot = head_hot()

    @pl.when(step == 0)
    def _():
        e = edge[...]
        xs[0:8, 0:CH] = dot(e, w[:, CH:])[8:16].astype(BF).astype(F32)
        xs[0:8, CH:] = dot(e, ws[:, 0:256])[8:16].astype(BF).astype(F32)
        state[...] = jnp.zeros_like(state)
        dp[...] = jnp.ones_like(dp)
        dprow[...] = jnp.ones_like(dprow)

    rows = hid[...]
    both = dot(rows, w[...]).astype(BF)
    gate_o[...] = both[:, :CH]
    xs[8:264, 0:CH] = both[:, CH:].astype(F32)
    sm = dot(rows, ws[...]).astype(BF)
    xs[8:264, CH:] = sm[:, :256].astype(F32)
    step_all = sm[:, 256:]
    row = lax.broadcasted_iota(jnp.int32, (128, 128), 0)
    col = lax.broadcasted_iota(jnp.int32, (128, 128), 1)
    pick = (row == col + where[1]).astype(F32)
    pick = jnp.where(col < MINE, pick, 0.0).astype(BF)
    wrow = lax.broadcasted_iota(jnp.int32, (128, CH), 0)
    wcol = lax.broadcasted_iota(jnp.int32, (128, CH), 1)
    pickx = (wrow == wcol // HEAD + where[1]).astype(F32).astype(BF)
    dt6 = softplus(dot(step_all, pick) + heads[0:1, :])
    log6 = heads[1:2, :] * dt6
    dtx = softplus(dot(step_all, pickx) + chan[5:6, :])

    pos = base + lax.broadcasted_iota(jnp.int32, (256, 128), 0)
    first = jnp.zeros((256, 128), jnp.int32)
    for k in range(1, 8):
        first = jnp.where(pos >= starts[k], starts[k], first)
    off = pos - first
    x = chan[4:5, :] + jnp.zeros((256, CH), F32)
    bc = cshared[4:5, :] + jnp.zeros((256, 256), F32)
    for lag in range(CONV):
        ok = (off >= lag).astype(F32)
        sx = xs[8 - lag : 264 - lag, 0:CH]
        sb = xs[8 - lag : 264 - lag, CH:]
        x = x + chan[lag : lag + 1, :] * sx * wide(ok)
        bc = bc + cshared[lag : lag + 1, :] * sb * jnp.concatenate([ok, ok], axis=1)
    tail = xs[256:264, :]
    xs[0:8, :] = tail
    x = silu(x)
    bc = silu(bc)
    b_all = bc[:, :128].astype(BF)
    c_all = bc[:, 128:].astype(BF)
    c_o[...] = c_all
    xdt_all = x * dtx
    lane = lax.broadcasted_iota(jnp.int32, (128, 128), 1)

    for sub in range(2):
        lo, hi = sub * 128, sub * 128 + 128
        p0 = base + lo
        f0 = first[lo:hi, :]
        prow = p0 + col
        frow = jnp.zeros((128, 128), jnp.int32)
        for k in range(1, 8):
            frow = jnp.where(prow >= starts[k], starts[k], frow)
        mask = (row >= col) & (f0 == frow)
        maskb = mask.astype(F32).astype(BF)
        cum = jnp.zeros((128, 128), F32)
        for part in three(log6[lo:hi, :]):
            cum = cum + dot(maskb, part)
        cumt = cum.T
        c = c_all[lo:hi, :]
        b = b_all[lo:hi, :]
        scores = dot_nt(c, b)
        xdt = xdt_all[lo:hi, :]
        xdtb = xdt.astype(BF)
        carried = f0 < p0
        ecum = jnp.exp(cum)
        cf = c.astype(F32)
        read[...] = dot_nt(
            jnp.where(carried, cf, 0.0).astype(BF), state[...].astype(BF)
        )
        flast = jnp.int32(0)
        glast = grps[0]
        for k in range(1, 8):
            got = p0 + 127 >= starts[k]
            flast = jnp.where(got, starts[k], flast)
            glast = jnp.where(got, grps[k], glast)

        @pl.when(flast >= p0)
        def _():
            gid = jnp.zeros((128, 128), jnp.int32) + grps[0]
            pcol = p0 + row
            for k in range(1, 8):
                gid = jnp.where(pcol >= starts[k], grps[k], gid)
            gid = jnp.where(f0 < p0, -1, gid)
            acc = read[...]
            for g in range(4):
                acc = acc + dot_nt(
                    jnp.where(gid == g, cf, 0.0).astype(BF), init[g].astype(BF)
                )
            read[...] = acc

        y = expand(ecum, hot) * read[...] + chan[6:7, :] * x[lo:hi, :]
        pieces = []
        for pair in range(3):
            xp = xdtb[:, pair * 128 : pair * 128 + 128]
            got = []
            for h in (2 * pair, 2 * pair + 1):
                diff = cum[:, h : h + 1] - cumt[h : h + 1, :]
                mix = jnp.exp(jnp.where(mask, diff, NEG)) * scores
                got.append(dot(mix.astype(BF), xp))
            pieces.append(jnp.where(lane < HEAD, got[0], got[1]))
        y_o[lo:hi, :] = y + jnp.concatenate(pieces, axis=1)

        same = f0 == flast
        w6 = jnp.exp(jnp.where(same, cum[127:128, :] - cum, NEG))
        xw = (xdt * expand(w6, hot)).astype(BF)
        summary = dot_tn(xw, b)
        carry = (flast < p0).astype(jnp.int32)
        scale = jnp.exp(jnp.broadcast_to(cumt[0:8, 127:128], (8, 128)))
        fac_o[lo:hi, :] = jnp.where(carried, ecum, 0.0) * dprow[0:1, :]
        keep = carry.astype(F32)
        dp[...] = dp[...] * scale * keep
        dprow[...] = dprow[...] * jnp.exp(cum[127:128, :]) * keep
        for h in range(MINE):
            a, z = h * HEAD, h * HEAD + HEAD
            old = state[a:z, :] * keep + init[glast, a:z, :] * (1.0 - keep)
            state[a:z, :] = scale[h : h + 1, :] * old + summary[a:z, :]
        end_o[sub] = state[...]
        dp_o[sub] = dp[...]


def finish_kernel(
    where, y, gate, c, fac, carry, chan, wout, ends, dp, out_o, sq_o, end_o
):
    hot = head_hot()
    cs = carry[...].astype(BF)
    full = y[...] + expand(fac[...], hot) * dot_nt(c[...], cs)
    g = full * silu(gate[...].astype(F32))
    sq_o[...] = jnp.broadcast_to(jnp.sum(g * g, axis=1, keepdims=True), sq_o.shape)
    gg = (g * chan[7:8, :]).astype(BF)
    out_o[...] = dot_nt(gg, wout[...]).astype(BF)
    for s in range(2):
        for h in range(MINE):
            a, z = h * HEAD, h * HEAD + HEAD
            end_o[s, a:z, :] = ends[s, a:z, :] + dp[s, h : h + 1, :] * carry[a:z, :]


def on_device(
    hidden_in, gate_proj, inner_proj, small_proj, row_layout, conv_inner, conv_shared,
    bias_inner, bias_shared, dt_bias, decay_log, skip_gain, norm_gain, out_proj,
    prompt_lengths, group_map, init_states, page_table,
):
    zx = ("z", "x")
    yt = ("y", "tp")
    yi, ci = lax.axis_index("y"), lax.axis_index("tp")
    gi = lax.axis_index("z") * 4 + lax.axis_index("x")
    seq = gi * 4 + yi
    d = hidden_in.shape[1]

    feature = jnp.arange(d, dtype=jnp.int32)
    logical = jnp.repeat(row_layout * 12, 12) + feature % 12
    onehot = (feature[:, None] == logical[None, :]).astype(BF)
    half = lax.dynamic_slice_in_dim(hidden_in, ci * 128, 128, 0)
    half = dot(half, onehot).astype(BF)
    hid = lax.all_gather(half, yt, axis=0, tiled=True)
    edge = lax.ppermute(hid[1008:], zx, [(i, i + 1) for i in range(15)])

    gp = gate_proj.astype(BF).reshape(12, 2, 4, CH)
    ip = inner_proj.astype(BF).reshape(12, 2, 4, CH)
    both = jnp.concatenate([gp, ip], axis=3).transpose(2, 1, 0, 3).reshape(96, 2 * CH)
    both = lax.all_to_all(both, yt, split_axis=0, concat_axis=0, tiled=True)
    w = lax.all_gather(both, zx, axis=0, tiled=True)
    ws = lax.all_gather(
        jnp.pad(small_proj.astype(BF), ((0, 0), (0, 80))), ("z", "x", "y", "tp"), axis=0, tiled=True
    )
    ot = out_proj.astype(BF).T.reshape(24, 4, CH).transpose(1, 0, 2).reshape(96, CH)
    ot = lax.all_to_all(ot, "y", split_axis=0, concat_axis=0, tiled=True)
    wout = lax.all_gather(ot, zx, axis=0, tiled=True)

    chan = jnp.concatenate(
        [
            conv_inner,
            bias_inner[None],
            jnp.repeat(dt_bias, HEAD)[None],
            jnp.repeat(skip_gain, HEAD)[None],
            norm_gain[None],
        ],
        axis=0,
    )
    cshared = jnp.concatenate([conv_shared, bias_shared[None], jnp.zeros((3, 256), F32)], axis=0)
    heads = jnp.stack([dt_bias, -jnp.exp(decay_log)])
    heads = jnp.pad(lax.dynamic_slice_in_dim(heads, yi * MINE, MINE, 1), ((0, 6), (0, 122)))
    place = jnp.stack([gi, ci * 24 + yi * MINE, yi]).astype(jnp.int32)
    init = init_states.reshape(4, 24 * HEAD, N)

    def spec(shape, index):
        return pl.BlockSpec(shape, index)

    const2 = lambda i, *_: (0, 0)
    tok2 = lambda i, *_: (i, 0)
    tok3 = lambda i, *_: (i, 0, 0)
    gate, y, c, fac, ends, dps = pl.pallas_call(
        local_kernel,
        grid_spec=pltpu.PrefetchScalarGridSpec(
            num_scalar_prefetch=3,
            grid=(4,),
            in_specs=[
                spec((256, d), tok2),
                spec((16, d), const2),
                spec((d, 2 * CH), const2),
                spec((d, 384), const2),
                spec((8, CH), lambda i, p, *_: (0, p[2])),
                spec((8, 256), const2),
                spec((8, 128), const2),
                spec((4, CH, N), lambda i, p, *_: (0, p[2], 0)),
            ],
            out_specs=[
                spec((256, CH), tok2),
                spec((256, CH), tok2),
                spec((256, N), tok2),
                spec((256, 128), tok2),
                spec((2, CH, N), tok3),
                spec((2, 8, 128), tok3),
            ],
            scratch_shapes=[
                pltpu.VMEM((264, CH + 256), F32),
                pltpu.VMEM((CH, N), F32),
                pltpu.VMEM((8, 128), F32),
                pltpu.VMEM((8, 128), F32),
                pltpu.VMEM((128, CH), F32),
            ],
        ),
        out_shape=[
            jax.ShapeDtypeStruct((1024, CH), BF),
            jax.ShapeDtypeStruct((1024, CH), F32),
            jax.ShapeDtypeStruct((1024, N), BF),
            jax.ShapeDtypeStruct((1024, 128), F32),
            jax.ShapeDtypeStruct((8, CH, N), F32),
            jax.ShapeDtypeStruct((8, 8, 128), F32),
        ],
        compiler_params=pltpu.CompilerParams(
            dimension_semantics=("arbitrary",), vmem_limit_bytes=40 << 20
        ),
        name="local",
    )(place, prompt_lengths, group_map, hid, edge, w, ws, chan, cshared, heads, init)

    parts = ends[7].reshape(3, 16, 8, N).transpose(1, 0, 2, 3).reshape(16, 24, N)
    parts = lax.all_to_all(parts, zx, split_axis=0, concat_axis=0, tiled=True)
    decs = lax.all_gather(dps[7], zx, axis=0)
    hb = gi // 8
    rows = lax.dynamic_slice_in_dim(decs[:, :6].reshape(16, 3, 2, 128), hb, 1, 2)
    rows = jnp.broadcast_to(rows, (16, 3, 8, 128)).reshape(16, 24, 128)
    run = jnp.zeros((24, N), F32)
    before = []
    for k in range(16):
        before.append(run)
        run = rows[k] * run + parts[k]
    back = lax.all_to_all(jnp.stack(before), zx, split_axis=0, concat_axis=0, tiled=True)
    carry = back.reshape(16, 3, 8, N).transpose(1, 0, 2, 3).reshape(CH, N)

    out, sq, endings = pl.pallas_call(
        finish_kernel,
        grid_spec=pltpu.PrefetchScalarGridSpec(
            num_scalar_prefetch=1,
            grid=(4,),
            in_specs=[
                spec((256, CH), tok2),
                spec((256, CH), tok2),
                spec((256, N), tok2),
                spec((256, 128), tok2),
                spec((CH, N), const2),
                spec((8, CH), lambda i, p: (0, p[2])),
                spec((d, CH), const2),
                spec((2, CH, N), tok3),
                spec((2, 8, 128), tok3),
            ],
            out_specs=[
                spec((256, d), tok2),
                spec((256, 128), tok2),
                spec((2, CH, N), tok3),
            ],
        ),
        out_shape=[
            jax.ShapeDtypeStruct((1024, d), BF),
            jax.ShapeDtypeStruct((1024, 128), F32),
            jax.ShapeDtypeStruct((8, CH, N), F32),
        ],
        compiler_params=pltpu.CompilerParams(
            dimension_semantics=("arbitrary",), vmem_limit_bytes=40 << 20
        ),
        name="finish",
    )(place, y, gate, c, fac, carry, chan, wout, ends, dps)

    total = lax.psum_scatter(sq[:, 0], yt, scatter_dimension=0, tiled=True)
    summed = lax.psum_scatter(out, yt, scatter_dimension=0, tiled=True)
    mixed = (summed.astype(F32) * lax.rsqrt(total / DI + EPS)[:, None]).astype(BF)

    pages = endings.reshape(8, MINE, HEAD, N)
    pages = lax.all_to_all(pages, "y", split_axis=0, concat_axis=1, tiled=True)
    swap = page_table[0] != seq * 2
    pages = jnp.where(swap, pages[::-1], pages)
    return (mixed, pages)


def solution(mesh):
    fine = Mesh(mesh.devices.reshape(4, 4, 4, 2), ("z", "x", "y", "tp"))
    seq = ("z", "x", "y")
    every = ("z", "x", "y", "tp")
    placed = (
        P(seq, None),
        P(every, None),
        P(every, None),
        P(every, None),
        P(),
        P(None, "tp"),
        P(),
        P("tp"),
        P(),
        P("tp"),
        P("tp"),
        P("tp"),
        P("tp"),
        P("tp", seq),
        P(),
        P(),
        P(None, "tp", None, None),
        P(seq),
    )
    return jax.shard_map(
        on_device,
        mesh=fine,
        in_specs=placed,
        out_specs=(P(every, None), P(seq, "tp", None, None)),
        check_vma=False,
    )
```

```python
import jax
import jax.numpy as jnp
from jax import lax
from jax.experimental import pallas as pl
from jax.experimental.pallas import tpu as pltpu
from jax.sharding import Mesh
from jax.sharding import PartitionSpec as P

N = 128
CONV = 4
PAGE = 128
DI = 3072
HEAD = 64
MINE = 6
CH = MINE * HEAD
EPS = 1e-05
BF = jnp.bfloat16
F32 = jnp.float32
NEG = -1e30


def dot(a, b):
    return jnp.dot(a, b, preferred_element_type=F32)


def dot_nt(a, b):
    return lax.dot_general(a, b, (((1,), (1,)), ((), ())), preferred_element_type=F32)


def dot_tn(a, b):
    return lax.dot_general(a, b, (((0,), (0,)), ((), ())), preferred_element_type=F32)


def silu(v):
    return v / (1.0 + jnp.exp(-v))


def softplus(v):
    return jnp.maximum(v, 0.0) + jnp.log1p(jnp.exp(-jnp.abs(v)))


def three(v):
    hi = v.astype(BF)
    rest = v - hi.astype(F32)
    mid = rest.astype(BF)
    return hi, mid, (rest - mid.astype(F32)).astype(BF)


def expand(v, hot):
    hi = v.astype(BF)
    lo = (v - hi.astype(F32)).astype(BF)
    return dot(hi, hot) + dot(lo, hot)


def head_hot():
    row = lax.broadcasted_iota(jnp.int32, (128, CH), 0)
    col = lax.broadcasted_iota(jnp.int32, (128, CH), 1)
    return (row == col // HEAD).astype(F32).astype(BF)


def wide(m):
    return jnp.concatenate([m, m, m], axis=1)


class Copies:
    def __init__(self, send, recv):
        self.send, self.recv, self.open = send, recv, []

    def go(self, src, dst, slot, device):
        copy = pltpu.make_async_remote_copy(
            src_ref=src,
            dst_ref=dst,
            send_sem=self.send.at[slot],
            recv_sem=self.recv.at[slot],
            device_id=device,
            device_id_type=pl.DeviceIdType.MESH,
        )
        copy.start()
        self.open.append(copy)

    def arrived(self, dst, slot):
        pltpu.make_async_remote_copy(
            src_ref=dst,
            dst_ref=dst,
            send_sem=self.send.at[slot],
            recv_sem=self.recv.at[slot],
            device_id=self.me,
            device_id_type=pl.DeviceIdType.MESH,
        ).wait_recv()

    def close(self):
        for copy in self.open:
            copy.wait_send()


def coords():
    return (
        lax.axis_index("z"),
        lax.axis_index("x"),
        lax.axis_index("y"),
        lax.axis_index("tp"),
    )


def greet(devices):
    barrier = pltpu.get_barrier_semaphore()
    for device in devices:
        pl.semaphore_signal(
            barrier, inc=1, device_id=device, device_id_type=pl.DeviceIdType.MESH
        )
    pl.semaphore_wait(barrier, len(devices))


class PlaneRing:
    def __init__(self, out, copies, rows):
        self.out, self.copies, self.half = out, copies, rows // 2
        z, x, y, c = coords()
        self.z, self.x, self.y, self.c = z, x, y, c
        self.a = x * (1 - c) + z * c
        self.b = z * (1 - c) + x * c

    def slot(self, da, db):
        a = (self.a + da + 4) % 4
        b = (self.b + db + 4) % 4
        return (b * 4 + a) * (1 - self.c) + (a * 4 + b) * self.c

    def device(self, da, db):
        a = (self.a + da + 4) % 4
        b = (self.b + db + 4) % 4
        c = self.c
        return (b * (1 - c) + a * c, a * (1 - c) + b * c, self.y, c)

    def full(self, da, db):
        return self.out.at[self.slot(da, db)]

    def part(self, da, db, low):
        return self.out.at[self.slot(da, db), pl.ds(0 if low else self.half, self.half)]

    def first(self, own):
        go = self.copies.go
        go(own, self.full(0, 0), 0, self.device(1, 0))
        go(own, self.full(0, 0), 1, self.device(-1, 0))
        go(own, self.full(0, 0), 4, self.device(0, 1))
        go(own, self.full(0, 0), 5, self.device(0, -1))

    def second(self, u, da):
        go = self.copies.go
        go(self.full(da, 0), self.full(da, 0), 4 + 4 * u, self.device(0, 1))
        go(self.full(da, 0), self.full(da, 0), 5 + 4 * u, self.device(0, -1))

    def along_a(self):
        go, arrived = self.copies.go, self.copies.arrived
        arrived(self.full(-1, 0), 0)
        go(self.part(-1, 0, True), self.part(-1, 0, True), 2, self.device(1, 0))
        self.second(1, -1)
        arrived(self.full(1, 0), 1)
        go(self.part(1, 0, False), self.part(1, 0, False), 3, self.device(-1, 0))
        self.second(2, 1)

    def along_b(self, u, da):
        go, arrived = self.copies.go, self.copies.arrived
        arrived(self.full(da, -1), 4 + 4 * u)
        go(self.part(da, -1, True), self.part(da, -1, True), 6 + 4 * u, self.device(0, 1))
        arrived(self.full(da, 1), 5 + 4 * u)
        go(self.part(da, 1, False), self.part(da, 1, False), 7 + 4 * u, self.device(0, -1))

    def across_a(self):
        arrived = self.copies.arrived
        arrived(self.part(2, 0, True), 2)
        arrived(self.part(2, 0, False), 3)
        self.second(3, 2)

    def finish(self):
        arrived = self.copies.arrived
        for u, da in enumerate((0, -1, 1, 2)):
            arrived(self.part(da, 2, True), 6 + 4 * u)
            arrived(self.part(da, 2, False), 7 + 4 * u)


def pack(width):
    row = lax.broadcasted_iota(jnp.int32, (96, 128), 0)
    col = lax.broadcasted_iota(jnp.int32, (96, 128), 1)
    padded = 128 // (96 // width)
    return (col == row // width * padded + row % width).astype(F32).astype(BF)


def gather_kernel(
    gate, inner, small, outp, half, w_o, hid_o, edge_o, wo_o,
    pieces, stage, unit, ostage, s1, r1, so, ro, su, ru, sh, rh, sc, rc, se, re, local,
):
    z, x, y, c = coords()
    q = y * 2 + c
    g = z * 4 + x
    after, before = (g + 1) % 16, (g + 15) % 16
    next_dev = (after // 4, after % 4, y, c)
    prev_dev = (before // 4, before % 4, y, c)
    pieces[...] = jnp.zeros_like(pieces)
    for t in range(8):
        a = 1536 * (t % 2) + CH * (t // 2)
        pieces[t, 0:12, 0:CH] = gate[:, a : a + CH].astype(BF)
        pieces[t, 0:12, CH : 2 * CH] = inner[:, a : a + CH].astype(BF)
        pieces[t, 0:12, 2 * CH : 2 * CH + 304] = small[...].astype(BF)

    group = [(z, x, ((q + k) % 8) // 2, (q + k) % 2) for k in range(1, 8)]
    greet(
        group
        + [(z, (x + 1) % 4, y, c), (z, (x + 3) % 4, y, c)]
        + [((z + 1) % 4, x, y, c), ((z + 3) % 4, x, y, c)]
        + [next_dev, prev_dev]
    )

    ones = Copies(s1, r1)
    outs = Copies(so, ro)
    hids = Copies(sh, rh)
    cross = Copies(sc, rc)
    units = Copies(su, ru)
    edges = Copies(se, re)
    for part in (ones, outs, hids, cross, units, edges):
        part.me = (z, x, y, 1 - c)
    for k in range(1, 8):
        t = (q + k) % 8
        ones.go(pieces.at[t], stage.at[q], k - 1, group[k - 1])
    for k in range(1, 4):
        t = (y + k) % 4
        outs.go(outp.at[t], ostage.at[y], k - 1, (z, x, t, c))
    right, left = (z, x, (y + 1) % 4, c), (z, x, (y + 3) % 4, c)
    mate = (z, x, y, 1 - c)

    def hslot(dy, core):
        return ((y + dy + 4) % 4) * 2 + core

    hids.go(half, hid_o.at[hslot(0, c)], 0, right)
    hids.go(half, hid_o.at[hslot(0, c)], 1, left)
    cross.go(half, hid_o.at[hslot(0, c)], 0, mate)
    keep = pltpu.make_async_copy(half, hid_o.at[hslot(0, c)], local.at[0])
    keep.start()
    stage[q] = pieces[q]
    ostage[y] = outp[y]

    for k in range(1, 8):
        ones.arrived(stage.at[(q + 8 - k) % 8], k - 1)
    packer = pack(12)
    for j in range(3):
        cols = slice(j * CH, j * CH + CH)
        unit[:, cols] = dot(packer, stage[:, :, cols].reshape(128, CH)).astype(BF)
    ring = PlaneRing(w_o, units, 96)
    ring.first(unit)
    mine = pltpu.make_async_copy(unit, w_o.at[g], local.at[1])
    mine.start()
    for k in range(1, 4):
        outs.arrived(ostage.at[(y + 4 - k) % 4], k - 1)
    wo_o[...] = dot(pack(24), ostage[...].reshape(128, CH)).astype(BF)

    ring.along_a()
    hids.arrived(hid_o.at[hslot(-1, c)], 0)
    hids.go(
        hid_o.at[hslot(-1, c), pl.ds(0, 64)], hid_o.at[hslot(-1, c), pl.ds(0, 64)], 2, right
    )
    hids.arrived(hid_o.at[hslot(1, c)], 1)
    hids.go(
        hid_o.at[hslot(1, c), pl.ds(64, 64)], hid_o.at[hslot(1, c), pl.ds(64, 64)], 3, left
    )
    cross.go(hid_o.at[hslot(-1, c)], hid_o.at[hslot(-1, c)], 1, mate)
    cross.go(hid_o.at[hslot(1, c)], hid_o.at[hslot(1, c)], 2, mate)
    ring.along_b(0, 0)
    ring.across_a()
    ring.along_b(1, -1)
    ring.along_b(2, 1)
    hids.arrived(hid_o.at[hslot(2, c), pl.ds(0, 64)], 2)
    hids.arrived(hid_o.at[hslot(2, c), pl.ds(64, 64)], 3)
    cross.go(hid_o.at[hslot(2, c)], hid_o.at[hslot(2, c)], 3, mate)
    keep.wait()
    cross.arrived(hid_o.at[hslot(0, 1 - c)], 0)
    cross.arrived(hid_o.at[hslot(-1, 1 - c)], 1)
    cross.arrived(hid_o.at[hslot(1, 1 - c)], 2)
    cross.arrived(hid_o.at[hslot(2, 1 - c)], 3)
    edges.go(hid_o.at[7, pl.ds(112, 16)], edge_o, 0, next_dev)
    ring.along_b(3, 2)
    ring.finish()
    edges.arrived(edge_o, 0)
    mine.wait()
    for part in (ones, outs, hids, cross, units, edges):
        part.close()


def scan_kernel(s, dec, wo, carry_o, w_o, parts, decs, befores, sp, rp, sd, rd, sb, rb, su, ru, local):
    z, x, y, c = coords()
    g = z * 4 + x
    peers = [(((g + k) % 16) // 4, ((g + k) % 16) % 4, y, c) for k in range(1, 16)]
    greet(peers)
    going, rates, back, units = Copies(sp, rp), Copies(sd, rd), Copies(sb, rb), Copies(su, ru)
    for part in (going, rates, back, units):
        part.me = (z, x, y, 1 - c)
    for k in range(1, 16):
        going.go(s.at[:, (g + k) % 16], parts.at[g], k - 1, peers[k - 1])
        rates.go(dec, decs.at[g], k - 1, peers[k - 1])
    ring = PlaneRing(w_o, units, 96)
    ring.first(wo)
    mine = pltpu.make_async_copy(wo, w_o.at[g], local.at[0])
    mine.start()
    parts[g] = s[:, g]
    decs[g] = dec[...]
    for k in range(1, 16):
        going.arrived(parts.at[(g + 16 - k) % 16], k - 1)
        rates.arrived(decs.at[(g + 16 - k) % 16], k - 1)
    hb = g // 8
    run = [jnp.zeros((8, 128), F32) for _ in range(3)]
    for k in range(16):
        for j in range(3):
            befores[k, j] = run[j]
            run[j] = decs[k, pl.ds(hb + 2 * j, 1), :] * run[j] + parts[k, j]
    for k in range(1, 16):
        back.go(befores.at[(g + k) % 16], carry_o.at[:, g], k - 1, peers[k - 1])
    carry_o[:, g] = befores[g]
    ring.along_a()
    ring.along_b(0, 0)
    ring.across_a()
    ring.along_b(1, -1)
    ring.along_b(2, 1)
    for k in range(1, 16):
        back.arrived(carry_o.at[:, (g + 16 - k) % 16], k - 1)
    ring.along_b(3, 2)
    ring.finish()
    mine.wait()
    for part in (going, rates, back, units):
        part.close()


def local_kernel(
    where, lens, grps, hid, edge, w, chan, cshared, heads, init,
    gate_o, y_o, c_o, fac_o, end_o, dp_o,
    xs, state, dp, dprow, read,
):
    step = pl.program_id(0)
    base = where[0] * 1024 + step * 256
    starts = []
    total = jnp.int32(0)
    for k in range(8):
        starts.append(total)
        total = total + lens[k]
    hot = head_hot()

    @pl.when(step == 0)
    def _():
        e = edge[...]
        xs[0:8, 0:CH] = dot(e, w[:, CH : 2 * CH])[8:16].astype(BF).astype(F32)
        xs[0:8, CH:] = dot(e, w[:, 2 * CH : 2 * CH + 256])[8:16].astype(BF).astype(F32)
        state[...] = jnp.zeros_like(state)
        dp[...] = jnp.ones_like(dp)
        dprow[...] = jnp.ones_like(dprow)

    rows = hid[...]
    both = dot(rows, w[:, : 2 * CH]).astype(BF)
    gate_o[...] = both[:, :CH]
    xs[8:264, 0:CH] = both[:, CH:].astype(F32)
    sm = dot(rows, w[:, 2 * CH :]).astype(BF)
    xs[8:264, CH:] = sm[:, :256].astype(F32)
    step_all = sm[:, 256:]
    row = lax.broadcasted_iota(jnp.int32, (128, 128), 0)
    col = lax.broadcasted_iota(jnp.int32, (128, 128), 1)
    pick = (row == col + where[1]).astype(F32)
    pick = jnp.where(col < MINE, pick, 0.0).astype(BF)
    wrow = lax.broadcasted_iota(jnp.int32, (128, CH), 0)
    wcol = lax.broadcasted_iota(jnp.int32, (128, CH), 1)
    pickx = (wrow == wcol // HEAD + where[1]).astype(F32).astype(BF)
    dt6 = softplus(dot(step_all, pick) + heads[0:1, :])
    log6 = heads[1:2, :] * dt6
    dtx = softplus(dot(step_all, pickx) + chan[5:6, :])

    pos = base + lax.broadcasted_iota(jnp.int32, (256, 128), 0)
    first = jnp.zeros((256, 128), jnp.int32)
    for k in range(1, 8):
        first = jnp.where(pos >= starts[k], starts[k], first)
    off = pos - first
    x = chan[4:5, :] + jnp.zeros((256, CH), F32)
    bc = cshared[4:5, :] + jnp.zeros((256, 256), F32)
    for lag in range(CONV):
        ok = (off >= lag).astype(F32)
        sx = xs[8 - lag : 264 - lag, 0:CH]
        sb = xs[8 - lag : 264 - lag, CH:]
        x = x + chan[lag : lag + 1, :] * sx * wide(ok)
        bc = bc + cshared[lag : lag + 1, :] * sb * jnp.concatenate([ok, ok], axis=1)
    tail = xs[256:264, :]
    xs[0:8, :] = tail
    x = silu(x)
    bc = silu(bc)
    b_all = bc[:, :128].astype(BF)
    c_all = bc[:, 128:].astype(BF)
    c_o[...] = c_all
    xdt_all = x * dtx
    lane = lax.broadcasted_iota(jnp.int32, (128, 128), 1)

    for sub in range(2):
        lo, hi = sub * 128, sub * 128 + 128
        p0 = base + lo
        f0 = first[lo:hi, :]
        prow = p0 + col
        frow = jnp.zeros((128, 128), jnp.int32)
        for k in range(1, 8):
            frow = jnp.where(prow >= starts[k], starts[k], frow)
        mask = (row >= col) & (f0 == frow)
        maskb = mask.astype(F32).astype(BF)
        cum = jnp.zeros((128, 128), F32)
        for part in three(log6[lo:hi, :]):
            cum = cum + dot(maskb, part)
        cumt = cum.T
        c = c_all[lo:hi, :]
        b = b_all[lo:hi, :]
        scores = dot_nt(c, b)
        xdt = xdt_all[lo:hi, :]
        xdtb = xdt.astype(BF)
        carried = f0 < p0
        ecum = jnp.exp(cum)
        cf = c.astype(F32)
        read[...] = dot_nt(
            jnp.where(carried, cf, 0.0).astype(BF), state[...].astype(BF)
        )
        flast = jnp.int32(0)
        glast = grps[0]
        for k in range(1, 8):
            got = p0 + 127 >= starts[k]
            flast = jnp.where(got, starts[k], flast)
            glast = jnp.where(got, grps[k], glast)

        @pl.when(flast >= p0)
        def _():
            gid = jnp.zeros((128, 128), jnp.int32) + grps[0]
            pcol = p0 + row
            for k in range(1, 8):
                gid = jnp.where(pcol >= starts[k], grps[k], gid)
            gid = jnp.where(f0 < p0, -1, gid)
            acc = read[...]
            for g in range(4):
                acc = acc + dot_nt(
                    jnp.where(gid == g, cf, 0.0).astype(BF), init[g].astype(BF)
                )
            read[...] = acc

        y = expand(ecum, hot) * read[...] + chan[6:7, :] * x[lo:hi, :]
        pieces = []
        for pair in range(3):
            xp = xdtb[:, pair * 128 : pair * 128 + 128]
            got = []
            for h in (2 * pair, 2 * pair + 1):
                diff = cum[:, h : h + 1] - cumt[h : h + 1, :]
                mix = jnp.exp(jnp.where(mask, diff, NEG)) * scores
                got.append(dot(mix.astype(BF), xp))
            pieces.append(jnp.where(lane < HEAD, got[0], got[1]))
        y_o[lo:hi, :] = y + jnp.concatenate(pieces, axis=1)

        same = f0 == flast
        w6 = jnp.exp(jnp.where(same, cum[127:128, :] - cum, NEG))
        xw = (xdt * expand(w6, hot)).astype(BF)
        summary = dot_tn(xw, b)
        carry = (flast < p0).astype(jnp.int32)
        scale = jnp.exp(jnp.broadcast_to(cumt[0:8, 127:128], (8, 128)))
        fac_o[lo:hi, :] = jnp.where(carried, ecum, 0.0) * dprow[0:1, :]
        keep = carry.astype(F32)
        dp[...] = dp[...] * scale * keep
        dprow[...] = dprow[...] * jnp.exp(cum[127:128, :]) * keep
        for h in range(MINE):
            a, z = h * HEAD, h * HEAD + HEAD
            old = state[a:z, :] * keep + init[glast, a:z, :] * (1.0 - keep)
            state[a:z, :] = scale[h : h + 1, :] * old + summary[a:z, :]
        end_o[sub] = state[...]
        dp_o[sub] = dp[...]


def finish_kernel(
    where, y, gate, c, fac, carry, chan, wout, ends, dp, out_o, sq_o, end_o
):
    hot = head_hot()
    cs = carry[...].astype(BF)
    full = y[...] + expand(fac[...], hot) * dot_nt(c[...], cs)
    g = full * silu(gate[...].astype(F32))
    sq_o[...] = jnp.broadcast_to(jnp.sum(g * g, axis=1, keepdims=True), sq_o.shape)
    gg = (g * chan[7:8, :]).astype(BF)
    out_o[...] = dot_nt(gg, wout[...]).astype(BF)
    for s in range(2):
        for h in range(MINE):
            a, z = h * HEAD, h * HEAD + HEAD
            end_o[s, a:z, :] = ends[s, a:z, :] + dp[s, h : h + 1, :] * carry[a:z, :]


def on_device(
    hidden_in, gate_proj, inner_proj, small_proj, row_layout, conv_inner, conv_shared,
    bias_inner, bias_shared, dt_bias, decay_log, skip_gain, norm_gain, out_proj,
    prompt_lengths, group_map, init_states, page_table,
):
    yt = ("y", "tp")
    yi, ci = lax.axis_index("y"), lax.axis_index("tp")
    gi = lax.axis_index("z") * 4 + lax.axis_index("x")
    seq = gi * 4 + yi
    d = hidden_in.shape[1]

    feature = jnp.arange(d, dtype=jnp.int32)
    logical = jnp.repeat(row_layout * 12, 12) + feature % 12
    onehot = (feature[:, None] == logical[None, :]).astype(BF)
    half = lax.dynamic_slice_in_dim(hidden_in, ci * 128, 128, 0)
    half = dot(half, onehot).astype(BF)
    outp = jnp.pad(
        out_proj.astype(BF).T.reshape(24, 4, CH).transpose(1, 0, 2), ((0, 0), (0, 8), (0, 0))
    )
    vm = pl.BlockSpec(memory_space=pltpu.VMEM)
    anyw = pl.BlockSpec(memory_space=pl.ANY)
    dma = pltpu.SemaphoreType.DMA
    w, hid, edge, wo = pl.pallas_call(
        gather_kernel,
        in_specs=[vm] * 5,
        out_specs=[anyw, anyw, anyw, vm],
        out_shape=[
            jax.ShapeDtypeStruct((16, 96, 3 * CH), BF),
            jax.ShapeDtypeStruct((8, 128, d), BF),
            jax.ShapeDtypeStruct((16, d), BF),
            jax.ShapeDtypeStruct((96, CH), BF),
        ],
        scratch_shapes=[
            pltpu.VMEM((8, 16, 3 * CH), BF),
            pltpu.VMEM((8, 16, 3 * CH), BF),
            pltpu.VMEM((96, 3 * CH), BF),
            pltpu.VMEM((4, 32, CH), BF),
            dma((7,)), dma((7,)),
            dma((3,)), dma((3,)),
            dma((20,)), dma((20,)),
            dma((4,)), dma((4,)),
            dma((4,)), dma((4,)),
            dma((1,)), dma((1,)),
            dma((2,)),
        ],
        compiler_params=pltpu.CompilerParams(
            collective_id=0, has_side_effects=True, vmem_limit_bytes=40 << 20
        ),
        name="gather",
    )(gate_proj, inner_proj, small_proj, outp, half)
    w = w.reshape(d, 3 * CH)
    hid = hid.reshape(1024, d)

    chan = jnp.concatenate(
        [
            conv_inner,
            bias_inner[None],
            jnp.repeat(dt_bias, HEAD)[None],
            jnp.repeat(skip_gain, HEAD)[None],
            norm_gain[None],
        ],
        axis=0,
    )
    cshared = jnp.concatenate([conv_shared, bias_shared[None], jnp.zeros((3, 256), F32)], axis=0)
    heads = jnp.stack([dt_bias, -jnp.exp(decay_log)])
    heads = jnp.pad(lax.dynamic_slice_in_dim(heads, yi * MINE, MINE, 1), ((0, 6), (0, 122)))
    place = jnp.stack([gi, ci * 24 + yi * MINE, yi]).astype(jnp.int32)
    init = init_states.reshape(4, 24 * HEAD, N)

    def spec(shape, index):
        return pl.BlockSpec(shape, index)

    const2 = lambda i, *_: (0, 0)
    tok2 = lambda i, *_: (i, 0)
    tok3 = lambda i, *_: (i, 0, 0)
    gate, y, c, fac, ends, dps = pl.pallas_call(
        local_kernel,
        grid_spec=pltpu.PrefetchScalarGridSpec(
            num_scalar_prefetch=3,
            grid=(4,),
            in_specs=[
                spec((256, d), tok2),
                spec((16, d), const2),
                spec((d, 3 * CH), const2),
                spec((8, CH), lambda i, p, *_: (0, p[2])),
                spec((8, 256), const2),
                spec((8, 128), const2),
                spec((4, CH, N), lambda i, p, *_: (0, p[2], 0)),
            ],
            out_specs=[
                spec((256, CH), tok2),
                spec((256, CH), tok2),
                spec((256, N), tok2),
                spec((256, 128), tok2),
                spec((2, CH, N), tok3),
                spec((2, 8, 128), tok3),
            ],
            scratch_shapes=[
                pltpu.VMEM((264, CH + 256), F32),
                pltpu.VMEM((CH, N), F32),
                pltpu.VMEM((8, 128), F32),
                pltpu.VMEM((8, 128), F32),
                pltpu.VMEM((128, CH), F32),
            ],
        ),
        out_shape=[
            jax.ShapeDtypeStruct((1024, CH), BF),
            jax.ShapeDtypeStruct((1024, CH), F32),
            jax.ShapeDtypeStruct((1024, N), BF),
            jax.ShapeDtypeStruct((1024, 128), F32),
            jax.ShapeDtypeStruct((8, CH, N), F32),
            jax.ShapeDtypeStruct((8, 8, 128), F32),
        ],
        compiler_params=pltpu.CompilerParams(
            dimension_semantics=("arbitrary",), vmem_limit_bytes=40 << 20
        ),
        name="local",
    )(place, prompt_lengths, group_map, hid, edge, w, chan, cshared, heads, init)

    carry, wout = pl.pallas_call(
        scan_kernel,
        in_specs=[vm] * 3,
        out_specs=[vm, anyw],
        out_shape=[
            jax.ShapeDtypeStruct((3, 16, 8, N), F32),
            jax.ShapeDtypeStruct((16, 96, CH), BF),
        ],
        scratch_shapes=[
            pltpu.VMEM((16, 3, 8, N), F32),
            pltpu.VMEM((16, 8, N), F32),
            pltpu.VMEM((16, 3, 8, N), F32),
            dma((15,)), dma((15,)),
            dma((15,)), dma((15,)),
            dma((15,)), dma((15,)),
            dma((20,)), dma((20,)),
            dma((1,)),
        ],
        compiler_params=pltpu.CompilerParams(
            collective_id=1, has_side_effects=True, vmem_limit_bytes=40 << 20
        ),
        name="scan",
    )(ends[7].reshape(3, 16, 8, N), dps[7], wo)
    carry = carry.reshape(CH, N)
    wout = wout.reshape(d, CH)

    out, sq, endings = pl.pallas_call(
        finish_kernel,
        grid_spec=pltpu.PrefetchScalarGridSpec(
            num_scalar_prefetch=1,
            grid=(4,),
            in_specs=[
                spec((256, CH), tok2),
                spec((256, CH), tok2),
                spec((256, N), tok2),
                spec((256, 128), tok2),
                spec((CH, N), const2),
                spec((8, CH), lambda i, p: (0, p[2])),
                spec((d, CH), const2),
                spec((2, CH, N), tok3),
                spec((2, 8, 128), tok3),
            ],
            out_specs=[
                spec((256, d), tok2),
                spec((256, 128), tok2),
                spec((2, CH, N), tok3),
            ],
        ),
        out_shape=[
            jax.ShapeDtypeStruct((1024, d), BF),
            jax.ShapeDtypeStruct((1024, 128), F32),
            jax.ShapeDtypeStruct((8, CH, N), F32),
        ],
        compiler_params=pltpu.CompilerParams(
            dimension_semantics=("arbitrary",), vmem_limit_bytes=40 << 20
        ),
        name="finish",
    )(place, y, gate, c, fac, carry, chan, wout, ends, dps)

    total = lax.psum_scatter(sq[:, 0], yt, scatter_dimension=0, tiled=True)
    summed = lax.psum_scatter(out, yt, scatter_dimension=0, tiled=True)
    mixed = (summed.astype(F32) * lax.rsqrt(total / DI + EPS)[:, None]).astype(BF)

    pages = endings.reshape(8, MINE, HEAD, N)
    pages = lax.all_to_all(pages, "y", split_axis=0, concat_axis=1, tiled=True)
    swap = page_table[0] != seq * 2
    pages = jnp.where(swap, pages[::-1], pages)
    return (mixed, pages)


def solution(mesh):
    fine = Mesh(mesh.devices.reshape(4, 4, 4, 2), ("z", "x", "y", "tp"))
    seq = ("z", "x", "y")
    every = ("z", "x", "y", "tp")
    placed = (
        P(seq, None),
        P(every, None),
        P(every, None),
        P(every, None),
        P(),
        P(None, "tp"),
        P(),
        P("tp"),
        P(),
        P("tp"),
        P("tp"),
        P("tp"),
        P("tp"),
        P("tp", seq),
        P(),
        P(),
        P(None, "tp", None, None),
        P(seq),
    )
    return jax.shard_map(
        on_device,
        mesh=fine,
        in_specs=placed,
        out_specs=(P(every, None), P(seq, "tp", None, None)),
        check_vma=False,
    )
```

```python
import jax
import jax.numpy as jnp
from jax import lax
from jax.experimental import pallas as pl
from jax.experimental.pallas import tpu as pltpu
from jax.sharding import Mesh
from jax.sharding import PartitionSpec as P

N = 128
CONV = 4
PAGE = 128
DI = 3072
HEAD = 64
MINE = 6
CH = MINE * HEAD
EPS = 1e-05
BF = jnp.bfloat16
F32 = jnp.float32
NEG = -1e30


def dot(a, b):
    return jnp.dot(a, b, preferred_element_type=F32)


def dot_nt(a, b):
    return lax.dot_general(a, b, (((1,), (1,)), ((), ())), preferred_element_type=F32)


def dot_tn(a, b):
    return lax.dot_general(a, b, (((0,), (0,)), ((), ())), preferred_element_type=F32)


def silu(v):
    return v / (1.0 + jnp.exp(-v))


def softplus(v):
    return jnp.maximum(v, 0.0) + jnp.log1p(jnp.exp(-jnp.abs(v)))


def three(v):
    hi = v.astype(BF)
    rest = v - hi.astype(F32)
    mid = rest.astype(BF)
    return hi, mid, (rest - mid.astype(F32)).astype(BF)


def expand(v, hot):
    hi = v.astype(BF)
    lo = (v - hi.astype(F32)).astype(BF)
    return dot(hi, hot) + dot(lo, hot)


def head_hot():
    row = lax.broadcasted_iota(jnp.int32, (128, CH), 0)
    col = lax.broadcasted_iota(jnp.int32, (128, CH), 1)
    return (row == col // HEAD).astype(F32).astype(BF)


def wide(m):
    return jnp.concatenate([m, m, m], axis=1)


class Copies:
    def __init__(self, send, recv):
        self.send, self.recv, self.open = send, recv, []

    def go(self, src, dst, slot, device):
        copy = pltpu.make_async_remote_copy(
            src_ref=src,
            dst_ref=dst,
            send_sem=self.send.at[slot],
            recv_sem=self.recv.at[slot],
            device_id=device,
            device_id_type=pl.DeviceIdType.MESH,
        )
        copy.start()
        self.open.append(copy)

    def arrived(self, dst, slot):
        pltpu.make_async_remote_copy(
            src_ref=dst,
            dst_ref=dst,
            send_sem=self.send.at[slot],
            recv_sem=self.recv.at[slot],
            device_id=self.me,
            device_id_type=pl.DeviceIdType.MESH,
        ).wait_recv()

    def close(self):
        for copy in self.open:
            copy.wait_send()


def coords():
    return (
        lax.axis_index("z"),
        lax.axis_index("x"),
        lax.axis_index("y"),
        lax.axis_index("tp"),
    )


def greet(devices):
    barrier = pltpu.get_barrier_semaphore()
    for device in devices:
        pl.semaphore_signal(
            barrier, inc=1, device_id=device, device_id_type=pl.DeviceIdType.MESH
        )
    pl.semaphore_wait(barrier, len(devices))


class PlaneRing:
    def __init__(self, out, copies, rows):
        self.out, self.copies, self.half = out, copies, rows // 2
        z, x, y, c = coords()
        self.z, self.x, self.y, self.c = z, x, y, c
        self.a = x * (1 - c) + z * c
        self.b = z * (1 - c) + x * c

    def slot(self, da, db):
        a = (self.a + da + 4) % 4
        b = (self.b + db + 4) % 4
        return (b * 4 + a) * (1 - self.c) + (a * 4 + b) * self.c

    def device(self, da, db):
        a = (self.a + da + 4) % 4
        b = (self.b + db + 4) % 4
        c = self.c
        return (b * (1 - c) + a * c, a * (1 - c) + b * c, self.y, c)

    def full(self, da, db):
        return self.out.at[self.slot(da, db)]

    def part(self, da, db, low):
        return self.out.at[self.slot(da, db), pl.ds(0 if low else self.half, self.half)]

    def first(self, own):
        go = self.copies.go
        go(own, self.full(0, 0), 0, self.device(1, 0))
        go(own, self.full(0, 0), 1, self.device(-1, 0))
        go(own, self.full(0, 0), 4, self.device(0, 1))
        go(own, self.full(0, 0), 5, self.device(0, -1))

    def second(self, u, da):
        go = self.copies.go
        go(self.full(da, 0), self.full(da, 0), 4 + 4 * u, self.device(0, 1))
        go(self.full(da, 0), self.full(da, 0), 5 + 4 * u, self.device(0, -1))

    def along_a(self):
        go, arrived = self.copies.go, self.copies.arrived
        arrived(self.full(-1, 0), 0)
        go(self.part(-1, 0, True), self.part(-1, 0, True), 2, self.device(1, 0))
        self.second(1, -1)
        arrived(self.full(1, 0), 1)
        go(self.part(1, 0, False), self.part(1, 0, False), 3, self.device(-1, 0))
        self.second(2, 1)

    def along_b(self, u, da):
        go, arrived = self.copies.go, self.copies.arrived
        arrived(self.full(da, -1), 4 + 4 * u)
        go(self.part(da, -1, True), self.part(da, -1, True), 6 + 4 * u, self.device(0, 1))
        arrived(self.full(da, 1), 5 + 4 * u)
        go(self.part(da, 1, False), self.part(da, 1, False), 7 + 4 * u, self.device(0, -1))

    def across_a(self):
        arrived = self.copies.arrived
        arrived(self.part(2, 0, True), 2)
        arrived(self.part(2, 0, False), 3)
        self.second(3, 2)

    def finish(self):
        arrived = self.copies.arrived
        for u, da in enumerate((0, -1, 1, 2)):
            arrived(self.part(da, 2, True), 6 + 4 * u)
            arrived(self.part(da, 2, False), 7 + 4 * u)


def pack(width):
    row = lax.broadcasted_iota(jnp.int32, (96, 128), 0)
    col = lax.broadcasted_iota(jnp.int32, (96, 128), 1)
    padded = 128 // (96 // width)
    return (col == row // width * padded + row % width).astype(F32).astype(BF)


def gather_kernel(
    gate, inner, small, outp, half, w_o, hid_o, edge_o, wo_o,
    pieces, stage, unit, ostage, s1, r1, so, ro, su, ru, sh, rh, sc, rc, se, re, local,
):
    z, x, y, c = coords()
    q = y * 2 + c
    g = z * 4 + x
    after, before = (g + 1) % 16, (g + 15) % 16
    next_dev = (after // 4, after % 4, y, c)
    prev_dev = (before // 4, before % 4, y, c)
    pieces[...] = jnp.zeros_like(pieces)
    for t in range(8):
        a = 1536 * (t % 2) + CH * (t // 2)
        pieces[t, 0:12, 0:CH] = gate[:, a : a + CH].astype(BF)
        pieces[t, 0:12, CH : 2 * CH] = inner[:, a : a + CH].astype(BF)
        pieces[t, 0:12, 2 * CH : 2 * CH + 304] = small[...].astype(BF)

    group = [(z, x, ((q + k) % 8) // 2, (q + k) % 2) for k in range(1, 8)]
    greet(
        group
        + [(z, (x + 1) % 4, y, c), (z, (x + 3) % 4, y, c)]
        + [((z + 1) % 4, x, y, c), ((z + 3) % 4, x, y, c)]
        + [next_dev, prev_dev]
    )

    ones = Copies(s1, r1)
    outs = Copies(so, ro)
    hids = Copies(sh, rh)
    cross = Copies(sc, rc)
    units = Copies(su, ru)
    edges = Copies(se, re)
    for part in (ones, outs, hids, cross, units, edges):
        part.me = (z, x, y, 1 - c)
    for k in range(1, 8):
        t = (q + k) % 8
        ones.go(pieces.at[t], stage.at[q], k - 1, group[k - 1])
    for k in range(1, 4):
        t = (y + k) % 4
        outs.go(outp.at[t], ostage.at[y], k - 1, (z, x, t, c))
    right, left = (z, x, (y + 1) % 4, c), (z, x, (y + 3) % 4, c)
    mate = (z, x, y, 1 - c)

    def hslot(dy, core):
        return ((y + dy + 4) % 4) * 2 + core

    hids.go(half, hid_o.at[hslot(0, c)], 0, right)
    hids.go(half, hid_o.at[hslot(0, c)], 1, left)
    cross.go(half, hid_o.at[hslot(0, c)], 0, mate)
    keep = pltpu.make_async_copy(half, hid_o.at[hslot(0, c)], local.at[0])
    keep.start()
    stage[q] = pieces[q]
    ostage[y] = outp[y]

    for k in range(1, 8):
        ones.arrived(stage.at[(q + 8 - k) % 8], k - 1)
    packer = pack(12)
    for j in range(3):
        cols = slice(j * CH, j * CH + CH)
        unit[:, cols] = dot(packer, stage[:, :, cols].reshape(128, CH)).astype(BF)
    ring = PlaneRing(w_o, units, 96)
    ring.first(unit)
    mine = pltpu.make_async_copy(unit, w_o.at[g], local.at[1])
    mine.start()
    for k in range(1, 4):
        outs.arrived(ostage.at[(y + 4 - k) % 4], k - 1)
    wo_o[...] = dot(pack(24), ostage[...].reshape(128, CH)).astype(BF)

    ring.along_a()
    hids.arrived(hid_o.at[hslot(-1, c)], 0)
    hids.go(
        hid_o.at[hslot(-1, c), pl.ds(0, 64)], hid_o.at[hslot(-1, c), pl.ds(0, 64)], 2, right
    )
    hids.arrived(hid_o.at[hslot(1, c)], 1)
    hids.go(
        hid_o.at[hslot(1, c), pl.ds(64, 64)], hid_o.at[hslot(1, c), pl.ds(64, 64)], 3, left
    )
    cross.go(hid_o.at[hslot(-1, c)], hid_o.at[hslot(-1, c)], 1, mate)
    cross.go(hid_o.at[hslot(1, c)], hid_o.at[hslot(1, c)], 2, mate)
    ring.along_b(0, 0)
    ring.across_a()
    ring.along_b(1, -1)
    ring.along_b(2, 1)
    hids.arrived(hid_o.at[hslot(2, c), pl.ds(0, 64)], 2)
    hids.arrived(hid_o.at[hslot(2, c), pl.ds(64, 64)], 3)
    cross.go(hid_o.at[hslot(2, c)], hid_o.at[hslot(2, c)], 3, mate)
    keep.wait()
    cross.arrived(hid_o.at[hslot(0, 1 - c)], 0)
    cross.arrived(hid_o.at[hslot(-1, 1 - c)], 1)
    cross.arrived(hid_o.at[hslot(1, 1 - c)], 2)
    cross.arrived(hid_o.at[hslot(2, 1 - c)], 3)
    edges.go(hid_o.at[7, pl.ds(112, 16)], edge_o, 0, next_dev)
    ring.along_b(3, 2)
    ring.finish()
    edges.arrived(edge_o, 0)
    mine.wait()
    for part in (ones, outs, hids, cross, units, edges):
        part.close()


def scan_kernel(
    s, dec, wo, ends, dps, carry_o, w_o, page_o, rate_o,
    parts, decs, befores, small, sp, rp, sd, rd, sb, rb, su, ru, sg, rg, sh, rh, local,
):
    z, x, y, c = coords()
    g = z * 4 + x
    peers = [(((g + k) % 16) // 4, ((g + k) % 16) % 4, y, c) for k in range(1, 16)]
    near = [(z, x, (y + k) % 4, c) for k in range(1, 4)]
    greet(peers + near)
    going, rates, back, units = Copies(sp, rp), Copies(sd, rd), Copies(sb, rb), Copies(su, ru)
    pages, decays = Copies(sg, rg), Copies(sh, rh)
    for part in (going, rates, back, units, pages, decays):
        part.me = (z, x, y, 1 - c)
    for k in range(1, 16):
        going.go(s.at[:, (g + k) % 16], parts.at[g], k - 1, peers[k - 1])
        rates.go(dec, decs.at[g], k - 1, peers[k - 1])
    ring = PlaneRing(w_o, units, 96)
    ring.first(wo)
    mine = pltpu.make_async_copy(wo, w_o.at[g], local.at[0])
    mine.start()
    parts[g] = s[:, g]
    decs[g] = dec[...]
    for k in range(8):
        small[k] = ends[k].astype(BF)
    for k in range(1, 4):
        t = (y + k) % 4
        pages.go(small.at[pl.ds(t * 2, 2)], page_o.at[y], k - 1, near[k - 1])
        decays.go(dps.at[pl.ds(t * 2, 2)], rate_o.at[y], k - 1, near[k - 1])
    for k in range(2):
        page_o[y, k] = small[y * 2 + k]
        rate_o[y, k] = dps[y * 2 + k]
    for k in range(1, 16):
        going.arrived(parts.at[(g + 16 - k) % 16], k - 1)
        rates.arrived(decs.at[(g + 16 - k) % 16], k - 1)
    hb = g // 8
    run = [jnp.zeros((8, 128), F32) for _ in range(3)]
    for k in range(16):
        for j in range(3):
            befores[k, j] = run[j]
            run[j] = decs[k, pl.ds(hb + 2 * j, 1), :] * run[j] + parts[k, j]
    for k in range(1, 16):
        back.go(befores.at[(g + k) % 16], carry_o.at[:, g], k - 1, peers[k - 1])
    carry_o[:, g] = befores[g]
    ring.along_a()
    ring.along_b(0, 0)
    ring.across_a()
    ring.along_b(1, -1)
    ring.along_b(2, 1)
    for k in range(1, 16):
        back.arrived(carry_o.at[:, (g + 16 - k) % 16], k - 1)
    ring.along_b(3, 2)
    ring.finish()
    mine.wait()
    for k in range(1, 4):
        t = (y + 4 - k) % 4
        pages.arrived(page_o.at[t], k - 1)
        decays.arrived(rate_o.at[t], k - 1)
    for part in (going, rates, back, units, pages, decays):
        part.close()


def local_kernel(
    where, lens, grps, hid, edge, w, chan, cshared, heads, init,
    gate_o, y_o, c_o, fac_o, end_o, dp_o,
    xs, state, dp, dprow, read,
):
    step = pl.program_id(0)
    base = where[0] * 1024 + step * 256
    starts = []
    total = jnp.int32(0)
    for k in range(8):
        starts.append(total)
        total = total + lens[k]
    hot = head_hot()

    @pl.when(step == 0)
    def _():
        e = edge[...]
        xs[0:8, 0:CH] = dot(e, w[:, CH : 2 * CH])[8:16].astype(BF).astype(F32)
        xs[0:8, CH:] = dot(e, w[:, 2 * CH : 2 * CH + 256])[8:16].astype(BF).astype(F32)
        state[...] = jnp.zeros_like(state)
        dp[...] = jnp.ones_like(dp)
        dprow[...] = jnp.ones_like(dprow)

    rows = hid[...]
    both = dot(rows, w[:, : 2 * CH]).astype(BF)
    gate_o[...] = both[:, :CH]
    xs[8:264, 0:CH] = both[:, CH:].astype(F32)
    sm = dot(rows, w[:, 2 * CH :]).astype(BF)
    xs[8:264, CH:] = sm[:, :256].astype(F32)
    step_all = sm[:, 256:]
    row = lax.broadcasted_iota(jnp.int32, (128, 128), 0)
    col = lax.broadcasted_iota(jnp.int32, (128, 128), 1)
    pick = (row == col + where[1]).astype(F32)
    pick = jnp.where(col < MINE, pick, 0.0).astype(BF)
    wrow = lax.broadcasted_iota(jnp.int32, (128, CH), 0)
    wcol = lax.broadcasted_iota(jnp.int32, (128, CH), 1)
    pickx = (wrow == wcol // HEAD + where[1]).astype(F32).astype(BF)
    dt6 = softplus(dot(step_all, pick) + heads[0:1, :])
    log6 = heads[1:2, :] * dt6
    dtx = softplus(dot(step_all, pickx) + chan[5:6, :])

    pos = base + lax.broadcasted_iota(jnp.int32, (256, 128), 0)
    first = jnp.zeros((256, 128), jnp.int32)
    for k in range(1, 8):
        first = jnp.where(pos >= starts[k], starts[k], first)
    off = pos - first
    x = chan[4:5, :] + jnp.zeros((256, CH), F32)
    bc = cshared[4:5, :] + jnp.zeros((256, 256), F32)
    for lag in range(CONV):
        ok = (off >= lag).astype(F32)
        sx = xs[8 - lag : 264 - lag, 0:CH]
        sb = xs[8 - lag : 264 - lag, CH:]
        x = x + chan[lag : lag + 1, :] * sx * wide(ok)
        bc = bc + cshared[lag : lag + 1, :] * sb * jnp.concatenate([ok, ok], axis=1)
    tail = xs[256:264, :]
    xs[0:8, :] = tail
    x = silu(x)
    bc = silu(bc)
    b_all = bc[:, :128].astype(BF)
    c_all = bc[:, 128:].astype(BF)
    c_o[...] = c_all
    xdt_all = x * dtx
    lane = lax.broadcasted_iota(jnp.int32, (128, 128), 1)

    for sub in range(2):
        lo, hi = sub * 128, sub * 128 + 128
        p0 = base + lo
        f0 = first[lo:hi, :]
        prow = p0 + col
        frow = jnp.zeros((128, 128), jnp.int32)
        for k in range(1, 8):
            frow = jnp.where(prow >= starts[k], starts[k], frow)
        mask = (row >= col) & (f0 == frow)
        maskb = mask.astype(F32).astype(BF)
        cum = jnp.zeros((128, 128), F32)
        for part in three(log6[lo:hi, :]):
            cum = cum + dot(maskb, part)
        cumt = cum.T
        c = c_all[lo:hi, :]
        b = b_all[lo:hi, :]
        scores = dot_nt(c, b)
        xdt = xdt_all[lo:hi, :]
        xdtb = xdt.astype(BF)
        carried = f0 < p0
        ecum = jnp.exp(cum)
        cf = c.astype(F32)
        read[...] = dot_nt(
            jnp.where(carried, cf, 0.0).astype(BF), state[...].astype(BF)
        )
        flast = jnp.int32(0)
        glast = grps[0]
        for k in range(1, 8):
            got = p0 + 127 >= starts[k]
            flast = jnp.where(got, starts[k], flast)
            glast = jnp.where(got, grps[k], glast)

        @pl.when(flast >= p0)
        def _():
            gid = jnp.zeros((128, 128), jnp.int32) + grps[0]
            pcol = p0 + row
            for k in range(1, 8):
                gid = jnp.where(pcol >= starts[k], grps[k], gid)
            gid = jnp.where(f0 < p0, -1, gid)
            acc = read[...]
            for g in range(4):
                acc = acc + dot_nt(
                    jnp.where(gid == g, cf, 0.0).astype(BF), init[g].astype(BF)
                )
            read[...] = acc

        y = expand(ecum, hot) * read[...] + chan[6:7, :] * x[lo:hi, :]
        pieces = []
        for pair in range(3):
            xp = xdtb[:, pair * 128 : pair * 128 + 128]
            got = []
            for h in (2 * pair, 2 * pair + 1):
                diff = cum[:, h : h + 1] - cumt[h : h + 1, :]
                mix = jnp.exp(jnp.where(mask, diff, NEG)) * scores
                got.append(dot(mix.astype(BF), xp))
            pieces.append(jnp.where(lane < HEAD, got[0], got[1]))
        y_o[lo:hi, :] = y + jnp.concatenate(pieces, axis=1)

        same = f0 == flast
        w6 = jnp.exp(jnp.where(same, cum[127:128, :] - cum, NEG))
        xw = (xdt * expand(w6, hot)).astype(BF)
        summary = dot_tn(xw, b)
        carry = (flast < p0).astype(jnp.int32)
        scale = jnp.exp(jnp.broadcast_to(cumt[0:8, 127:128], (8, 128)))
        fac_o[lo:hi, :] = jnp.where(carried, ecum, 0.0) * dprow[0:1, :]
        keep = carry.astype(F32)
        dp[...] = dp[...] * scale * keep
        dprow[...] = dprow[...] * jnp.exp(cum[127:128, :]) * keep
        for h in range(MINE):
            a, z = h * HEAD, h * HEAD + HEAD
            old = state[a:z, :] * keep + init[glast, a:z, :] * (1.0 - keep)
            state[a:z, :] = scale[h : h + 1, :] * old + summary[a:z, :]
        end_o[sub] = state[...]
        dp_o[sub] = dp[...]


def finish_kernel(
    y_in, gate, c_in, fac, carry, gain, wout,
    out_o, carry_o,
    opp, ahead, behind, own, xs, xr, low, high, from_l, from_r, sq, sqr,
    sm, rm, sy, ry, sq_s, sq_r, sc, rc,
):
    z, x, y, c = coords()
    q = y * 2 + c
    group = [(z, x, ((q + k) % 8) // 2, (q + k) % 2) for k in range(1, 8)]
    greet(group)
    mates, rings, sums, states = Copies(sm, rm), Copies(sy, ry), Copies(sq_s, sq_r), Copies(sc, rc)
    for part in (mates, rings, sums, states):
        part.me = (z, x, y, 1 - c)
    mate = (z, x, y, 1 - c)
    right, left = (z, x, (y + 1) % 4, c), (z, x, (y + 3) % 4, c)
    cs = carry[...].astype(BF)
    carry_o[y] = cs
    for k in range(1, 4):
        states.go(carry_o.at[y], carry_o.at[y], k - 1, (z, x, (y + k) % 4, c))
    hot = head_hot()
    ones = jnp.ones((8, CH), BF)

    def partial(dy, k, keep):
        t = (y + dy) % 4
        for part in range(2):
            core = c if part else 1 - c
            rows = pl.ds(pl.multiple_of(t * 256 + core * 128, 128), 128)
            full = y_in[rows, :] + expand(fac[rows, :], hot) * dot_nt(c_in[rows, :], cs)
            g = full * silu(gate[rows, :].astype(F32))
            g2 = g * g
            hi = g2.astype(BF)
            lo = (g2 - hi.astype(F32)).astype(BF)
            sq[t * 2 + core] = dot_nt(ones, hi) + dot_nt(ones, lo)
            gg = (g * gain[...]).astype(BF)
            for n in range(0, 1536, 512):
                got = dot_nt(gg, wout[n : n + 512, :]).astype(BF)
                if part:
                    keep[:, n : n + 512] = got
                else:
                    xs[k, :, n : n + 512] = got
            if not part:
                mates.go(xs.at[k], xr.at[k], k, mate)

    def join(k, keep):
        mates.arrived(xr.at[k], k)
        keep[...] = (keep[...].astype(F32) + xr[k].astype(F32)).astype(BF)

    partial(2, 0, opp)
    partial(1, 1, ahead)
    join(0, opp)
    rings.go(opp.at[pl.ds(0, 64)], low, 0, right)
    rings.go(opp.at[pl.ds(64, 64)], high, 1, left)
    partial(3, 2, behind)
    join(1, ahead)
    rings.arrived(low, 0)
    ahead[0:64, :] = (ahead[0:64, :].astype(F32) + low[...].astype(F32)).astype(BF)
    rings.go(ahead, from_l, 2, right)
    join(2, behind)
    rings.arrived(high, 1)
    behind[64:128, :] = (behind[64:128, :].astype(F32) + high[...].astype(F32)).astype(BF)
    rings.go(behind, from_r, 3, left)
    partial(0, 3, own)
    for k in range(1, 8):
        sums.go(sq.at[(q + k) % 8], sqr.at[q], k - 1, group[k - 1])
    sqr[q] = sq[q]
    for k in range(1, 8):
        sums.arrived(sqr.at[(q + 8 - k) % 8], k - 1)
    total = sqr[0]
    for k in range(1, 8):
        total = total + sqr[k]
    scale = lax.rsqrt(total / DI + EPS)
    scale = jnp.broadcast_to(scale[0:1, :], (128, 128)).T
    join(3, own)
    rings.arrived(from_l, 2)
    rings.arrived(from_r, 3)
    for n in range(0, 1536, 128):
        cols = slice(n, n + 128)
        whole = own[:, cols].astype(F32) + from_l[:, cols].astype(F32) + from_r[:, cols].astype(F32)
        out_o[:, cols] = (whole * scale).astype(BF)
    for k in range(1, 4):
        states.arrived(carry_o.at[(y + 4 - k) % 4], k - 1)
    for part in (mates, rings, sums, states):
        part.close()


def on_device(
    hidden_in, gate_proj, inner_proj, small_proj, row_layout, conv_inner, conv_shared,
    bias_inner, bias_shared, dt_bias, decay_log, skip_gain, norm_gain, out_proj,
    prompt_lengths, group_map, init_states, page_table,
):
    yi, ci = lax.axis_index("y"), lax.axis_index("tp")
    gi = lax.axis_index("z") * 4 + lax.axis_index("x")
    seq = gi * 4 + yi
    d = hidden_in.shape[1]

    feature = jnp.arange(d, dtype=jnp.int32)
    logical = jnp.repeat(row_layout * 12, 12) + feature % 12
    onehot = (feature[:, None] == logical[None, :]).astype(BF)
    half = lax.dynamic_slice_in_dim(hidden_in, ci * 128, 128, 0)
    half = dot(half, onehot).astype(BF)
    outp = jnp.pad(
        out_proj.astype(BF).T.reshape(24, 4, CH).transpose(1, 0, 2), ((0, 0), (0, 8), (0, 0))
    )
    vm = pl.BlockSpec(memory_space=pltpu.VMEM)
    anyw = pl.BlockSpec(memory_space=pl.ANY)
    dma = pltpu.SemaphoreType.DMA
    w, hid, edge, wo = pl.pallas_call(
        gather_kernel,
        in_specs=[vm] * 5,
        out_specs=[anyw, anyw, anyw, vm],
        out_shape=[
            jax.ShapeDtypeStruct((16, 96, 3 * CH), BF),
            jax.ShapeDtypeStruct((8, 128, d), BF),
            jax.ShapeDtypeStruct((16, d), BF),
            jax.ShapeDtypeStruct((96, CH), BF),
        ],
        scratch_shapes=[
            pltpu.VMEM((8, 16, 3 * CH), BF),
            pltpu.VMEM((8, 16, 3 * CH), BF),
            pltpu.VMEM((96, 3 * CH), BF),
            pltpu.VMEM((4, 32, CH), BF),
            dma((7,)), dma((7,)),
            dma((3,)), dma((3,)),
            dma((20,)), dma((20,)),
            dma((4,)), dma((4,)),
            dma((4,)), dma((4,)),
            dma((1,)), dma((1,)),
            dma((2,)),
        ],
        compiler_params=pltpu.CompilerParams(
            collective_id=0, has_side_effects=True, vmem_limit_bytes=40 << 20
        ),
        name="gather",
    )(gate_proj, inner_proj, small_proj, outp, half)
    w = w.reshape(d, 3 * CH)
    hid = hid.reshape(1024, d)

    chan = jnp.concatenate(
        [
            conv_inner,
            bias_inner[None],
            jnp.repeat(dt_bias, HEAD)[None],
            jnp.repeat(skip_gain, HEAD)[None],
            norm_gain[None],
        ],
        axis=0,
    )
    cshared = jnp.concatenate([conv_shared, bias_shared[None], jnp.zeros((3, 256), F32)], axis=0)
    heads = jnp.stack([dt_bias, -jnp.exp(decay_log)])
    heads = jnp.pad(lax.dynamic_slice_in_dim(heads, yi * MINE, MINE, 1), ((0, 6), (0, 122)))
    place = jnp.stack([gi, ci * 24 + yi * MINE, yi]).astype(jnp.int32)
    init = init_states.reshape(4, 24 * HEAD, N)

    def spec(shape, index):
        return pl.BlockSpec(shape, index)

    const2 = lambda i, *_: (0, 0)
    tok2 = lambda i, *_: (i, 0)
    tok3 = lambda i, *_: (i, 0, 0)
    gate, y, c, fac, ends, dps = pl.pallas_call(
        local_kernel,
        grid_spec=pltpu.PrefetchScalarGridSpec(
            num_scalar_prefetch=3,
            grid=(4,),
            in_specs=[
                spec((256, d), tok2),
                spec((16, d), const2),
                spec((d, 3 * CH), const2),
                spec((8, CH), lambda i, p, *_: (0, p[2])),
                spec((8, 256), const2),
                spec((8, 128), const2),
                spec((4, CH, N), lambda i, p, *_: (0, p[2], 0)),
            ],
            out_specs=[
                spec((256, CH), tok2),
                spec((256, CH), tok2),
                spec((256, N), tok2),
                spec((256, 128), tok2),
                spec((2, CH, N), tok3),
                spec((2, 8, 128), tok3),
            ],
            scratch_shapes=[
                pltpu.VMEM((264, CH + 256), F32),
                pltpu.VMEM((CH, N), F32),
                pltpu.VMEM((8, 128), F32),
                pltpu.VMEM((8, 128), F32),
                pltpu.VMEM((128, CH), F32),
            ],
        ),
        out_shape=[
            jax.ShapeDtypeStruct((1024, CH), BF),
            jax.ShapeDtypeStruct((1024, CH), F32),
            jax.ShapeDtypeStruct((1024, N), BF),
            jax.ShapeDtypeStruct((1024, 128), F32),
            jax.ShapeDtypeStruct((8, CH, N), F32),
            jax.ShapeDtypeStruct((8, 8, 128), F32),
        ],
        compiler_params=pltpu.CompilerParams(
            dimension_semantics=("arbitrary",), vmem_limit_bytes=40 << 20
        ),
        name="local",
    )(place, prompt_lengths, group_map, hid, edge, w, chan, cshared, heads, init)

    carry, wout, page, rate = pl.pallas_call(
        scan_kernel,
        in_specs=[vm] * 5,
        out_specs=[vm, anyw, vm, vm],
        out_shape=[
            jax.ShapeDtypeStruct((3, 16, 8, N), F32),
            jax.ShapeDtypeStruct((16, 96, CH), BF),
            jax.ShapeDtypeStruct((4, 2, CH, N), BF),
            jax.ShapeDtypeStruct((4, 2, 8, N), F32),
        ],
        scratch_shapes=[
            pltpu.VMEM((16, 3, 8, N), F32),
            pltpu.VMEM((16, 8, N), F32),
            pltpu.VMEM((16, 3, 8, N), F32),
            pltpu.VMEM((8, CH, N), BF),
            dma((15,)), dma((15,)),
            dma((15,)), dma((15,)),
            dma((15,)), dma((15,)),
            dma((20,)), dma((20,)),
            dma((3,)), dma((3,)),
            dma((3,)), dma((3,)),
            dma((1,)),
        ],
        compiler_params=pltpu.CompilerParams(
            collective_id=1, has_side_effects=True, vmem_limit_bytes=40 << 20
        ),
        name="scan",
    )(ends[7].reshape(3, 16, 8, N), dps[7], wo, ends, dps)
    carry = carry.reshape(CH, N)
    wout = wout.reshape(d, CH)

    gain = lax.dynamic_slice_in_dim(norm_gain, yi * CH, CH, 0)[None]
    block = pltpu.VMEM((128, d), BF)
    halfb = pltpu.VMEM((64, d), BF)
    mixed, carries = pl.pallas_call(
        finish_kernel,
        in_specs=[vm] * 7,
        out_specs=[vm, vm],
        out_shape=[
            jax.ShapeDtypeStruct((128, d), BF),
            jax.ShapeDtypeStruct((4, CH, N), BF),
        ],
        scratch_shapes=[
            block, block, block, block,
            pltpu.VMEM((4, 128, d), BF),
            pltpu.VMEM((4, 128, d), BF),
            halfb, halfb, block, block,
            pltpu.VMEM((8, 8, 128), F32),
            pltpu.VMEM((8, 8, 128), F32),
            dma((4,)), dma((4,)),
            dma((4,)), dma((4,)),
            dma((7,)), dma((7,)),
            dma((3,)), dma((3,)),
        ],
        compiler_params=pltpu.CompilerParams(
            collective_id=2, has_side_effects=True, vmem_limit_bytes=40 << 20
        ),
        name="finish",
    )(y, gate, c, fac, carry, gain, wout)

    rate = rate[:, :, :MINE, None, :]
    pages = page.reshape(4, 2, MINE, HEAD, N).astype(F32)
    pages = pages + rate * carries.reshape(4, 1, MINE, HEAD, N).astype(F32)
    pages = pages.transpose(1, 0, 2, 3, 4).reshape(2, 4 * MINE, HEAD, N)
    swap = page_table[0] != seq * 2
    pages = jnp.where(swap, pages[::-1], pages)
    return (mixed, pages)


def solution(mesh):
    fine = Mesh(mesh.devices.reshape(4, 4, 4, 2), ("z", "x", "y", "tp"))
    seq = ("z", "x", "y")
    every = ("z", "x", "y", "tp")
    placed = (
        P(seq, None),
        P(every, None),
        P(every, None),
        P(every, None),
        P(),
        P(None, "tp"),
        P(),
        P("tp"),
        P(),
        P("tp"),
        P("tp"),
        P("tp"),
        P("tp"),
        P("tp", seq),
        P(),
        P(),
        P(None, "tp", None, None),
        P(seq),
    )
    return jax.shard_map(
        on_device,
        mesh=fine,
        in_specs=placed,
        out_specs=(P(every, None), P(seq, "tp", None, None)),
        check_vma=False,
    )
```

```python
import jax
import jax.numpy as jnp
from jax import lax
from jax.experimental import pallas as pl
from jax.experimental.pallas import tpu as pltpu
from jax.sharding import Mesh
from jax.sharding import PartitionSpec as P

N = 128
CONV = 4
PAGE = 128
DI = 3072
HEAD = 64
MINE = 6
CH = MINE * HEAD
EPS = 1e-05
BF = jnp.bfloat16
F32 = jnp.float32
NEG = -1e30


def dot(a, b):
    return jnp.dot(a, b, preferred_element_type=F32)


def dot_nt(a, b):
    return lax.dot_general(a, b, (((1,), (1,)), ((), ())), preferred_element_type=F32)


def dot_tn(a, b):
    return lax.dot_general(a, b, (((0,), (0,)), ((), ())), preferred_element_type=F32)


def silu(v):
    return v / (1.0 + jnp.exp(-v))


def softplus(v):
    return jnp.maximum(v, 0.0) + jnp.log1p(jnp.exp(-jnp.abs(v)))


def three(v):
    hi = v.astype(BF)
    rest = v - hi.astype(F32)
    mid = rest.astype(BF)
    return hi, mid, (rest - mid.astype(F32)).astype(BF)


def expand(v, hot):
    hi = v.astype(BF)
    lo = (v - hi.astype(F32)).astype(BF)
    return dot(hi, hot) + dot(lo, hot)


def head_hot():
    row = lax.broadcasted_iota(jnp.int32, (128, CH), 0)
    col = lax.broadcasted_iota(jnp.int32, (128, CH), 1)
    return (row == col // HEAD).astype(F32).astype(BF)


def wide(m):
    return jnp.concatenate([m, m, m], axis=1)


class Copies:
    def __init__(self, send, recv):
        self.send, self.recv, self.open = send, recv, []

    def go(self, src, dst, slot, device):
        copy = pltpu.make_async_remote_copy(
            src_ref=src,
            dst_ref=dst,
            send_sem=self.send.at[slot],
            recv_sem=self.recv.at[slot],
            device_id=device,
            device_id_type=pl.DeviceIdType.MESH,
        )
        copy.start()
        self.open.append(copy)

    def arrived(self, dst, slot):
        pltpu.make_async_remote_copy(
            src_ref=dst,
            dst_ref=dst,
            send_sem=self.send.at[slot],
            recv_sem=self.recv.at[slot],
            device_id=self.me,
            device_id_type=pl.DeviceIdType.MESH,
        ).wait_recv()

    def close(self):
        for copy in self.open:
            copy.wait_send()


def coords():
    return (
        lax.axis_index("z"),
        lax.axis_index("x"),
        lax.axis_index("y"),
        lax.axis_index("tp"),
    )


def greet(devices):
    barrier = pltpu.get_barrier_semaphore()
    for device in devices:
        pl.semaphore_signal(
            barrier, inc=1, device_id=device, device_id_type=pl.DeviceIdType.MESH
        )
    pl.semaphore_wait(barrier, len(devices))


class PlaneRing:
    def __init__(self, out, copies, rows):
        self.out, self.copies, self.half = out, copies, rows // 2
        z, x, y, c = coords()
        self.z, self.x, self.y, self.c = z, x, y, c
        self.a = x * (1 - c) + z * c
        self.b = z * (1 - c) + x * c

    def slot(self, da, db):
        a = (self.a + da + 4) % 4
        b = (self.b + db + 4) % 4
        return (b * 4 + a) * (1 - self.c) + (a * 4 + b) * self.c

    def device(self, da, db):
        a = (self.a + da + 4) % 4
        b = (self.b + db + 4) % 4
        c = self.c
        return (b * (1 - c) + a * c, a * (1 - c) + b * c, self.y, c)

    def full(self, da, db):
        return self.out.at[self.slot(da, db)]

    def part(self, da, db, low):
        return self.out.at[self.slot(da, db), pl.ds(0 if low else self.half, self.half)]

    def first(self, own):
        go = self.copies.go
        go(own, self.full(0, 0), 0, self.device(1, 0))
        go(own, self.full(0, 0), 1, self.device(-1, 0))
        go(own, self.full(0, 0), 4, self.device(0, 1))
        go(own, self.full(0, 0), 5, self.device(0, -1))

    def second(self, u, da):
        go = self.copies.go
        go(self.full(da, 0), self.full(da, 0), 4 + 4 * u, self.device(0, 1))
        go(self.full(da, 0), self.full(da, 0), 5 + 4 * u, self.device(0, -1))

    def along_a(self):
        go, arrived = self.copies.go, self.copies.arrived
        arrived(self.full(-1, 0), 0)
        go(self.part(-1, 0, True), self.part(-1, 0, True), 2, self.device(1, 0))
        self.second(1, -1)
        arrived(self.full(1, 0), 1)
        go(self.part(1, 0, False), self.part(1, 0, False), 3, self.device(-1, 0))
        self.second(2, 1)

    def along_b(self, u, da):
        go, arrived = self.copies.go, self.copies.arrived
        arrived(self.full(da, -1), 4 + 4 * u)
        go(self.part(da, -1, True), self.part(da, -1, True), 6 + 4 * u, self.device(0, 1))
        arrived(self.full(da, 1), 5 + 4 * u)
        go(self.part(da, 1, False), self.part(da, 1, False), 7 + 4 * u, self.device(0, -1))

    def across_a(self):
        arrived = self.copies.arrived
        arrived(self.part(2, 0, True), 2)
        arrived(self.part(2, 0, False), 3)
        self.second(3, 2)

    def finish(self):
        arrived = self.copies.arrived
        for u, da in enumerate((0, -1, 1, 2)):
            arrived(self.part(da, 2, True), 6 + 4 * u)
            arrived(self.part(da, 2, False), 7 + 4 * u)


def pack(width):
    row = lax.broadcasted_iota(jnp.int32, (96, 128), 0)
    col = lax.broadcasted_iota(jnp.int32, (96, 128), 1)
    padded = 128 // (96 // width)
    return (col == row // width * padded + row % width).astype(F32).astype(BF)


def gather_kernel(
    gate, inner, small, outp, half, w_o, hid_o, edge_o, wo_o,
    pieces, stage, unit, ostage, s1, r1, so, ro, su, ru, sh, rh, sc, rc, se, re, local,
):
    z, x, y, c = coords()
    q = y * 2 + c
    g = z * 4 + x
    after, before = (g + 1) % 16, (g + 15) % 16
    next_dev = (after // 4, after % 4, y, c)
    prev_dev = (before // 4, before % 4, y, c)
    pieces[...] = jnp.zeros_like(pieces)
    for t in range(8):
        a = 1536 * (t % 2) + CH * (t // 2)
        pieces[t, 0:12, 0:CH] = gate[:, a : a + CH].astype(BF)
        pieces[t, 0:12, CH : 2 * CH] = inner[:, a : a + CH].astype(BF)
        pieces[t, 0:12, 2 * CH : 2 * CH + 304] = small[...].astype(BF)

    group = [(z, x, ((q + k) % 8) // 2, (q + k) % 2) for k in range(1, 8)]
    greet(
        group
        + [(z, (x + 1) % 4, y, c), (z, (x + 3) % 4, y, c)]
        + [((z + 1) % 4, x, y, c), ((z + 3) % 4, x, y, c)]
        + [next_dev, prev_dev]
    )

    ones = Copies(s1, r1)
    outs = Copies(so, ro)
    hids = Copies(sh, rh)
    cross = Copies(sc, rc)
    units = Copies(su, ru)
    edges = Copies(se, re)
    for part in (ones, outs, hids, cross, units, edges):
        part.me = (z, x, y, 1 - c)
    for k in range(1, 8):
        t = (q + k) % 8
        ones.go(pieces.at[t], stage.at[q], k - 1, group[k - 1])
    for k in range(1, 4):
        t = (y + k) % 4
        outs.go(outp.at[t], ostage.at[y], k - 1, (z, x, t, c))
    right, left = (z, x, (y + 1) % 4, c), (z, x, (y + 3) % 4, c)
    mate = (z, x, y, 1 - c)

    def hslot(dy, core):
        return ((y + dy + 4) % 4) * 2 + core

    hids.go(half, hid_o.at[hslot(0, c)], 0, right)
    hids.go(half, hid_o.at[hslot(0, c)], 1, left)
    cross.go(half, hid_o.at[hslot(0, c)], 0, mate)
    keep = pltpu.make_async_copy(half, hid_o.at[hslot(0, c)], local.at[0])
    keep.start()
    stage[q] = pieces[q]
    ostage[y] = outp[y]

    for k in range(1, 8):
        ones.arrived(stage.at[(q + 8 - k) % 8], k - 1)
    packer = pack(12)
    for j in range(3):
        cols = slice(j * CH, j * CH + CH)
        unit[:, cols] = dot(packer, stage[:, :, cols].reshape(128, CH)).astype(BF)
    ring = PlaneRing(w_o, units, 96)
    ring.first(unit)
    mine = pltpu.make_async_copy(unit, w_o.at[g], local.at[1])
    mine.start()
    for k in range(1, 4):
        outs.arrived(ostage.at[(y + 4 - k) % 4], k - 1)
    wo_o[...] = dot(pack(24), ostage[...].reshape(128, CH)).astype(BF)

    ring.along_a()
    hids.arrived(hid_o.at[hslot(-1, c)], 0)
    hids.go(
        hid_o.at[hslot(-1, c), pl.ds(0, 64)], hid_o.at[hslot(-1, c), pl.ds(0, 64)], 2, right
    )
    hids.arrived(hid_o.at[hslot(1, c)], 1)
    hids.go(
        hid_o.at[hslot(1, c), pl.ds(64, 64)], hid_o.at[hslot(1, c), pl.ds(64, 64)], 3, left
    )
    cross.go(hid_o.at[hslot(-1, c)], hid_o.at[hslot(-1, c)], 1, mate)
    cross.go(hid_o.at[hslot(1, c)], hid_o.at[hslot(1, c)], 2, mate)
    ring.along_b(0, 0)
    ring.across_a()
    ring.along_b(1, -1)
    ring.along_b(2, 1)
    hids.arrived(hid_o.at[hslot(2, c), pl.ds(0, 64)], 2)
    hids.arrived(hid_o.at[hslot(2, c), pl.ds(64, 64)], 3)
    cross.go(hid_o.at[hslot(2, c)], hid_o.at[hslot(2, c)], 3, mate)
    keep.wait()
    cross.arrived(hid_o.at[hslot(0, 1 - c)], 0)
    cross.arrived(hid_o.at[hslot(-1, 1 - c)], 1)
    cross.arrived(hid_o.at[hslot(1, 1 - c)], 2)
    cross.arrived(hid_o.at[hslot(2, 1 - c)], 3)
    edges.go(hid_o.at[7, pl.ds(112, 16)], edge_o, 0, next_dev)
    ring.along_b(3, 2)
    ring.finish()
    edges.arrived(edge_o, 0)
    mine.wait()
    for part in (ones, outs, hids, cross, units, edges):
        part.close()


def local_kernel(
    where, lens, grps, hid, edge, w, chan, cshared, heads, init,
    gate_o, y_o, c_o, fac_o, end_o, dp_o,
    xs, state, dp, dprow, read,
):
    step = pl.program_id(0)
    base = where[0] * 1024 + step * 256
    starts = []
    total = jnp.int32(0)
    for k in range(8):
        starts.append(total)
        total = total + lens[k]
    hot = head_hot()

    @pl.when(step == 0)
    def _():
        e = edge[...]
        xs[0:8, 0:CH] = dot(e, w[:, CH : 2 * CH])[8:16].astype(BF).astype(F32)
        xs[0:8, CH:] = dot(e, w[:, 2 * CH : 2 * CH + 256])[8:16].astype(BF).astype(F32)
        state[...] = jnp.zeros_like(state)
        dp[...] = jnp.ones_like(dp)
        dprow[...] = jnp.ones_like(dprow)

    rows = hid[...]
    both = dot(rows, w[:, : 2 * CH]).astype(BF)
    gate_o[...] = both[:, :CH]
    xs[8:264, 0:CH] = both[:, CH:].astype(F32)
    sm = dot(rows, w[:, 2 * CH :]).astype(BF)
    xs[8:264, CH:] = sm[:, :256].astype(F32)
    step_all = sm[:, 256:]
    row = lax.broadcasted_iota(jnp.int32, (128, 128), 0)
    col = lax.broadcasted_iota(jnp.int32, (128, 128), 1)
    pick = (row == col + where[1]).astype(F32)
    pick = jnp.where(col < MINE, pick, 0.0).astype(BF)
    wrow = lax.broadcasted_iota(jnp.int32, (128, CH), 0)
    wcol = lax.broadcasted_iota(jnp.int32, (128, CH), 1)
    pickx = (wrow == wcol // HEAD + where[1]).astype(F32).astype(BF)
    dt6 = softplus(dot(step_all, pick) + heads[0:1, :])
    log6 = heads[1:2, :] * dt6
    dtx = softplus(dot(step_all, pickx) + chan[5:6, :])

    pos = base + lax.broadcasted_iota(jnp.int32, (256, 128), 0)
    first = jnp.zeros((256, 128), jnp.int32)
    for k in range(1, 8):
        first = jnp.where(pos >= starts[k], starts[k], first)
    off = pos - first
    x = chan[4:5, :] + jnp.zeros((256, CH), F32)
    bc = cshared[4:5, :] + jnp.zeros((256, 256), F32)
    for lag in range(CONV):
        ok = (off >= lag).astype(F32)
        sx = xs[8 - lag : 264 - lag, 0:CH]
        sb = xs[8 - lag : 264 - lag, CH:]
        x = x + chan[lag : lag + 1, :] * sx * wide(ok)
        bc = bc + cshared[lag : lag + 1, :] * sb * jnp.concatenate([ok, ok], axis=1)
    tail = xs[256:264, :]
    xs[0:8, :] = tail
    x = silu(x)
    bc = silu(bc)
    b_all = bc[:, :128].astype(BF)
    c_all = bc[:, 128:].astype(BF)
    c_o[...] = c_all
    xdt_all = x * dtx
    lane = lax.broadcasted_iota(jnp.int32, (128, 128), 1)

    for sub in range(2):
        lo, hi = sub * 128, sub * 128 + 128
        p0 = base + lo
        f0 = first[lo:hi, :]
        prow = p0 + col
        frow = jnp.zeros((128, 128), jnp.int32)
        for k in range(1, 8):
            frow = jnp.where(prow >= starts[k], starts[k], frow)
        mask = (row >= col) & (f0 == frow)
        maskb = mask.astype(F32).astype(BF)
        cum = jnp.zeros((128, 128), F32)
        for part in three(log6[lo:hi, :]):
            cum = cum + dot(maskb, part)
        cumt = cum.T
        c = c_all[lo:hi, :]
        b = b_all[lo:hi, :]
        scores = dot_nt(c, b)
        xdt = xdt_all[lo:hi, :]
        xdtb = xdt.astype(BF)
        carried = f0 < p0
        ecum = jnp.exp(cum)
        cf = c.astype(F32)
        read[...] = dot_nt(
            jnp.where(carried, cf, 0.0).astype(BF), state[...].astype(BF)
        )
        flast = jnp.int32(0)
        glast = grps[0]
        for k in range(1, 8):
            got = p0 + 127 >= starts[k]
            flast = jnp.where(got, starts[k], flast)
            glast = jnp.where(got, grps[k], glast)

        @pl.when(flast >= p0)
        def _():
            gid = jnp.zeros((128, 128), jnp.int32) + grps[0]
            pcol = p0 + row
            for k in range(1, 8):
                gid = jnp.where(pcol >= starts[k], grps[k], gid)
            gid = jnp.where(f0 < p0, -1, gid)
            acc = read[...]
            for g in range(4):
                acc = acc + dot_nt(
                    jnp.where(gid == g, cf, 0.0).astype(BF), init[g].astype(BF)
                )
            read[...] = acc

        y = expand(ecum, hot) * read[...] + chan[6:7, :] * x[lo:hi, :]
        pieces = []
        for pair in range(3):
            xp = xdtb[:, pair * 128 : pair * 128 + 128]
            got = []
            for h in (2 * pair, 2 * pair + 1):
                diff = cum[:, h : h + 1] - cumt[h : h + 1, :]
                mix = jnp.exp(jnp.where(mask, diff, NEG)) * scores
                got.append(dot(mix.astype(BF), xp))
            pieces.append(jnp.where(lane < HEAD, got[0], got[1]))
        y_o[lo:hi, :] = y + jnp.concatenate(pieces, axis=1)

        same = f0 == flast
        w6 = jnp.exp(jnp.where(same, cum[127:128, :] - cum, NEG))
        xw = (xdt * expand(w6, hot)).astype(BF)
        summary = dot_tn(xw, b)
        carry = (flast < p0).astype(jnp.int32)
        scale = jnp.exp(jnp.broadcast_to(cumt[0:8, 127:128], (8, 128)))
        fac_o[lo:hi, :] = jnp.where(carried, ecum, 0.0) * dprow[0:1, :]
        keep = carry.astype(F32)
        dp[...] = dp[...] * scale * keep
        dprow[...] = dprow[...] * jnp.exp(cum[127:128, :]) * keep
        for h in range(MINE):
            a, z = h * HEAD, h * HEAD + HEAD
            old = state[a:z, :] * keep + init[glast, a:z, :] * (1.0 - keep)
            state[a:z, :] = scale[h : h + 1, :] * old + summary[a:z, :]
        end_o[sub] = state[...]
        dp_o[sub] = dp[...]


def mix_kernel(
    s, dec, wo, ends, dps, y_in, gate, c_in, fac, gain,
    out_o, carry_o, page_o, rate_o,
    carry, w_o, parts, decs, befores, small, fx, sg,
    opp, ahead, behind, own, xs, xr, low, high, from_l, from_r, sq, sqr,
    sp, rp, sd, rd, sb, rb, su, ru, sg_s, sg_r, sh, rh,
    sm, rm, sy, ry, sq_s, sq_r, sc, rc, local,
):
    z, x, y, c = coords()
    g = z * 4 + x
    q = y * 2 + c
    peers = [(((g + k) % 16) // 4, ((g + k) % 16) % 4, y, c) for k in range(1, 16)]
    group = [(z, x, ((q + k) % 8) // 2, (q + k) % 2) for k in range(1, 8)]
    near = [(z, x, (y + k) % 4, c) for k in range(1, 4)]
    greet(peers + group)
    going, rates, back, units = Copies(sp, rp), Copies(sd, rd), Copies(sb, rb), Copies(su, ru)
    pages, decays = Copies(sg_s, sg_r), Copies(sh, rh)
    mates, rings, sums, states = Copies(sm, rm), Copies(sy, ry), Copies(sq_s, sq_r), Copies(sc, rc)
    mate = (z, x, y, 1 - c)
    right, left = (z, x, (y + 1) % 4, c), (z, x, (y + 3) % 4, c)
    for part in (going, rates, back, units, pages, decays, mates, rings, sums, states):
        part.me = mate
    for k in range(1, 16):
        going.go(s.at[:, (g + k) % 16], parts.at[g], k - 1, peers[k - 1])
        rates.go(dec, decs.at[g], k - 1, peers[k - 1])
    ring = PlaneRing(w_o, units, 96)
    ring.first(wo)
    mine = pltpu.make_async_copy(wo, w_o.at[g], local.at[0])
    mine.start()
    parts[g] = s[:, g]
    decs[g] = dec[...]
    for k in range(8):
        small[k] = ends[k].astype(BF)
    for k in range(1, 4):
        t = (y + k) % 4
        pages.go(small.at[pl.ds(t * 2, 2)], page_o.at[y], k - 1, near[k - 1])
        decays.go(dps.at[pl.ds(t * 2, 2)], rate_o.at[y], k - 1, near[k - 1])
    for k in range(2):
        page_o[y, k] = small[y * 2 + k]
        rate_o[y, k] = dps[y * 2 + k]
    for k in range(1, 16):
        going.arrived(parts.at[(g + 16 - k) % 16], k - 1)
        rates.arrived(decs.at[(g + 16 - k) % 16], k - 1)
    hb = g // 8
    run = [jnp.zeros((8, 128), F32) for _ in range(3)]
    for k in range(16):
        for j in range(3):
            befores[k, j] = run[j]
            run[j] = decs[k, pl.ds(hb + 2 * j, 1), :] * run[j] + parts[k, j]
    for k in range(1, 16):
        back.go(befores.at[(g + k) % 16], carry.at[:, g], k - 1, peers[k - 1])
    carry[:, g] = befores[g]
    ring.along_a()
    ring.along_b(0, 0)
    hot = head_hot()
    for k in range(8):
        rows = slice(k * 128, k * 128 + 128)
        fx[rows, :] = expand(fac[rows, :], hot)
        sg[rows, :] = silu(gate[rows, :].astype(F32))
    ring.across_a()
    ring.along_b(1, -1)
    ring.along_b(2, 1)
    ring.along_b(3, 2)
    for k in range(1, 16):
        back.arrived(carry.at[:, (g + 16 - k) % 16], k - 1)
    cs = carry[...].reshape(CH, N).astype(BF)
    carry_o[y] = cs
    for k in range(1, 4):
        states.go(carry_o.at[y], carry_o.at[y], k - 1, near[k - 1])
    ring.finish()
    mine.wait()
    ones = jnp.ones((8, CH), BF)

    def partial(dy, k, keep):
        t = (y + dy) % 4
        for part in range(2):
            core = c if part else 1 - c
            rows = pl.ds(pl.multiple_of(t * 256 + core * 128, 128), 128)
            full = y_in[rows, :] + fx[rows, :] * dot_nt(c_in[rows, :], cs)
            g = full * sg[rows, :]
            g2 = g * g
            hi = g2.astype(BF)
            lo = (g2 - hi.astype(F32)).astype(BF)
            sq[t * 2 + core] = dot_nt(ones, hi) + dot_nt(ones, lo)
            gg = (g * gain[...]).astype(BF)
            for n in range(0, 1536, 384):
                got = dot_nt(gg, w_o[n // 96 : n // 96 + 4].reshape(384, CH)).astype(BF)
                if part:
                    keep[:, n : n + 384] = got
                else:
                    xs[k, :, n : n + 384] = got
            if not part:
                mates.go(xs.at[k], xr.at[k], k, mate)

    def join(k, keep):
        mates.arrived(xr.at[k], k)
        keep[...] = (keep[...].astype(F32) + xr[k].astype(F32)).astype(BF)

    partial(2, 0, opp)
    partial(1, 1, ahead)
    join(0, opp)
    rings.go(opp.at[pl.ds(0, 64)], low, 0, right)
    rings.go(opp.at[pl.ds(64, 64)], high, 1, left)
    partial(3, 2, behind)
    join(1, ahead)
    rings.arrived(low, 0)
    ahead[0:64, :] = (ahead[0:64, :].astype(F32) + low[...].astype(F32)).astype(BF)
    rings.go(ahead, from_l, 2, right)
    join(2, behind)
    rings.arrived(high, 1)
    behind[64:128, :] = (behind[64:128, :].astype(F32) + high[...].astype(F32)).astype(BF)
    rings.go(behind, from_r, 3, left)
    partial(0, 3, own)
    for k in range(1, 8):
        sums.go(sq.at[(q + k) % 8], sqr.at[q], k - 1, group[k - 1])
    sqr[q] = sq[q]
    for k in range(1, 8):
        sums.arrived(sqr.at[(q + 8 - k) % 8], k - 1)
    total = sqr[0]
    for k in range(1, 8):
        total = total + sqr[k]
    scale = lax.rsqrt(total / DI + EPS)
    scale = jnp.broadcast_to(scale[0:1, :], (128, 128)).T
    join(3, own)
    rings.arrived(from_l, 2)
    rings.arrived(from_r, 3)
    for n in range(0, 1536, 128):
        cols = slice(n, n + 128)
        whole = own[:, cols].astype(F32) + from_l[:, cols].astype(F32) + from_r[:, cols].astype(F32)
        out_o[:, cols] = (whole * scale).astype(BF)
    for k in range(1, 4):
        t = (y + 4 - k) % 4
        states.arrived(carry_o.at[t], k - 1)
        pages.arrived(page_o.at[t], k - 1)
        decays.arrived(rate_o.at[t], k - 1)
    for part in (going, rates, back, units, pages, decays, mates, rings, sums, states):
        part.close()


def on_device(
    hidden_in, gate_proj, inner_proj, small_proj, row_layout, conv_inner, conv_shared,
    bias_inner, bias_shared, dt_bias, decay_log, skip_gain, norm_gain, out_proj,
    prompt_lengths, group_map, init_states, page_table,
):
    yi, ci = lax.axis_index("y"), lax.axis_index("tp")
    gi = lax.axis_index("z") * 4 + lax.axis_index("x")
    seq = gi * 4 + yi
    d = hidden_in.shape[1]

    feature = jnp.arange(d, dtype=jnp.int32)
    logical = jnp.repeat(row_layout * 12, 12) + feature % 12
    onehot = (feature[:, None] == logical[None, :]).astype(BF)
    half = lax.dynamic_slice_in_dim(hidden_in, ci * 128, 128, 0)
    half = dot(half, onehot).astype(BF)
    outp = jnp.pad(
        out_proj.astype(BF).T.reshape(24, 4, CH).transpose(1, 0, 2), ((0, 0), (0, 8), (0, 0))
    )
    vm = pl.BlockSpec(memory_space=pltpu.VMEM)
    anyw = pl.BlockSpec(memory_space=pl.ANY)
    dma = pltpu.SemaphoreType.DMA
    w, hid, edge, wo = pl.pallas_call(
        gather_kernel,
        in_specs=[vm] * 5,
        out_specs=[anyw, anyw, anyw, vm],
        out_shape=[
            jax.ShapeDtypeStruct((16, 96, 3 * CH), BF),
            jax.ShapeDtypeStruct((8, 128, d), BF),
            jax.ShapeDtypeStruct((16, d), BF),
            jax.ShapeDtypeStruct((96, CH), BF),
        ],
        scratch_shapes=[
            pltpu.VMEM((8, 16, 3 * CH), BF),
            pltpu.VMEM((8, 16, 3 * CH), BF),
            pltpu.VMEM((96, 3 * CH), BF),
            pltpu.VMEM((4, 32, CH), BF),
            dma((7,)), dma((7,)),
            dma((3,)), dma((3,)),
            dma((20,)), dma((20,)),
            dma((4,)), dma((4,)),
            dma((4,)), dma((4,)),
            dma((1,)), dma((1,)),
            dma((2,)),
        ],
        compiler_params=pltpu.CompilerParams(
            collective_id=0, has_side_effects=True, vmem_limit_bytes=10 << 20
        ),
        name="gather",
    )(gate_proj, inner_proj, small_proj, outp, half)
    w = w.reshape(d, 3 * CH)
    hid = hid.reshape(1024, d)

    chan = jnp.concatenate(
        [
            conv_inner,
            bias_inner[None],
            jnp.repeat(dt_bias, HEAD)[None],
            jnp.repeat(skip_gain, HEAD)[None],
            norm_gain[None],
        ],
        axis=0,
    )
    cshared = jnp.concatenate([conv_shared, bias_shared[None], jnp.zeros((3, 256), F32)], axis=0)
    heads = jnp.stack([dt_bias, -jnp.exp(decay_log)])
    heads = jnp.pad(lax.dynamic_slice_in_dim(heads, yi * MINE, MINE, 1), ((0, 6), (0, 122)))
    place = jnp.stack([gi, ci * 24 + yi * MINE, yi]).astype(jnp.int32)
    init = init_states.reshape(4, 24 * HEAD, N)

    def spec(shape, index):
        return pl.BlockSpec(shape, index)

    const2 = lambda i, *_: (0, 0)
    tok2 = lambda i, *_: (i, 0)
    tok3 = lambda i, *_: (i, 0, 0)
    gate, y, c, fac, ends, dps = pl.pallas_call(
        local_kernel,
        grid_spec=pltpu.PrefetchScalarGridSpec(
            num_scalar_prefetch=3,
            grid=(4,),
            in_specs=[
                spec((256, d), tok2),
                spec((16, d), const2),
                spec((d, 3 * CH), const2),
                spec((8, CH), lambda i, p, *_: (0, p[2])),
                spec((8, 256), const2),
                spec((8, 128), const2),
                spec((4, CH, N), lambda i, p, *_: (0, p[2], 0)),
            ],
            out_specs=[
                spec((256, CH), tok2),
                spec((256, CH), tok2),
                spec((256, N), tok2),
                spec((256, 128), tok2),
                spec((2, CH, N), tok3),
                spec((2, 8, 128), tok3),
            ],
            scratch_shapes=[
                pltpu.VMEM((264, CH + 256), F32),
                pltpu.VMEM((CH, N), F32),
                pltpu.VMEM((8, 128), F32),
                pltpu.VMEM((8, 128), F32),
                pltpu.VMEM((128, CH), F32),
            ],
        ),
        out_shape=[
            jax.ShapeDtypeStruct((1024, CH), BF),
            jax.ShapeDtypeStruct((1024, CH), F32),
            jax.ShapeDtypeStruct((1024, N), BF),
            jax.ShapeDtypeStruct((1024, 128), F32),
            jax.ShapeDtypeStruct((8, CH, N), F32),
            jax.ShapeDtypeStruct((8, 8, 128), F32),
        ],
        compiler_params=pltpu.CompilerParams(
            dimension_semantics=("arbitrary",), vmem_limit_bytes=22 << 20
        ),
        name="local",
    )(place, prompt_lengths, group_map, hid, edge, w, chan, cshared, heads, init)

    gain = lax.dynamic_slice_in_dim(norm_gain, yi * CH, CH, 0)[None]
    block = pltpu.VMEM((128, d), BF)
    halfb = pltpu.VMEM((64, d), BF)
    mixed, carries, page, rate = pl.pallas_call(
        mix_kernel,
        in_specs=[vm] * 10,
        out_specs=[vm] * 4,
        out_shape=[
            jax.ShapeDtypeStruct((128, d), BF),
            jax.ShapeDtypeStruct((4, CH, N), BF),
            jax.ShapeDtypeStruct((4, 2, CH, N), BF),
            jax.ShapeDtypeStruct((4, 2, 8, N), F32),
        ],
        scratch_shapes=[
            pltpu.VMEM((3, 16, 8, N), F32),
            pltpu.VMEM((16, 96, CH), BF),
            pltpu.VMEM((16, 3, 8, N), F32),
            pltpu.VMEM((16, 8, N), F32),
            pltpu.VMEM((16, 3, 8, N), F32),
            pltpu.VMEM((8, CH, N), BF),
            pltpu.VMEM((1024, CH), F32),
            pltpu.VMEM((1024, CH), F32),
            block, block, block, block,
            pltpu.VMEM((4, 128, d), BF),
            pltpu.VMEM((4, 128, d), BF),
            halfb, halfb, block, block,
            pltpu.VMEM((8, 8, 128), F32),
            pltpu.VMEM((8, 8, 128), F32),
            dma((15,)), dma((15,)),
            dma((15,)), dma((15,)),
            dma((15,)), dma((15,)),
            dma((20,)), dma((20,)),
            dma((3,)), dma((3,)),
            dma((3,)), dma((3,)),
            dma((4,)), dma((4,)),
            dma((4,)), dma((4,)),
            dma((7,)), dma((7,)),
            dma((3,)), dma((3,)),
            dma((1,)),
        ],
        compiler_params=pltpu.CompilerParams(
            collective_id=1, has_side_effects=True, vmem_limit_bytes=20 << 20
        ),
        name="mix",
    )(ends[7].reshape(3, 16, 8, N), dps[7], wo, ends, dps, y, gate, c, fac, gain)

    rate = rate[:, :, :MINE, None, :]
    pages = page.reshape(4, 2, MINE, HEAD, N).astype(F32)
    pages = pages + rate * carries.reshape(4, 1, MINE, HEAD, N).astype(F32)
    pages = pages.transpose(1, 0, 2, 3, 4).reshape(2, 4 * MINE, HEAD, N)
    swap = page_table[0] != seq * 2
    pages = jnp.where(swap, pages[::-1], pages)
    return (mixed, pages)


def solution(mesh):
    fine = Mesh(mesh.devices.reshape(4, 4, 4, 2), ("z", "x", "y", "tp"))
    seq = ("z", "x", "y")
    every = ("z", "x", "y", "tp")
    placed = (
        P(seq, None),
        P(every, None),
        P(every, None),
        P(every, None),
        P(),
        P(None, "tp"),
        P(),
        P("tp"),
        P(),
        P("tp"),
        P("tp"),
        P("tp"),
        P("tp"),
        P("tp", seq),
        P(),
        P(),
        P(None, "tp", None, None),
        P(seq),
    )
    return jax.shard_map(
        on_device,
        mesh=fine,
        in_specs=placed,
        out_specs=(P(every, None), P(seq, "tp", None, None)),
        check_vma=False,
    )
```

```python
import jax
import jax.numpy as jnp
from jax import lax
from jax.experimental import pallas as pl
from jax.experimental.pallas import tpu as pltpu
from jax.sharding import Mesh
from jax.sharding import PartitionSpec as P

N = 128
CONV = 4
PAGE = 128
DI = 3072
HEAD = 64
MINE = 6
CH = MINE * HEAD
EPS = 1e-05
BF = jnp.bfloat16
F32 = jnp.float32
NEG = -1e30


def dot(a, b):
    return jnp.dot(a, b, preferred_element_type=F32)


def dot_nt(a, b):
    return lax.dot_general(a, b, (((1,), (1,)), ((), ())), preferred_element_type=F32)


def dot_tn(a, b):
    return lax.dot_general(a, b, (((0,), (0,)), ((), ())), preferred_element_type=F32)


def silu(v):
    return v / (1.0 + jnp.exp(-v))


def softplus(v):
    return jnp.maximum(v, 0.0) + jnp.log1p(jnp.exp(-jnp.abs(v)))


def three(v):
    hi = v.astype(BF)
    rest = v - hi.astype(F32)
    mid = rest.astype(BF)
    return hi, mid, (rest - mid.astype(F32)).astype(BF)


def expand(v, hot):
    hi = v.astype(BF)
    lo = (v - hi.astype(F32)).astype(BF)
    return dot(hi, hot) + dot(lo, hot)


def head_hot():
    row = lax.broadcasted_iota(jnp.int32, (128, CH), 0)
    col = lax.broadcasted_iota(jnp.int32, (128, CH), 1)
    return (row == col // HEAD).astype(F32).astype(BF)


def wide(m):
    return jnp.concatenate([m, m, m], axis=1)


class Copies:
    def __init__(self, send, recv):
        self.send, self.recv, self.open = send, recv, []

    def go(self, src, dst, slot, device):
        copy = pltpu.make_async_remote_copy(
            src_ref=src,
            dst_ref=dst,
            send_sem=self.send.at[slot],
            recv_sem=self.recv.at[slot],
            device_id=device,
            device_id_type=pl.DeviceIdType.MESH,
        )
        copy.start()
        self.open.append(copy)

    def arrived(self, dst, slot):
        pltpu.make_async_remote_copy(
            src_ref=dst,
            dst_ref=dst,
            send_sem=self.send.at[slot],
            recv_sem=self.recv.at[slot],
            device_id=self.me,
            device_id_type=pl.DeviceIdType.MESH,
        ).wait_recv()

    def close(self):
        for copy in self.open:
            copy.wait_send()


def coords():
    return (
        lax.axis_index("z"),
        lax.axis_index("x"),
        lax.axis_index("y"),
        lax.axis_index("tp"),
    )


def greet(devices):
    barrier = pltpu.get_barrier_semaphore()
    for device in devices:
        pl.semaphore_signal(
            barrier, inc=1, device_id=device, device_id_type=pl.DeviceIdType.MESH
        )
    pl.semaphore_wait(barrier, len(devices))


class Plane:
    def __init__(self, out, copies, rows, relay):
        self.out, self.copies, self.half, self.relay = out, copies, rows // 2, relay
        z, x, y, c = coords()
        self.y, self.c = y, c
        self.a = x * (1 - c) + z * c
        self.b = z * (1 - c) + x * c

    def at(self, da, db):
        a = (self.a + da + 8) % 4
        b = (self.b + db + 8) % 4
        c = self.c
        return b * (1 - c) + a * c, a * (1 - c) + b * c

    def device(self, da, db):
        z, x = self.at(da, db)
        return (z, x, self.y, self.c)

    def full(self, d, db=0):
        z, x = self.at(-d, db)
        return self.out.at[z * 4 + x]

    def low(self, d, db):
        z, x = self.at(-d, db)
        return self.out.at[z * 4 + x, pl.ds(0, self.half)]

    def high(self, d, db):
        z, x = self.at(-d, db)
        return self.out.at[z * 4 + x, pl.ds(self.half, self.half)]

    def first(self, own):
        for d in (1, 3, 2):
            self.copies.go(own, self.full(0), d - 1, self.device(d, 0))
        self.second(0, own)

    def second(self, d, src=None):
        src = self.full(d) if src is None else src
        self.copies.go(src, self.full(d), 3 + 4 * d, self.device(0, 1))
        self.copies.go(src, self.full(d), 4 + 4 * d, self.device(0, -1))
        if d not in self.relay:
            self.copies.go(src, self.full(d), 5 + 4 * d, self.device(0, 2))

    def turn(self, d):
        self.copies.arrived(self.full(d), d - 1)
        self.second(d)

    def pass_on(self, d):
        self.copies.arrived(self.full(d, -1), 3 + 4 * d)
        if d in self.relay:
            self.copies.go(self.low(d, -1), self.low(d, -1), 5 + 4 * d, self.device(0, 1))
        self.copies.arrived(self.full(d, 1), 4 + 4 * d)
        if d in self.relay:
            self.copies.go(self.high(d, 1), self.high(d, 1), 6 + 4 * d, self.device(0, -1))

    def end(self, d):
        if d in self.relay:
            self.copies.arrived(self.low(d, 2), 5 + 4 * d)
            self.copies.arrived(self.high(d, 2), 6 + 4 * d)
        else:
            self.copies.arrived(self.full(d, 2), 5 + 4 * d)


def pack(width):
    row = lax.broadcasted_iota(jnp.int32, (96, 128), 0)
    col = lax.broadcasted_iota(jnp.int32, (96, 128), 1)
    padded = 128 // (96 // width)
    return (col == row // width * padded + row % width).astype(F32).astype(BF)


UNIT = 1024
COPY = {
    "stage": 7, "ostage": 3, "hid": 6, "cross": 4, "w": 19, "edge": 1, "wo": 19, "bc": 1,
    "part": 15, "rate": 15, "back": 15, "page": 3, "decay": 3,
    "mate": 4, "ring": 4, "sum": 7, "state": 3,
}


def buffers(d):
    vmem = pltpu.VMEM
    return {
        "pieces": vmem((8, 16, UNIT), BF),
        "stage": vmem((8, 16, UNIT), BF),
        "ostage": vmem((4, 32, CH), BF),
        "unit": vmem((96, UNIT), BF),
        "ounit": vmem((96, CH), BF),
        "half": vmem((128, d), BF),
        "w": vmem((16, 96, UNIT), BF),
        "wo": vmem((16, 96, CH), BF),
        "hid": vmem((8, 128, d), BF),
        "edge": vmem((16, d), BF),
        "initf": vmem((4, CH, N), F32),
        "initb": vmem((CH, 4 * N), BF),
        "sg": vmem((1024, CH), F32),
        "xs": vmem((1032, CH + 2 * N), F32),
        "bc": vmem((2, 1040, N), BF),
        "steps": vmem((1024, 128), BF),
        "y": vmem((1024, CH), F32),
        "xdt": vmem((1024, CH), BF),
        "b": vmem((1024, N), BF),
        "c": vmem((1024, N), BF),
        "cum": vmem((1024, 128), F32),
        "fx": vmem((1024, CH), F32),
        "state": vmem((3, 16, 8, N), F32),
        "small": vmem((9, CH, N), BF),
        "dps": vmem((8, 8, N), F32),
        "parts": vmem((16, 3, 8, N), F32),
        "decs": vmem((16, 8, N), F32),
        "befores": vmem((16, 3, 8, N), F32),
        "carry": vmem((3, 16, 8, N), F32),
        "carries": vmem((4, CH, N), BF),
        "pages": vmem((4, 2, CH, N), BF),
        "rates": vmem((4, 2, 8, N), F32),
        "opp": vmem((128, d), BF),
        "ahead": vmem((128, d), BF),
        "behind": vmem((128, d), BF),
        "own": vmem((128, d), BF),
        "xs_out": vmem((4, 128, d), BF),
        "xs_in": vmem((4, 128, d), BF),
        "low": vmem((64, d), BF),
        "high": vmem((64, d), BF),
        "from_l": vmem((128, d), BF),
        "from_r": vmem((128, d), BF),
        "sq": vmem((8, 8, 128), F32),
        "sqr": vmem((8, 8, 128), F32),
    }


def layer_kernel(
    hidden, gate_w, inner_w, small_w, layout, cinner, cshared, binner, bshared, hd, ngain, outp,
    lens, grps, init, pt, out_o, page_o, *refs,
):
    d = hidden.shape[1]
    names = list(buffers(d))
    r = dict(zip(names, refs))
    sems = refs[len(names):]
    z, x, y, c = coords()
    me_not = (z, x, y, 1 - c)
    cp = {}
    for i, name in enumerate(COPY):
        cp[name] = Copies(sems[2 * i], sems[2 * i + 1])
        cp[name].me = me_not
    local = sems[2 * len(COPY)]
    q = y * 2 + c
    g = z * 4 + x
    mate = me_not
    right, left = (z, x, (y + 1) % 4, c), (z, x, (y + 3) % 4, c)
    near = [(z, x, (y + k) % 4, c) for k in range(1, 4)]
    group = [(z, x, ((q + k) % 8) // 2, (q + k) % 2) for k in range(1, 8)]
    peers = [(((g + k) % 16) // 4, ((g + k) % 16) % 4, y, c) for k in range(1, 16)]
    next_dev = peers[0]
    barrier = pltpu.get_barrier_semaphore()
    for device in group + peers:
        pl.semaphore_signal(
            barrier, inc=1, device_id=device, device_id_type=pl.DeviceIdType.MESH
        )

    fetch = pltpu.make_async_copy(
        init.at[:, pl.ds(pl.multiple_of(y * CH, CH), CH)], r["initf"], local.at[0]
    )
    fetch.start()
    pieces, stage = r["pieces"], r["stage"]
    pieces[...] = jnp.zeros_like(pieces)
    for t in range(8):
        a = 1536 * (t % 2) + CH * (t // 2)
        pieces[t, 0:12, 0:CH] = gate_w[:, a : a + CH].astype(BF)
        pieces[t, 0:12, CH : 2 * CH] = inner_w[:, a : a + CH].astype(BF)
        b = N * (t % 2)
        pieces[t, 0:12, 2 * CH : 2 * CH + N] = small_w[:, b : b + N].astype(BF)
        pieces[t, 0:12, 2 * CH + N : 2 * CH + N + 48] = small_w[:, 2 * N :].astype(BF)
    pl.semaphore_wait(barrier, len(group) + len(peers))

    for k in range(1, 8):
        cp["stage"].go(pieces.at[(q + k) % 8], stage.at[q], k - 1, group[k - 1])
    for k in range(1, 4):
        cp["ostage"].go(outp.at[(y + k) % 4], r["ostage"].at[y], k - 1, near[k - 1])
    stage[q] = pieces[q]
    r["ostage"][y] = outp[y]

    half = r["half"]
    lay = jnp.broadcast_to(layout[...], (8, 128)).astype(F32).astype(BF)
    rows = hidden[pl.ds(pl.multiple_of(c * 128, 128), 128), :]
    for j in range(0, d, CH):
        brow = lax.broadcasted_iota(jnp.int32, (128, CH), 0)
        bcol = lax.broadcasted_iota(jnp.int32, (128, CH), 1) + j
        block = dot(lay, (brow == bcol // 12).astype(F32).astype(BF))[0:1]
        want = block * 12.0 + (bcol[0:1] % 12).astype(F32)
        frow = lax.broadcasted_iota(jnp.int32, (d, CH), 0).astype(F32)
        pick = jnp.where(frow == want, 1.0, 0.0).astype(BF)
        half[:, j : j + CH] = dot(rows, pick).astype(BF)

    hid = r["hid"]

    def hslot(dy, core):
        return ((y + dy + 4) % 4) * 2 + core

    def hpart(dy, low):
        return hid.at[hslot(dy, c), pl.ds(0 if low else 64, 64)]

    lo, hi = pl.ds(0, 64), pl.ds(64, 64)
    cp["hid"].go(half.at[lo], hpart(0, True), 0, right)
    cp["hid"].go(half.at[hi], hpart(0, False), 2, left)
    cp["hid"].go(half.at[hi], hpart(0, False), 1, right)
    cp["hid"].go(half.at[lo], hpart(0, True), 3, left)
    cp["cross"].go(half, hid.at[hslot(0, c)], 0, mate)
    hid[q] = half[...]

    for k in range(1, 8):
        cp["stage"].arrived(stage.at[(q + 8 - k) % 8], k - 1)
    packer = pack(12)
    for j in range(0, UNIT, 512):
        r["unit"][:, j : j + 512] = dot(
            packer, stage[:, :, j : j + 512].reshape(128, 512)
        ).astype(BF)
    ring = Plane(r["w"], cp["w"], 96, (0, 1, 3))
    ring.first(r["unit"])
    mine = pltpu.make_async_copy(r["unit"], r["w"].at[g], local.at[1])
    mine.start()
    for k in range(1, 4):
        cp["ostage"].arrived(r["ostage"].at[(y + 4 - k) % 4], k - 1)
    r["ounit"][...] = dot(pack(24), r["ostage"][...].reshape(128, CH)).astype(BF)
    fetch.wait()
    for k in range(4):
        r["initb"][:, k * N : k * N + N] = r["initf"][k].astype(BF)

    cp["hid"].arrived(hpart(-1, True), 0)
    cp["hid"].go(hpart(-1, True), hpart(-1, True), 4, right)
    cp["hid"].arrived(hpart(1, False), 2)
    cp["hid"].go(hpart(1, False), hpart(1, False), 5, left)
    ring.turn(1)
    ring.turn(3)
    ring.turn(2)
    ring.pass_on(0)
    cp["hid"].arrived(hpart(-1, False), 1)
    cp["cross"].go(hid.at[hslot(-1, c)], hid.at[hslot(-1, c)], 1, mate)
    cp["hid"].arrived(hpart(1, True), 3)
    cp["cross"].go(hid.at[hslot(1, c)], hid.at[hslot(1, c)], 2, mate)
    ring.pass_on(1)
    ring.pass_on(3)
    oring = Plane(r["wo"], cp["wo"], 96, ())
    cp["hid"].arrived(hpart(2, True), 4)
    cp["hid"].arrived(hpart(2, False), 5)
    cp["cross"].go(hid.at[hslot(2, c)], hid.at[hslot(2, c)], 3, mate)
    for k, dy in enumerate((0, -1, 1, 2)):
        cp["cross"].arrived(hid.at[hslot(dy, 1 - c)], k)
    cp["edge"].go(hid.at[7, pl.ds(112, 16)], r["edge"], 0, next_dev)
    ring.pass_on(2)
    for k in range(4):
        ring.end(k)
    mine.wait()
    oring.first(r["ounit"])
    mine = pltpu.make_async_copy(r["ounit"], r["wo"].at[g], local.at[1])
    mine.start()

    w, xs, bc, steps, sg = r["w"], r["xs"], r["bc"], r["steps"], r["sg"]

    def columns(a, z):
        return w[:, :, a:z].reshape(d, z - a)

    cp["edge"].arrived(r["edge"], 0)
    bc[c, 0:16, :] = dot(r["edge"][...], columns(2 * CH, 2 * CH + N)).astype(BF)

    def project_bc(i, _):
        at = pl.multiple_of(i * 256, 256)
        got = dot(hid[pl.ds(i * 2, 2)].reshape(256, d), columns(2 * CH, UNIT)).astype(BF)
        bc[c, pl.ds(pl.multiple_of(at + 16, 16), 256), :] = got[:, :N]
        steps[pl.ds(at, 256), :] = got[:, N:]
        return 0

    lax.fori_loop(0, 4, project_bc, 0)
    cp["bc"].go(bc.at[c], bc.at[c], 0, mate)
    xs[0:8, 0:CH] = dot(r["edge"][...], columns(CH, 2 * CH))[8:16].astype(BF).astype(F32)

    def project(i, _):
        at = pl.multiple_of(i * 256, 256)
        got = dot(hid[pl.ds(i * 2, 2)].reshape(256, d), columns(0, 2 * CH)).astype(BF)
        sg[pl.ds(at, 256), :] = got[:, :CH].astype(F32)
        xs[pl.ds(pl.multiple_of(at + 8, 8), 256), 0:CH] = got[:, CH:].astype(F32)
        return 0

    lax.fori_loop(0, 4, project, 0)
    for k in (1, 3, 2):
        oring.turn(k)
    cp["bc"].arrived(bc.at[1 - c], 0)
    for k in range(2):
        xs[0:8, CH + k * N : CH + k * N + N] = bc[k, 0:16, :].astype(F32)[8:16]
        xs[8:1032, CH + k * N : CH + k * N + N] = bc[k, 16:1040, :].astype(F32)

    hot = head_hot()
    starts = []
    total = jnp.int32(0)
    for k in range(8):
        starts.append(total)
        total = total + lens[k]
    mychan = pl.ds(pl.multiple_of(y * CH, CH), CH)
    row = lax.broadcasted_iota(jnp.int32, (128, 128), 0)
    col = lax.broadcasted_iota(jnp.int32, (128, 128), 1)
    head0 = c * 24 + y * MINE
    pick = jnp.where(col < MINE, (row == col + head0).astype(F32), 0.0).astype(BF)
    local6 = jnp.where(col < MINE, (row == col + y * MINE).astype(F32), 0.0).astype(BF)
    wrow = lax.broadcasted_iota(jnp.int32, (128, CH), 0)
    wcol = lax.broadcasted_iota(jnp.int32, (128, CH), 1)
    pickx = (wrow == wcol // HEAD + head0).astype(F32).astype(BF)
    localx = (wrow == wcol // HEAD + y * MINE).astype(F32).astype(BF)
    hv = hd[...]
    hsplit = three(hv)
    heads6 = sum(dot(part, local6) for part in hsplit)
    headsx = sum(dot(part, localx) for part in hsplit)
    rate6 = jnp.where(col[0:1] < MINE, -jnp.exp(heads6[1:2]), 0.0)
    bias6, biasx, skipx = heads6[0:1], headsx[0:1], headsx[2:3]
    taps = cinner[:, mychan]
    biasc = binner[:, mychan]
    state, small, dps = r["state"], r["small"], r["dps"]
    small[0] = jnp.zeros((CH, N), BF)

    def find(pos):
        first = jnp.zeros(pos.shape, jnp.int32)
        for k in range(1, 8):
            first = jnp.where(pos >= starts[k], starts[k], first)
        return first

    def advance(i, held):
        old, dp, dprow = held
        at = pl.multiple_of(i * 256, 256)
        base = g * 1024 + i * 256
        first = find(base + lax.broadcasted_iota(jnp.int32, (256, 128), 0))
        off = base + lax.broadcasted_iota(jnp.int32, (256, 128), 0) - first
        xc = biasc + jnp.zeros((256, CH), F32)
        bcc = bshared[...] + jnp.zeros((256, 2 * N), F32)
        window = xs[pl.ds(at, 264), :]
        for lag in range(CONV):
            ok = (off >= lag).astype(F32)
            part = window[8 - lag : 264 - lag, :]
            xc = xc + taps[lag : lag + 1, :] * part[:, :CH] * wide(ok)
            bcc = bcc + cshared[lag : lag + 1, :] * part[:, CH:] * jnp.concatenate([ok, ok], axis=1)
        xc = silu(xc)
        bcc = silu(bcc)
        b_all = bcc[:, :N].astype(BF)
        r["b"][pl.ds(at, 256), :] = b_all
        r["c"][pl.ds(at, 256), :] = bcc[:, N:].astype(BF)
        step = steps[pl.ds(at, 256), :]
        dt6 = softplus(dot(step, pick) + bias6)
        log6 = rate6 * dt6
        dtx = softplus(dot(step, pickx) + biasx)
        xdt_all = xc * dtx
        r["xdt"][pl.ds(at, 256), :] = xdt_all.astype(BF)
        r["y"][pl.ds(at, 256), :] = skipx * xc
        for sub in range(2):
            k = i * 2 + sub
            p0 = base + sub * 128
            rows = slice(sub * 128, sub * 128 + 128)
            f0 = first[rows, :]
            mask = (row >= col) & (f0 == find(p0 + col))
            maskb = mask.astype(F32).astype(BF)
            cum = sum(dot(maskb, part) for part in three(log6[rows, :]))
            there = pl.ds(pl.multiple_of(at + sub * 128, 128), 128)
            r["cum"][there, :] = cum
            cumt = cum.T
            flast = jnp.int32(0)
            glast = grps[0]
            for j in range(1, 8):
                got = p0 + 127 >= starts[j]
                flast = jnp.where(got, starts[j], flast)
                glast = jnp.where(got, grps[j], glast)
            w6 = jnp.exp(jnp.where(f0 == flast, cum[127:128, :] - cum, NEG))
            xw = (xdt_all[rows, :] * expand(w6, hot)).astype(BF)
            summary = dot_tn(xw, b_all[rows, :])
            keep = (flast < p0).astype(F32)
            ecum = jnp.exp(cum)
            r["fx"][there, :] = expand(
                jnp.where(f0 < p0, ecum, 0.0) * dprow, hot
            )
            scale = jnp.exp(jnp.broadcast_to(cumt[0:8, 127:128], (8, 128)))
            dp = dp * scale * keep
            dprow = dprow * jnp.exp(cum[127:128, :]) * keep
            dps[k] = dp
            start = r["initf"][0]
            for j in range(1, 4):
                start = jnp.where(glast == j, r["initf"][j], start)
            old = jnp.where(flast < p0, old, start)
            old = jnp.concatenate(
                [scale[h : h + 1, :] * old[h * HEAD : h * HEAD + HEAD, :] for h in range(MINE)], axis=0
            ) + summary
            small[k + 1] = old.astype(BF)
        return old, dp, dprow

    last, dplast, _ = lax.fori_loop(
        0, 4, advance, (jnp.zeros((CH, N), F32), jnp.ones((8, 128), F32), jnp.ones((1, 128), F32))
    )
    state[...] = last.reshape(3, 16, 8, N)

    parts, decs, befores, carry = r["parts"], r["decs"], r["befores"], r["carry"]
    for k in range(1, 16):
        cp["part"].go(state.at[:, (g + k) % 16], parts.at[g], k - 1, peers[k - 1])
        cp["rate"].go(dps.at[7], decs.at[g], k - 1, peers[k - 1])
    parts[g] = state[:, g]
    decs[g] = dps[7]
    for k in range(1, 4):
        t = (y + k) % 4
        cp["page"].go(small.at[pl.ds(t * 2 + 1, 2)], r["pages"].at[y], k - 1, near[k - 1])
        cp["decay"].go(dps.at[pl.ds(t * 2, 2)], r["rates"].at[y], k - 1, near[k - 1])
    for k in range(2):
        r["pages"][y, k] = small[y * 2 + 1 + k]
        r["rates"][y, k] = dps[y * 2 + k]

    def inside(i, _):
        for sub in range(2):
            k = i * 2 + sub
            p0 = g * 1024 + k * 128
            at = pl.ds(pl.multiple_of(k * 128, 128), 128)
            f0 = find(p0 + row)
            mask = (row >= col) & (f0 == find(p0 + col))
            cum = r["cum"][at, :]
            cumt = cum.T
            cb = r["c"][at, :]
            cf = cb.astype(F32)
            scores = dot_nt(cb, r["b"][at, :])
            gid = jnp.zeros((128, 128), jnp.int32) + grps[0]
            for j in range(1, 8):
                gid = jnp.where(p0 + row >= starts[j], grps[j], gid)
            gid = jnp.where(f0 < p0, 4, gid)
            chot = jnp.concatenate(
                [jnp.where(gid == j, cf, 0.0).astype(BF) for j in range(4)], axis=1
            )
            read = dot_nt(jnp.where(gid == 4, cf, 0.0).astype(BF), small[k])
            read = read + dot_nt(chot, r["initb"][...])
            lane = col
            pieces = []
            for pair in range(3):
                xp = r["xdt"][at, pair * 128 : pair * 128 + 128]
                got = []
                for h in (2 * pair, 2 * pair + 1):
                    diff = cum[:, h : h + 1] - cumt[h : h + 1, :]
                    mix = jnp.exp(jnp.where(mask, diff, NEG)) * scores
                    got.append(dot(mix.astype(BF), xp))
                pieces.append(jnp.where(lane < HEAD, got[0], got[1]))
            r["y"][at, :] = (
                r["y"][at, :] + expand(jnp.exp(cum), hot) * read + jnp.concatenate(pieces, axis=1)
            )
            sg[at, :] = silu(sg[at, :])
        return 0

    lax.fori_loop(0, 2, inside, 0)
    for k in range(1, 16):
        cp["part"].arrived(parts.at[(g + 16 - k) % 16], k - 1)
        cp["rate"].arrived(decs.at[(g + 16 - k) % 16], k - 1)
    hb = g // 8
    run = [jnp.zeros((8, 128), F32) for _ in range(3)]
    for k in range(16):
        for j in range(3):
            befores[k, j] = run[j]
            run[j] = decs[k, pl.ds(hb + 2 * j, 1), :] * run[j] + parts[k, j]
    for k in range(1, 16):
        cp["back"].go(befores.at[(g + k) % 16], carry.at[:, g], k - 1, peers[k - 1])
    carry[:, g] = befores[g]
    for k in range(4):
        oring.pass_on(k)
        oring.end(k)
    mine.wait()
    lax.fori_loop(2, 4, inside, 0)
    for k in range(1, 16):
        cp["back"].arrived(carry.at[:, (g + 16 - k) % 16], k - 1)

    carries = r["carries"]
    cs = carry[...].reshape(CH, N).astype(BF)
    carries[y] = cs
    for k in range(1, 4):
        cp["state"].go(carries.at[y], carries.at[y], k - 1, near[k - 1])
    ones = jnp.ones((8, CH), BF)
    gain = ngain[:, mychan]
    xs_out, xs_in, sq, sqr = r["xs_out"], r["xs_in"], r["sq"], r["sqr"]

    def partial(dy, k, keep):
        t = (y + dy) % 4
        for part in range(2):
            core = c if part else 1 - c
            at = pl.ds(pl.multiple_of(t * 256 + core * 128, 128), 128)
            full = r["y"][at, :] + r["fx"][at, :] * dot_nt(r["c"][at, :], cs)
            gv = full * sg[at, :]
            g2 = gv * gv
            top = g2.astype(BF)
            rest = (g2 - top.astype(F32)).astype(BF)
            sq[t * 2 + core] = dot_nt(ones, top) + dot_nt(ones, rest)
            gg = (gv * gain).astype(BF)
            for n in range(0, 1536, CH):
                got = dot_nt(gg, r["wo"][n // 96 : n // 96 + 4].reshape(CH, CH)).astype(BF)
                if part:
                    keep[:, n : n + CH] = got
                else:
                    xs_out[k, :, n : n + CH] = got
            if not part:
                cp["mate"].go(xs_out.at[k], xs_in.at[k], k, mate)

    def join(k, keep):
        cp["mate"].arrived(xs_in.at[k], k)
        keep[...] = (keep[...].astype(F32) + xs_in[k].astype(F32)).astype(BF)

    opp, ahead, behind, own = r["opp"], r["ahead"], r["behind"], r["own"]
    partial(2, 0, opp)
    partial(1, 1, ahead)
    join(0, opp)
    cp["ring"].go(opp.at[lo], r["low"], 0, right)
    cp["ring"].go(opp.at[hi], r["high"], 1, left)
    partial(3, 2, behind)
    join(1, ahead)
    cp["ring"].arrived(r["low"], 0)
    ahead[0:64, :] = (ahead[0:64, :].astype(F32) + r["low"][...].astype(F32)).astype(BF)
    cp["ring"].go(ahead, r["from_l"], 2, right)
    join(2, behind)
    cp["ring"].arrived(r["high"], 1)
    behind[64:128, :] = (behind[64:128, :].astype(F32) + r["high"][...].astype(F32)).astype(BF)
    cp["ring"].go(behind, r["from_r"], 3, left)
    partial(0, 3, own)
    for k in range(1, 8):
        cp["sum"].go(sq.at[(q + k) % 8], sqr.at[q], k - 1, group[k - 1])
    sqr[q] = sq[q]
    join(3, own)

    swap = pt[0] != (g * 4 + y) * 2
    for k in range(4):
        t = (y + 4 - k) % 4
        if k:
            cp["state"].arrived(carries.at[t], k - 1)
            cp["page"].arrived(r["pages"].at[t], k - 1)
            cp["decay"].arrived(r["rates"].at[t], k - 1)
        for h in range(MINE):
            at = slice(h * HEAD, h * HEAD + HEAD)
            came = carries[t, at, :].astype(F32)
            one, two = (
                r["pages"][t, j, at, :].astype(F32) + r["rates"][t, j, h : h + 1, :] * came
                for j in range(2)
            )
            page_o[0, t, at, :] = jnp.where(swap, two, one)
            page_o[1, t, at, :] = jnp.where(swap, one, two)

    for k in range(1, 8):
        cp["sum"].arrived(sqr.at[(q + 8 - k) % 8], k - 1)
    total = sqr[0]
    for k in range(1, 8):
        total = total + sqr[k]
    scale = lax.rsqrt(total / DI + EPS)
    scale = jnp.broadcast_to(scale[0:1, :], (128, 128)).T
    cp["ring"].arrived(r["from_l"], 2)
    cp["ring"].arrived(r["from_r"], 3)
    for n in range(0, 1536, 128):
        cols = slice(n, n + 128)
        whole = sum(v[:, cols].astype(F32) for v in (own, r["from_l"], r["from_r"]))
        out_o[:, cols] = (whole * scale).astype(BF)
    for name in COPY:
        cp[name].close()


def on_device(
    hidden_in, gate_proj, inner_proj, small_proj, row_layout, conv_inner, conv_shared,
    bias_inner, bias_shared, dt_bias, decay_log, skip_gain, norm_gain, out_proj,
    prompt_lengths, group_map, init_states, page_table,
):
    d = hidden_in.shape[1]
    outp = jnp.pad(
        out_proj.astype(BF).T.reshape(24, 4, CH).transpose(1, 0, 2), ((0, 0), (0, 8), (0, 0))
    )
    hd = jnp.pad(jnp.stack([dt_bias, decay_log, skip_gain]), ((0, 5), (0, 104)))
    vm = pl.BlockSpec(memory_space=pltpu.VMEM)
    sm = pl.BlockSpec(memory_space=pltpu.SMEM)
    dma = pltpu.SemaphoreType.DMA
    scratch = list(buffers(d).values())
    for count in COPY.values():
        scratch += [dma((count,)), dma((count,))]
    mixed, pages = pl.pallas_call(
        layer_kernel,
        in_specs=[vm] * 12 + [sm, sm, pl.BlockSpec(memory_space=pl.ANY), sm],
        out_specs=[vm, vm],
        out_shape=[
            jax.ShapeDtypeStruct((128, d), BF),
            jax.ShapeDtypeStruct((2, 4, CH, N), F32),
        ],
        scratch_shapes=scratch + [dma((2,))],
        compiler_params=pltpu.CompilerParams(
            collective_id=0, has_side_effects=True, vmem_limit_bytes=48 << 20
        ),
        name="layer",
    )(
        hidden_in, gate_proj, inner_proj, small_proj, row_layout[None], conv_inner, conv_shared,
        bias_inner[None], bias_shared[None], hd, norm_gain[None], outp,
        prompt_lengths, group_map, init_states.reshape(4, 24 * HEAD, N), page_table,
    )
    return (mixed, pages.reshape(2, 24, HEAD, N))


def solution(mesh):
    fine = Mesh(mesh.devices.reshape(4, 4, 4, 2), ("z", "x", "y", "tp"))
    seq = ("z", "x", "y")
    every = ("z", "x", "y", "tp")
    placed = (
        P(seq, None),
        P(every, None),
        P(every, None),
        P(every, None),
        P(),
        P(None, "tp"),
        P(),
        P("tp"),
        P(),
        P("tp"),
        P("tp"),
        P("tp"),
        P("tp"),
        P("tp", seq),
        P(),
        P(),
        P(None, "tp", None, None),
        P(seq),
    )
    return jax.shard_map(
        on_device,
        mesh=fine,
        in_specs=placed,
        out_specs=(P(every, None), P(seq, "tp", None, None)),
        check_vma=False,
    )
```

```python
import jax
import jax.numpy as jnp
from jax import lax
from jax.experimental import pallas as pl
from jax.experimental.pallas import tpu as pltpu
from jax.sharding import Mesh
from jax.sharding import PartitionSpec as P

N = 128
CONV = 4
PAGE = 128
DI = 3072
HEAD = 64
MINE = 6
CH = MINE * HEAD
EPS = 1e-05
BF = jnp.bfloat16
F32 = jnp.float32
NEG = -1e30


def dot(a, b):
    return jnp.dot(a, b, preferred_element_type=F32)


def dot_nt(a, b):
    return lax.dot_general(a, b, (((1,), (1,)), ((), ())), preferred_element_type=F32)


def dot_tn(a, b):
    return lax.dot_general(a, b, (((0,), (0,)), ((), ())), preferred_element_type=F32)


def silu(v):
    return v / (1.0 + jnp.exp(-v))


def softplus(v):
    return jnp.maximum(v, 0.0) + jnp.log1p(jnp.exp(-jnp.abs(v)))


def three(v):
    hi = v.astype(BF)
    rest = v - hi.astype(F32)
    mid = rest.astype(BF)
    return hi, mid, (rest - mid.astype(F32)).astype(BF)


def expand(v, hot):
    hi = v.astype(BF)
    lo = (v - hi.astype(F32)).astype(BF)
    return dot(hi, hot) + dot(lo, hot)


def head_hot():
    row = lax.broadcasted_iota(jnp.int32, (128, CH), 0)
    col = lax.broadcasted_iota(jnp.int32, (128, CH), 1)
    return (row == col // HEAD).astype(F32).astype(BF)


def wide(m):
    return jnp.concatenate([m, m, m], axis=1)


class Copies:
    def __init__(self, send, recv):
        self.send, self.recv, self.open = send, recv, []

    def go(self, src, dst, slot, device):
        copy = pltpu.make_async_remote_copy(
            src_ref=src,
            dst_ref=dst,
            send_sem=self.send.at[slot],
            recv_sem=self.recv.at[slot],
            device_id=device,
            device_id_type=pl.DeviceIdType.MESH,
        )
        copy.start()
        self.open.append(copy)

    def arrived(self, dst, slot):
        pltpu.make_async_remote_copy(
            src_ref=dst,
            dst_ref=dst,
            send_sem=self.send.at[slot],
            recv_sem=self.recv.at[slot],
            device_id=self.me,
            device_id_type=pl.DeviceIdType.MESH,
        ).wait_recv()

    def close(self):
        for copy in self.open:
            copy.wait_send()


def coords():
    return (
        lax.axis_index("z"),
        lax.axis_index("x"),
        lax.axis_index("y"),
        lax.axis_index("tp"),
    )


def greet(devices):
    barrier = pltpu.get_barrier_semaphore()
    for device in devices:
        pl.semaphore_signal(
            barrier, inc=1, device_id=device, device_id_type=pl.DeviceIdType.MESH
        )
    pl.semaphore_wait(barrier, len(devices))


class Plane:
    def __init__(self, out, copies, rows, relay):
        self.out, self.copies, self.half, self.relay = out, copies, rows // 2, relay
        z, x, y, c = coords()
        self.y, self.c = y, c
        self.a = x * (1 - c) + z * c
        self.b = z * (1 - c) + x * c

    def at(self, da, db):
        a = (self.a + da + 8) % 4
        b = (self.b + db + 8) % 4
        c = self.c
        return b * (1 - c) + a * c, a * (1 - c) + b * c

    def device(self, da, db):
        z, x = self.at(da, db)
        return (z, x, self.y, self.c)

    def full(self, d, db=0):
        z, x = self.at(-d, db)
        return self.out.at[z * 4 + x]

    def low(self, d, db):
        z, x = self.at(-d, db)
        return self.out.at[z * 4 + x, pl.ds(0, self.half)]

    def high(self, d, db):
        z, x = self.at(-d, db)
        return self.out.at[z * 4 + x, pl.ds(self.half, self.half)]

    def first(self, own):
        for d in (1, 3, 2):
            self.copies.go(own, self.full(0), d - 1, self.device(d, 0))
        self.second(0, own)

    def second(self, d, src=None):
        src = self.full(d) if src is None else src
        self.copies.go(src, self.full(d), 3 + 4 * d, self.device(0, 1))
        self.copies.go(src, self.full(d), 4 + 4 * d, self.device(0, -1))
        if d not in self.relay:
            self.copies.go(src, self.full(d), 5 + 4 * d, self.device(0, 2))

    def turn(self, d):
        self.copies.arrived(self.full(d), d - 1)
        self.second(d)

    def pass_on(self, d):
        self.copies.arrived(self.full(d, -1), 3 + 4 * d)
        if d in self.relay:
            self.copies.go(self.low(d, -1), self.low(d, -1), 5 + 4 * d, self.device(0, 1))
        self.copies.arrived(self.full(d, 1), 4 + 4 * d)
        if d in self.relay:
            self.copies.go(self.high(d, 1), self.high(d, 1), 6 + 4 * d, self.device(0, -1))

    def end(self, d):
        if d in self.relay:
            self.copies.arrived(self.low(d, 2), 5 + 4 * d)
            self.copies.arrived(self.high(d, 2), 6 + 4 * d)
        else:
            self.copies.arrived(self.full(d, 2), 5 + 4 * d)


def pack(width):
    row = lax.broadcasted_iota(jnp.int32, (96, 128), 0)
    col = lax.broadcasted_iota(jnp.int32, (96, 128), 1)
    padded = 128 // (96 // width)
    return (col == row // width * padded + row % width).astype(F32).astype(BF)


UNIT = 1024
COPY = {
    "stage": 7, "ostage": 3, "hid": 6, "cross": 4, "w": 19, "edge": 1, "wo": 19, "bc": 1,
    "part": 15, "rate": 15, "back": 15, "page": 3, "decay": 3,
    "mate": 4, "ring": 4, "sum": 7, "state": 3,
}


def buffers(d):
    vmem = pltpu.VMEM
    return {
        "hidden": vmem((128, d), BF),
        "gate_w": vmem((12, DI), F32),
        "inner_w": vmem((12, DI), F32),
        "small_w": vmem((12, 304), F32),
        "cinner": vmem((4, CH), F32),
        "cshared": vmem((4, 2 * N), F32),
        "binner": vmem((1, CH), F32),
        "ngain": vmem((1, CH), F32),
        "params": vmem((1, 512), F32),
        "out_w": vmem((24, d), F32),
        "lens": pltpu.SMEM((8,), jnp.int32),
        "grps": pltpu.SMEM((8,), jnp.int32),
        "pt": pltpu.SMEM((2,), jnp.int32),
        "outp": vmem((4, 32, CH), BF),
        "pieces": vmem((8, 16, UNIT), BF),
        "stage": vmem((8, 16, UNIT), BF),
        "ostage": vmem((4, 32, CH), BF),
        "unit": vmem((96, UNIT), BF),
        "ounit": vmem((96, CH), BF),
        "half": vmem((128, d), BF),
        "w": vmem((16, 96, UNIT), BF),
        "wo": vmem((16, 96, CH), BF),
        "hid": vmem((8, 128, d), BF),
        "edge": vmem((16, d), BF),
        "initf": vmem((4, CH, N), F32),
        "initb": vmem((CH, 4 * N), BF),
        "sg": vmem((1024, CH), F32),
        "xs": vmem((1032, CH + 2 * N), F32),
        "bc": vmem((2, 1040, N), BF),
        "steps": vmem((1024, 128), BF),
        "y": vmem((1024, CH), F32),
        "xdt": vmem((1024, CH), BF),
        "b": vmem((1024, N), BF),
        "c": vmem((1024, N), BF),
        "cum": vmem((1024, 128), F32),
        "fx": vmem((1024, CH), F32),
        "state": vmem((3, 16, 8, N), F32),
        "small": vmem((9, CH, N), BF),
        "dps": vmem((8, 8, N), F32),
        "parts": vmem((16, 3, 8, N), F32),
        "decs": vmem((16, 8, N), F32),
        "befores": vmem((16, 3, 8, N), F32),
        "carry": vmem((3, 16, 8, N), F32),
        "carries": vmem((4, CH, N), BF),
        "pages": vmem((4, 2, CH, N), BF),
        "rates": vmem((4, 2, 8, N), F32),
        "opp": vmem((128, d), BF),
        "ahead": vmem((128, d), BF),
        "behind": vmem((128, d), BF),
        "own": vmem((128, d), BF),
        "xs_out": vmem((4, 128, d), BF),
        "xs_in": vmem((4, 128, d), BF),
        "low": vmem((64, d), BF),
        "high": vmem((64, d), BF),
        "from_l": vmem((128, d), BF),
        "from_r": vmem((128, d), BF),
        "sq": vmem((8, 8, 128), F32),
        "sqr": vmem((8, 8, 128), F32),
        "snaps": vmem((2, 4, CH, N), F32),
        "res": vmem((128, d), BF),
    }


def layer_kernel(
    hidden_h, gate_h, inner_h, small_h, cinner_h, cshared_h, binner_h, ngain_h, params_h, out_h,
    lens_h, grps_h, pt_h, init, out_o, page_o, *refs,
):
    d = hidden_h.shape[1]
    names = list(buffers(d))
    r = dict(zip(names, refs))
    sems = refs[len(names):]
    z, x, y, c = coords()
    me_not = (z, x, y, 1 - c)
    cp = {}
    for i, name in enumerate(COPY):
        cp[name] = Copies(sems[2 * i], sems[2 * i + 1])
        cp[name].me = me_not
    local = sems[2 * len(COPY)]
    q = y * 2 + c
    g = z * 4 + x
    mate = me_not
    right, left = (z, x, (y + 1) % 4, c), (z, x, (y + 3) % 4, c)
    near = [(z, x, (y + k) % 4, c) for k in range(1, 4)]
    group = [(z, x, ((q + k) % 8) // 2, (q + k) % 2) for k in range(1, 8)]
    peers = [(((g + k) % 16) // 4, ((g + k) % 16) % 4, y, c) for k in range(1, 16)]
    next_dev = peers[0]
    barrier = pltpu.get_barrier_semaphore()
    for device in group + peers:
        pl.semaphore_signal(
            barrier, inc=1, device_id=device, device_id_type=pl.DeviceIdType.MESH
        )

    mychan = pl.ds(pl.multiple_of(y * CH, CH), CH)
    loads = {
        "gate_w": gate_h,
        "inner_w": inner_h,
        "small_w": small_h,
        "hidden": hidden_h.at[pl.ds(pl.multiple_of(c * 128, 128), 128)],
        "out_w": out_h,
        "params": params_h,
        "binner": binner_h.at[mychan],
        "ngain": ngain_h.at[mychan],
        "cinner": cinner_h.at[:, mychan],
        "cshared": cshared_h,
        "lens": lens_h,
        "grps": grps_h,
        "pt": pt_h,
        "initf": init.at[:, mychan],
    }
    for i, name in enumerate(loads):
        to = r[name].at[0] if name in ("params", "binner", "ngain") else r[name]
        loads[name] = pltpu.make_async_copy(loads[name], to, local.at[2 + i])
        loads[name].start()
    gate_w, inner_w, small_w, hidden = r["gate_w"], r["inner_w"], r["small_w"], r["hidden"]
    params, cinner, cshared = r["params"], r["cinner"], r["cshared"]
    lens, grps, pt, outp = r["lens"], r["grps"], r["pt"], r["outp"]
    pieces, stage = r["pieces"], r["stage"]
    outp[...] = jnp.zeros_like(outp)
    pieces[...] = jnp.zeros_like(pieces)
    for name in ("gate_w", "inner_w", "small_w", "out_w"):
        loads[name].wait()
    for t in range(4):
        outp[t, 0:24, :] = r["out_w"][:, t * CH : t * CH + CH].astype(BF)
    for t in range(8):
        a = 1536 * (t % 2) + CH * (t // 2)
        pieces[t, 0:12, 0:CH] = gate_w[:, a : a + CH].astype(BF)
        pieces[t, 0:12, CH : 2 * CH] = inner_w[:, a : a + CH].astype(BF)
        b = N * (t % 2)
        pieces[t, 0:12, 2 * CH : 2 * CH + N] = small_w[:, b : b + N].astype(BF)
        pieces[t, 0:12, 2 * CH + N : 2 * CH + N + 48] = small_w[:, 2 * N :].astype(BF)
    pl.semaphore_wait(barrier, len(group) + len(peers))

    for k in range(1, 8):
        cp["stage"].go(pieces.at[(q + k) % 8], stage.at[q], k - 1, group[k - 1])
    for k in range(1, 4):
        cp["ostage"].go(outp.at[(y + k) % 4], r["ostage"].at[y], k - 1, near[k - 1])
    stage[q] = pieces[q]
    r["ostage"][y] = outp[y]

    half = r["half"]
    loads["params"].wait()
    loads["hidden"].wait()
    lay = jnp.broadcast_to(params[:, 128:256], (8, 128)).astype(BF)
    rows = hidden[...]
    for j in range(0, d, CH):
        brow = lax.broadcasted_iota(jnp.int32, (128, CH), 0)
        bcol = lax.broadcasted_iota(jnp.int32, (128, CH), 1) + j
        block = dot(lay, (brow == bcol // 12).astype(F32).astype(BF))[0:1]
        want = block * 12.0 + (bcol[0:1] % 12).astype(F32)
        frow = lax.broadcasted_iota(jnp.int32, (d, CH), 0).astype(F32)
        pick = jnp.where(frow == want, 1.0, 0.0).astype(BF)
        half[:, j : j + CH] = dot(rows, pick).astype(BF)

    hid = r["hid"]

    def hslot(dy, core):
        return ((y + dy + 4) % 4) * 2 + core

    def hpart(dy, low):
        return hid.at[hslot(dy, c), pl.ds(0 if low else 64, 64)]

    lo, hi = pl.ds(0, 64), pl.ds(64, 64)
    cp["hid"].go(half.at[lo], hpart(0, True), 0, right)
    cp["hid"].go(half.at[hi], hpart(0, False), 2, left)
    cp["hid"].go(half.at[hi], hpart(0, False), 1, right)
    cp["hid"].go(half.at[lo], hpart(0, True), 3, left)
    cp["cross"].go(half, hid.at[hslot(0, c)], 0, mate)
    hid[q] = half[...]

    for k in range(1, 8):
        cp["stage"].arrived(stage.at[(q + 8 - k) % 8], k - 1)
    packer = pack(12)
    for j in range(0, UNIT, 512):
        r["unit"][:, j : j + 512] = dot(
            packer, stage[:, :, j : j + 512].reshape(128, 512)
        ).astype(BF)
    ring = Plane(r["w"], cp["w"], 96, (0, 1, 3))
    ring.first(r["unit"])
    mine = pltpu.make_async_copy(r["unit"], r["w"].at[g], local.at[1])
    mine.start()
    for k in range(1, 4):
        cp["ostage"].arrived(r["ostage"].at[(y + 4 - k) % 4], k - 1)
    r["ounit"][...] = dot(pack(24), r["ostage"][...].reshape(128, CH)).astype(BF)
    for name in ("initf", "cinner", "cshared", "binner", "ngain", "lens", "grps", "pt"):
        loads[name].wait()
    for k in range(4):
        r["initb"][:, k * N : k * N + N] = r["initf"][k].astype(BF)

    cp["hid"].arrived(hpart(-1, True), 0)
    cp["hid"].go(hpart(-1, True), hpart(-1, True), 4, right)
    cp["hid"].arrived(hpart(1, False), 2)
    cp["hid"].go(hpart(1, False), hpart(1, False), 5, left)
    ring.turn(1)
    ring.turn(3)
    ring.turn(2)
    ring.pass_on(0)
    cp["hid"].arrived(hpart(-1, False), 1)
    cp["cross"].go(hid.at[hslot(-1, c)], hid.at[hslot(-1, c)], 1, mate)
    cp["hid"].arrived(hpart(1, True), 3)
    cp["cross"].go(hid.at[hslot(1, c)], hid.at[hslot(1, c)], 2, mate)
    ring.pass_on(1)
    ring.pass_on(3)
    oring = Plane(r["wo"], cp["wo"], 96, ())
    cp["hid"].arrived(hpart(2, True), 4)
    cp["hid"].arrived(hpart(2, False), 5)
    cp["cross"].go(hid.at[hslot(2, c)], hid.at[hslot(2, c)], 3, mate)
    for k, dy in enumerate((0, -1, 1, 2)):
        cp["cross"].arrived(hid.at[hslot(dy, 1 - c)], k)
    cp["edge"].go(hid.at[7, pl.ds(112, 16)], r["edge"], 0, next_dev)
    ring.pass_on(2)
    for k in range(4):
        ring.end(k)
    mine.wait()
    oring.first(r["ounit"])
    mine = pltpu.make_async_copy(r["ounit"], r["wo"].at[g], local.at[1])
    mine.start()

    w, xs, bc, steps, sg = r["w"], r["xs"], r["bc"], r["steps"], r["sg"]

    def columns(a, z):
        return w[:, :, a:z].reshape(d, z - a)

    cp["edge"].arrived(r["edge"], 0)
    bc[c, 0:16, :] = dot(r["edge"][...], columns(2 * CH, 2 * CH + N)).astype(BF)

    def project_bc(i, _):
        at = pl.multiple_of(i * 256, 256)
        got = dot(hid[pl.ds(i * 2, 2)].reshape(256, d), columns(2 * CH, UNIT)).astype(BF)
        bc[c, pl.ds(pl.multiple_of(at + 16, 16), 256), :] = got[:, :N]
        steps[pl.ds(at, 256), :] = got[:, N:]
        return 0

    lax.fori_loop(0, 4, project_bc, 0)
    cp["bc"].go(bc.at[c], bc.at[c], 0, mate)
    xs[0:8, 0:CH] = dot(r["edge"][...], columns(CH, 2 * CH))[8:16].astype(BF).astype(F32)

    def project(i, _):
        at = pl.multiple_of(i * 256, 256)
        got = dot(hid[pl.ds(i * 2, 2)].reshape(256, d), columns(0, 2 * CH)).astype(BF)
        sg[pl.ds(at, 256), :] = got[:, :CH].astype(F32)
        xs[pl.ds(pl.multiple_of(at + 8, 8), 256), 0:CH] = got[:, CH:].astype(F32)
        return 0

    lax.fori_loop(0, 4, project, 0)
    for k in (1, 3, 2):
        oring.turn(k)
    cp["bc"].arrived(bc.at[1 - c], 0)
    for k in range(2):
        xs[0:8, CH + k * N : CH + k * N + N] = bc[k, 0:16, :].astype(F32)[8:16]
        xs[8:1032, CH + k * N : CH + k * N + N] = bc[k, 16:1040, :].astype(F32)

    hot = head_hot()
    starts = []
    total = jnp.int32(0)
    for k in range(8):
        starts.append(total)
        total = total + lens[k]
    row = lax.broadcasted_iota(jnp.int32, (128, 128), 0)
    col = lax.broadcasted_iota(jnp.int32, (128, 128), 1)
    head0 = c * 24 + y * MINE
    pick = jnp.where(col < MINE, (row == col + head0).astype(F32), 0.0).astype(BF)
    wrow = lax.broadcasted_iota(jnp.int32, (128, CH), 0)
    wcol = lax.broadcasted_iota(jnp.int32, (128, CH), 1)
    pickx = (wrow == wcol // HEAD + head0).astype(F32).astype(BF)
    hsplit = three(jnp.broadcast_to(params[:, 0:128], (8, 128)))

    def take(kind):
        at = jnp.where(col < MINE, (row == col + y * MINE + 24 * kind).astype(F32), 0.0).astype(BF)
        return sum(dot(part, at) for part in hsplit)[0:1]

    def takex(kind):
        at = (wrow == wcol // HEAD + y * MINE + 24 * kind).astype(F32).astype(BF)
        return sum(dot(part, at) for part in hsplit)[0:1]

    rate6 = jnp.where(col[0:1] < MINE, -jnp.exp(take(1)), 0.0)
    bias6, biasx, skipx = take(0), takex(0), takex(2)
    taps = cinner[...]
    biasc = r["binner"][...]
    state, small, dps = r["state"], r["small"], r["dps"]
    small[0] = jnp.zeros((CH, N), BF)

    def find(pos):
        first = jnp.zeros(pos.shape, jnp.int32)
        for k in range(1, 8):
            first = jnp.where(pos >= starts[k], starts[k], first)
        return first

    def advance(i, held):
        old, dp, dprow = held
        at = pl.multiple_of(i * 256, 256)
        base = g * 1024 + i * 256
        first = find(base + lax.broadcasted_iota(jnp.int32, (256, 128), 0))
        off = base + lax.broadcasted_iota(jnp.int32, (256, 128), 0) - first
        xc = biasc + jnp.zeros((256, CH), F32)
        bcc = params[:, 256:512] + jnp.zeros((256, 2 * N), F32)
        window = xs[pl.ds(at, 264), :]
        for lag in range(CONV):
            ok = (off >= lag).astype(F32)
            part = window[8 - lag : 264 - lag, :]
            xc = xc + taps[lag : lag + 1, :] * part[:, :CH] * wide(ok)
            bcc = bcc + cshared[lag : lag + 1, :] * part[:, CH:] * jnp.concatenate([ok, ok], axis=1)
        xc = silu(xc)
        bcc = silu(bcc)
        b_all = bcc[:, :N].astype(BF)
        r["b"][pl.ds(at, 256), :] = b_all
        r["c"][pl.ds(at, 256), :] = bcc[:, N:].astype(BF)
        step = steps[pl.ds(at, 256), :]
        dt6 = softplus(dot(step, pick) + bias6)
        log6 = rate6 * dt6
        dtx = softplus(dot(step, pickx) + biasx)
        xdt_all = xc * dtx
        r["xdt"][pl.ds(at, 256), :] = xdt_all.astype(BF)
        r["y"][pl.ds(at, 256), :] = skipx * xc
        for sub in range(2):
            k = i * 2 + sub
            p0 = base + sub * 128
            rows = slice(sub * 128, sub * 128 + 128)
            f0 = first[rows, :]
            mask = (row >= col) & (f0 == find(p0 + col))
            maskb = mask.astype(F32).astype(BF)
            cum = sum(dot(maskb, part) for part in three(log6[rows, :]))
            there = pl.ds(pl.multiple_of(at + sub * 128, 128), 128)
            r["cum"][there, :] = cum
            cumt = cum.T
            flast = jnp.int32(0)
            glast = grps[0]
            for j in range(1, 8):
                got = p0 + 127 >= starts[j]
                flast = jnp.where(got, starts[j], flast)
                glast = jnp.where(got, grps[j], glast)
            w6 = jnp.exp(jnp.where(f0 == flast, cum[127:128, :] - cum, NEG))
            xw = (xdt_all[rows, :] * expand(w6, hot)).astype(BF)
            summary = dot_tn(xw, b_all[rows, :])
            keep = (flast < p0).astype(F32)
            ecum = jnp.exp(cum)
            r["fx"][there, :] = expand(
                jnp.where(f0 < p0, ecum, 0.0) * dprow, hot
            )
            scale = jnp.exp(jnp.broadcast_to(cumt[0:8, 127:128], (8, 128)))
            dp = dp * scale * keep
            dprow = dprow * jnp.exp(cum[127:128, :]) * keep
            dps[k] = dp
            start = r["initf"][0]
            for j in range(1, 4):
                start = jnp.where(glast == j, r["initf"][j], start)
            old = jnp.where(flast < p0, old, start)
            old = jnp.concatenate(
                [scale[h : h + 1, :] * old[h * HEAD : h * HEAD + HEAD, :] for h in range(MINE)], axis=0
            ) + summary
            small[k + 1] = old.astype(BF)
        return old, dp, dprow

    last, dplast, _ = lax.fori_loop(
        0, 4, advance, (jnp.zeros((CH, N), F32), jnp.ones((8, 128), F32), jnp.ones((1, 128), F32))
    )
    state[...] = last.reshape(3, 16, 8, N)

    parts, decs, befores, carry = r["parts"], r["decs"], r["befores"], r["carry"]
    for k in range(1, 16):
        cp["part"].go(state.at[:, (g + k) % 16], parts.at[g], k - 1, peers[k - 1])
        cp["rate"].go(dps.at[7], decs.at[g], k - 1, peers[k - 1])
    parts[g] = state[:, g]
    decs[g] = dps[7]
    for k in range(1, 4):
        t = (y + k) % 4
        cp["page"].go(small.at[pl.ds(t * 2 + 1, 2)], r["pages"].at[y], k - 1, near[k - 1])
        cp["decay"].go(dps.at[pl.ds(t * 2, 2)], r["rates"].at[y], k - 1, near[k - 1])
    for k in range(2):
        r["pages"][y, k] = small[y * 2 + 1 + k]
        r["rates"][y, k] = dps[y * 2 + k]

    def inside(i, _):
        for sub in range(2):
            k = i * 2 + sub
            p0 = g * 1024 + k * 128
            at = pl.ds(pl.multiple_of(k * 128, 128), 128)
            f0 = find(p0 + row)
            mask = (row >= col) & (f0 == find(p0 + col))
            cum = r["cum"][at, :]
            cumt = cum.T
            cb = r["c"][at, :]
            cf = cb.astype(F32)
            scores = dot_nt(cb, r["b"][at, :])
            gid = jnp.zeros((128, 128), jnp.int32) + grps[0]
            for j in range(1, 8):
                gid = jnp.where(p0 + row >= starts[j], grps[j], gid)
            gid = jnp.where(f0 < p0, 4, gid)
            chot = jnp.concatenate(
                [jnp.where(gid == j, cf, 0.0).astype(BF) for j in range(4)], axis=1
            )
            read = dot_nt(jnp.where(gid == 4, cf, 0.0).astype(BF), small[k])
            read = read + dot_nt(chot, r["initb"][...])
            lane = col
            pieces = []
            for pair in range(3):
                xp = r["xdt"][at, pair * 128 : pair * 128 + 128]
                got = []
                for h in (2 * pair, 2 * pair + 1):
                    diff = cum[:, h : h + 1] - cumt[h : h + 1, :]
                    mix = jnp.exp(jnp.where(mask, diff, NEG)) * scores
                    got.append(dot(mix.astype(BF), xp))
                pieces.append(jnp.where(lane < HEAD, got[0], got[1]))
            r["y"][at, :] = (
                r["y"][at, :] + expand(jnp.exp(cum), hot) * read + jnp.concatenate(pieces, axis=1)
            )
            sg[at, :] = silu(sg[at, :])
        return 0

    lax.fori_loop(0, 2, inside, 0)
    for k in range(1, 16):
        cp["part"].arrived(parts.at[(g + 16 - k) % 16], k - 1)
        cp["rate"].arrived(decs.at[(g + 16 - k) % 16], k - 1)
    hb = g // 8
    run = [jnp.zeros((8, 128), F32) for _ in range(3)]
    for k in range(16):
        for j in range(3):
            befores[k, j] = run[j]
            run[j] = decs[k, pl.ds(hb + 2 * j, 1), :] * run[j] + parts[k, j]
    for k in range(1, 16):
        cp["back"].go(befores.at[(g + k) % 16], carry.at[:, g], k - 1, peers[k - 1])
    carry[:, g] = befores[g]
    for k in range(4):
        oring.pass_on(k)
        oring.end(k)
    mine.wait()
    lax.fori_loop(2, 4, inside, 0)
    for k in range(1, 16):
        cp["back"].arrived(carry.at[:, (g + 16 - k) % 16], k - 1)

    carries = r["carries"]
    cs = carry[...].reshape(CH, N).astype(BF)
    carries[y] = cs
    for k in range(1, 4):
        cp["state"].go(carries.at[y], carries.at[y], k - 1, near[k - 1])
    ones = jnp.ones((8, CH), BF)
    gain = r["ngain"][...]
    xs_out, xs_in, sq, sqr = r["xs_out"], r["xs_in"], r["sq"], r["sqr"]

    def partial(dy, k, keep):
        t = (y + dy) % 4
        for part in range(2):
            core = c if part else 1 - c
            at = pl.ds(pl.multiple_of(t * 256 + core * 128, 128), 128)
            full = r["y"][at, :] + r["fx"][at, :] * dot_nt(r["c"][at, :], cs)
            gv = full * sg[at, :]
            g2 = gv * gv
            top = g2.astype(BF)
            rest = (g2 - top.astype(F32)).astype(BF)
            sq[t * 2 + core] = dot_nt(ones, top) + dot_nt(ones, rest)
            gg = (gv * gain).astype(BF)
            for n in range(0, 1536, CH):
                got = dot_nt(gg, r["wo"][n // 96 : n // 96 + 4].reshape(CH, CH)).astype(BF)
                if part:
                    keep[:, n : n + CH] = got
                else:
                    xs_out[k, :, n : n + CH] = got
            if not part:
                cp["mate"].go(xs_out.at[k], xs_in.at[k], k, mate)

    def join(k, keep):
        cp["mate"].arrived(xs_in.at[k], k)
        keep[...] = (keep[...].astype(F32) + xs_in[k].astype(F32)).astype(BF)

    opp, ahead, behind, own = r["opp"], r["ahead"], r["behind"], r["own"]
    partial(2, 0, opp)
    partial(1, 1, ahead)
    join(0, opp)
    cp["ring"].go(opp.at[lo], r["low"], 0, right)
    cp["ring"].go(opp.at[hi], r["high"], 1, left)
    partial(3, 2, behind)
    join(1, ahead)
    cp["ring"].arrived(r["low"], 0)
    ahead[0:64, :] = (ahead[0:64, :].astype(F32) + r["low"][...].astype(F32)).astype(BF)
    cp["ring"].go(ahead, r["from_l"], 2, right)
    join(2, behind)
    cp["ring"].arrived(r["high"], 1)
    behind[64:128, :] = (behind[64:128, :].astype(F32) + r["high"][...].astype(F32)).astype(BF)
    cp["ring"].go(behind, r["from_r"], 3, left)
    partial(0, 3, own)
    for k in range(1, 8):
        cp["sum"].go(sq.at[(q + k) % 8], sqr.at[q], k - 1, group[k - 1])
    sqr[q] = sq[q]
    join(3, own)

    swap = pt[0] != (g * 4 + y) * 2
    for k in range(4):
        t = (y + 4 - k) % 4
        if k:
            cp["state"].arrived(carries.at[t], k - 1)
            cp["page"].arrived(r["pages"].at[t], k - 1)
            cp["decay"].arrived(r["rates"].at[t], k - 1)
        for h in range(MINE):
            at = slice(h * HEAD, h * HEAD + HEAD)
            came = carries[t, at, :].astype(F32)
            one, two = (
                r["pages"][t, j, at, :].astype(F32) + r["rates"][t, j, h : h + 1, :] * came
                for j in range(2)
            )
            r["snaps"][0, t, at, :] = jnp.where(swap, two, one)
            r["snaps"][1, t, at, :] = jnp.where(swap, one, two)
    snaps = pltpu.make_async_copy(r["snaps"], page_o, local.at[0])
    snaps.start()

    for k in range(1, 8):
        cp["sum"].arrived(sqr.at[(q + 8 - k) % 8], k - 1)
    total = sqr[0]
    for k in range(1, 8):
        total = total + sqr[k]
    scale = lax.rsqrt(total / DI + EPS)
    scale = jnp.broadcast_to(scale[0:1, :], (128, 128)).T
    cp["ring"].arrived(r["from_l"], 2)
    cp["ring"].arrived(r["from_r"], 3)
    for n in range(0, 1536, 128):
        cols = slice(n, n + 128)
        whole = sum(v[:, cols].astype(F32) for v in (own, r["from_l"], r["from_r"]))
        r["res"][:, cols] = (whole * scale).astype(BF)
    res = pltpu.make_async_copy(r["res"], out_o, local.at[16])
    res.start()
    res.wait()
    snaps.wait()
    for name in COPY:
        cp[name].close()


def on_device(
    hidden_in, gate_proj, inner_proj, small_proj, row_layout, conv_inner, conv_shared,
    bias_inner, bias_shared, dt_bias, decay_log, skip_gain, norm_gain, out_proj,
    prompt_lengths, group_map, init_states, page_table,
):
    d = hidden_in.shape[1]
    params = jnp.concatenate(
        [dt_bias, decay_log, skip_gain, jnp.zeros((56,), F32), row_layout.astype(F32), bias_shared]
    )
    hbm = pl.BlockSpec(memory_space=pltpu.HBM)
    dma = pltpu.SemaphoreType.DMA
    scratch = list(buffers(d).values())
    for count in COPY.values():
        scratch += [dma((count,)), dma((count,))]
    mixed, pages = pl.pallas_call(
        layer_kernel,
        in_specs=[hbm] * 14,
        out_specs=[hbm, hbm],
        out_shape=[
            jax.ShapeDtypeStruct((128, d), BF),
            jax.ShapeDtypeStruct((2, 4, CH, N), F32),
        ],
        scratch_shapes=scratch + [dma((18,))],
        compiler_params=pltpu.CompilerParams(
            collective_id=0, has_side_effects=True, vmem_limit_bytes=60 << 20
        ),
        name="layer",
    )(
        hidden_in, gate_proj, inner_proj, small_proj, conv_inner, conv_shared, bias_inner, norm_gain, params,
        out_proj.T, prompt_lengths, group_map, page_table, init_states.reshape(4, 24 * HEAD, N),
    )
    return (mixed, pages.reshape(2, 24, HEAD, N))


def solution(mesh):
    fine = Mesh(mesh.devices.reshape(4, 4, 4, 2), ("z", "x", "y", "tp"))
    seq = ("z", "x", "y")
    every = ("z", "x", "y", "tp")
    placed = (
        P(seq, None),
        P(every, None),
        P(every, None),
        P(every, None),
        P(),
        P(None, "tp"),
        P(),
        P("tp"),
        P(),
        P("tp"),
        P("tp"),
        P("tp"),
        P("tp"),
        P("tp", seq),
        P(),
        P(),
        P(None, "tp", None, None),
        P(seq),
    )
    return jax.shard_map(
        on_device,
        mesh=fine,
        in_specs=placed,
        out_specs=(P(every, None), P(seq, "tp", None, None)),
        check_vma=False,
    )
```

```python
from types import SimpleNamespace

import jax
import jax.numpy as jnp
from jax import lax
from jax.experimental import pallas as pl
from jax.experimental.pallas import tpu as pltpu
from jax.sharding import Mesh
from jax.sharding import PartitionSpec as P

N = 128
CONV = 4
PAGE = 128
DI = 3072
HEAD = 64
MINE = 6
CH = MINE * HEAD
EPS = 1e-05
BF = jnp.bfloat16
F32 = jnp.float32
NEG = -1e30


def dot(a, b):
    return jnp.dot(a, b, preferred_element_type=F32)


def dot_nt(a, b):
    return lax.dot_general(a, b, (((1,), (1,)), ((), ())), preferred_element_type=F32)


def dot_tn(a, b):
    return lax.dot_general(a, b, (((0,), (0,)), ((), ())), preferred_element_type=F32)


def silu(v):
    return v / (1.0 + jnp.exp(-v))


def softplus(v):
    return jnp.maximum(v, 0.0) + jnp.log1p(jnp.exp(-jnp.abs(v)))


def three(v):
    hi = v.astype(BF)
    rest = v - hi.astype(F32)
    mid = rest.astype(BF)
    return hi, mid, (rest - mid.astype(F32)).astype(BF)


def expand(v, hot):
    hi = v.astype(BF)
    lo = (v - hi.astype(F32)).astype(BF)
    return dot(hi, hot) + dot(lo, hot)


def head_hot():
    row = lax.broadcasted_iota(jnp.int32, (128, CH), 0)
    col = lax.broadcasted_iota(jnp.int32, (128, CH), 1)
    return (row == col // HEAD).astype(F32).astype(BF)


def wide(m):
    return jnp.concatenate([m, m, m], axis=1)


class Copies:
    def __init__(self, send, recv):
        self.send, self.recv, self.open = send, recv, []

    def go(self, src, dst, slot, device):
        copy = pltpu.make_async_remote_copy(
            src_ref=src,
            dst_ref=dst,
            send_sem=self.send.at[slot],
            recv_sem=self.recv.at[slot],
            device_id=device,
            device_id_type=pl.DeviceIdType.MESH,
        )
        copy.start()
        self.open.append(copy)

    def arrived(self, dst, slot):
        pltpu.make_async_remote_copy(
            src_ref=dst,
            dst_ref=dst,
            send_sem=self.send.at[slot],
            recv_sem=self.recv.at[slot],
            device_id=self.me,
            device_id_type=pl.DeviceIdType.MESH,
        ).wait_recv()

    def close(self):
        for copy in self.open:
            copy.wait_send()


def coords():
    return (
        lax.axis_index("z"),
        lax.axis_index("x"),
        lax.axis_index("y"),
        lax.axis_index("tp"),
    )


class Plane:
    def __init__(self, out, copies, rows, relay):
        self.out, self.copies, self.half, self.relay = out, copies, rows // 2, relay
        z, x, y, c = coords()
        self.y, self.c = y, c
        self.a = x * (1 - c) + z * c
        self.b = z * (1 - c) + x * c

    def at(self, da, db):
        a = (self.a + da + 8) % 4
        b = (self.b + db + 8) % 4
        c = self.c
        return b * (1 - c) + a * c, a * (1 - c) + b * c

    def device(self, da, db):
        z, x = self.at(da, db)
        return (z, x, self.y, self.c)

    def full(self, d, db=0):
        z, x = self.at(-d, db)
        return self.out.at[z * 4 + x]

    def low(self, d, db):
        z, x = self.at(-d, db)
        return self.out.at[z * 4 + x, pl.ds(0, self.half)]

    def high(self, d, db):
        z, x = self.at(-d, db)
        return self.out.at[z * 4 + x, pl.ds(self.half, self.half)]

    def first(self, own):
        for d in (1, 3, 2):
            self.copies.go(own, self.full(0), d - 1, self.device(d, 0))
        self.second(0, own)

    def second(self, d, src=None):
        src = self.full(d) if src is None else src
        self.copies.go(src, self.full(d), 3 + 4 * d, self.device(0, 1))
        self.copies.go(src, self.full(d), 4 + 4 * d, self.device(0, -1))
        if d not in self.relay:
            self.copies.go(src, self.full(d), 5 + 4 * d, self.device(0, 2))

    def turn(self, d):
        self.copies.arrived(self.full(d), d - 1)
        self.second(d)

    def pass_on(self, d):
        self.copies.arrived(self.full(d, -1), 3 + 4 * d)
        if d in self.relay:
            self.copies.go(self.low(d, -1), self.low(d, -1), 5 + 4 * d, self.device(0, 1))
        self.copies.arrived(self.full(d, 1), 4 + 4 * d)
        if d in self.relay:
            self.copies.go(self.high(d, 1), self.high(d, 1), 6 + 4 * d, self.device(0, -1))

    def end(self, d):
        if d in self.relay:
            self.copies.arrived(self.low(d, 2), 5 + 4 * d)
            self.copies.arrived(self.high(d, 2), 6 + 4 * d)
        else:
            self.copies.arrived(self.full(d, 2), 5 + 4 * d)


def pack(width):
    row = lax.broadcasted_iota(jnp.int32, (96, 128), 0)
    col = lax.broadcasted_iota(jnp.int32, (96, 128), 1)
    padded = 128 // (96 // width)
    return (col == row // width * padded + row % width).astype(F32).astype(BF)


UNIT = 1024
COPY = dict(
    stage=7, ostage=3, hid=6, cross=4, w=19, edge=1, wo=19, bc=2,
    part=15, back=15, page=3, decay=3, gated=3, square=3, mate=2, state=3,
)


def buffers(d):
    vmem = pltpu.VMEM
    return dict(
        hidden=vmem((128, d), BF),
        gate_w=vmem((12, DI), F32),
        inner_w=vmem((12, DI), F32),
        small_w=vmem((12, 304), F32),
        cinner=vmem((4, CH), F32),
        cshared=vmem((4, 2 * N), F32),
        binner=vmem((1, CH), F32),
        ngain=vmem((1, CH), F32),
        params=vmem((1, 512), F32),
        out_w=vmem((24, d), F32),
        lens=pltpu.SMEM((8,), jnp.int32),
        grps=pltpu.SMEM((8,), jnp.int32),
        pt=pltpu.SMEM((2,), jnp.int32),
        pieces=vmem((8, 16, UNIT), BF),
        stage=vmem((8, 16, UNIT), BF),
        unit=vmem((96, UNIT), BF),
        half=vmem((128, d), BF),
        w=vmem((16, 96, UNIT), BF),
        hid=vmem((8, 128, d), BF),
        edge=vmem((16, d), BF),
        initf=vmem((4, CH, N), F32),
        initb=vmem((CH, 4 * N), BF),
        sg=vmem((1024, CH), F32),
        xs=vmem((1032, CH + 2 * N), F32),
        steps=vmem((1024, 128), BF),
        y=vmem((1024, CH), F32),
        xdt=vmem((1024, CH), BF),
        b=vmem((1024, N), BF),
        c=vmem((1024, N), BF),
        cum=vmem((1024, 128), F32),
        fx=vmem((1024, CH), F32),
        small=vmem((9, CH, N), BF),
        dps=vmem((8, 8, N), F32),
        carries=vmem((4, CH, N), BF),
        pages=vmem((4, 2, CH, N), BF),
        rates=vmem((4, 2, 8, N), F32),
        outp=vmem((32, d), BF),
        ostage=vmem((4, 32, d), BF),
        ounit=vmem((96, d), BF),
        wo=vmem((16, 96, d), BF),
        bc=vmem((2, 1040, N), BF),
        state=vmem((16, 4, 8, N), F32),
        parts=vmem((16, 4, 8, N), F32),
        befores=vmem((16, 3, 8, N), F32),
        carry=vmem((16, 3, 8, N), F32),
        gated=vmem((4, 256, CH), BF),
        came=vmem((4, 256, CH), BF),
        sq=vmem((4, 8, 256), F32),
        sqin=vmem((4, 8, 256), F32),
        acc=vmem((256, d), F32),
        pout=vmem((128, d), BF),
        pin=vmem((128, d), BF),
        sqown=vmem((8, 256), F32),
        sqmate=vmem((8, 256), F32),
        snaps=vmem((2, 4, CH, N), F32),
        res=vmem((128, d), BF),
    )


def layer_kernel(
    hidden_h, gate_h, inner_h, small_h, cinner_h, cshared_h, binner_h, ngain_h, params_h, out_h,
    lens_h, grps_h, pt_h, init, out_o, page_o, *refs,
):
    d = hidden_h.shape[1]
    names = list(buffers(d))
    r = SimpleNamespace(**dict(zip(names, refs)))
    sems = refs[len(names):]
    z, x, y, c = coords()
    me_not = (z, x, y, 1 - c)
    cp = SimpleNamespace()
    for i, name in enumerate(COPY):
        setattr(cp, name, Copies(sems[2 * i], sems[2 * i + 1]))
        getattr(cp, name).me = me_not
    local = sems[2 * len(COPY)]
    q = y * 2 + c
    g = z * 4 + x
    mate = me_not
    right, left = (z, x, (y + 1) % 4, c), (z, x, (y + 3) % 4, c)
    near = [(z, x, (y + k) % 4, c) for k in range(1, 4)]
    group = [(z, x, ((q + k) % 8) // 2, (q + k) % 2) for k in range(1, 8)]
    peers = [(((g + k) % 16) // 4, ((g + k) % 16) % 4, y, c) for k in range(1, 16)]
    next_dev = peers[0]
    barrier = pltpu.get_barrier_semaphore()
    for device in group + peers:
        pl.semaphore_signal(
            barrier, inc=1, device_id=device, device_id_type=pl.DeviceIdType.MESH
        )

    mychan = pl.ds(pl.multiple_of(y * CH, CH), CH)
    loads = dict(
        gate_w=gate_h,
        inner_w=inner_h,
        small_w=small_h,
        hidden=hidden_h.at[pl.ds(pl.multiple_of(c * 128, 128), 128)],
        out_w=out_h,
        params=params_h,
        binner=binner_h.at[mychan],
        ngain=ngain_h.at[mychan],
        cinner=cinner_h.at[:, mychan],
        cshared=cshared_h,
        lens=lens_h,
        grps=grps_h,
        pt=pt_h,
        initf=init.at[:, mychan],
    )
    load = SimpleNamespace()
    for i, name in enumerate(loads):
        to = getattr(r, name)
        if loads[name].ndim == 1 and to.shape[0] == 1:
            to = to.at[0]
        setattr(load, name, pltpu.make_async_copy(loads[name], to, local.at[2 + i]))
        getattr(load, name).start()
    gate_w, inner_w, small_w, hidden = r.gate_w, r.inner_w, r.small_w, r.hidden
    params, cinner, cshared = r.params, r.cinner, r.cshared
    lens, grps, pt, outp = r.lens, r.grps, r.pt, r.outp
    pieces, stage = r.pieces, r.stage
    outp[...] = jnp.zeros_like(outp)
    pieces[...] = jnp.zeros_like(pieces)
    for one in (load.gate_w, load.inner_w, load.small_w, load.out_w):
        one.wait()
    outp[0:24, :] = r.out_w[...].astype(BF)
    for t in range(8):
        a = 1536 * (t % 2) + CH * (t // 2)
        pieces[t, 0:12, 0:CH] = gate_w[:, a : a + CH].astype(BF)
        pieces[t, 0:12, CH : 2 * CH] = inner_w[:, a : a + CH].astype(BF)
        b = N * (t % 2)
        pieces[t, 0:12, 2 * CH : 2 * CH + N] = small_w[:, b : b + N].astype(BF)
        pieces[t, 0:12, 2 * CH + N : 2 * CH + N + 48] = small_w[:, 2 * N :].astype(BF)
    half = r.half
    load.params.wait()
    load.hidden.wait()
    lay = jnp.broadcast_to(params[:, 128:256], (8, 128)).astype(BF)
    rows = hidden[...]
    for j in range(0, d, CH):
        brow = lax.broadcasted_iota(jnp.int32, (128, CH), 0)
        bcol = lax.broadcasted_iota(jnp.int32, (128, CH), 1) + j
        block = dot(lay, (brow == bcol // 12).astype(F32).astype(BF))[0:1]
        want = block * 12.0 + (bcol[0:1] % 12).astype(F32)
        frow = lax.broadcasted_iota(jnp.int32, (d, CH), 0).astype(F32)
        pick = jnp.where(frow == want, 1.0, 0.0).astype(BF)
        half[:, j : j + CH] = dot(rows, pick).astype(BF)
    pl.semaphore_wait(barrier, len(group) + len(peers))

    for k in range(1, 8):
        cp.stage.go(pieces.at[(q + k) % 8], stage.at[q], k - 1, group[k - 1])
    stage[q] = pieces[q]
    r.ostage[y] = outp[...]

    hid = r.hid

    def hslot(dy, core):
        return ((y + dy + 4) % 4) * 2 + core

    def hpart(dy, low):
        return hid.at[hslot(dy, c), pl.ds(0 if low else 64, 64)]

    lo, hi = pl.ds(0, 64), pl.ds(64, 64)
    cp.hid.go(half.at[lo], hpart(0, True), 0, right)
    cp.hid.go(half.at[hi], hpart(0, False), 2, left)
    cp.hid.go(half.at[hi], hpart(0, False), 1, right)
    cp.hid.go(half.at[lo], hpart(0, True), 3, left)
    cp.cross.go(half, hid.at[hslot(0, c)], 0, mate)
    hid[q] = half[...]

    for k in range(1, 8):
        cp.stage.arrived(stage.at[(q + 8 - k) % 8], k - 1)
    packer = pack(12)
    for j in range(0, UNIT, 512):
        r.unit[:, j : j + 512] = dot(
            packer, stage[:, :, j : j + 512].reshape(128, 512)
        ).astype(BF)
    ring = Plane(r.w, cp.w, 96, (0, 1, 3))
    ring.first(r.unit)
    mine = pltpu.make_async_copy(r.unit, r.w.at[g], local.at[1])
    mine.start()
    for one in (load.initf, load.cinner, load.cshared, load.binner, load.ngain, load.lens, load.grps, load.pt):
        one.wait()
    for k in range(4):
        r.initb[:, k * N : k * N + N] = r.initf[k].astype(BF)

    cp.hid.arrived(hpart(-1, True), 0)
    cp.hid.go(hpart(-1, True), hpart(-1, True), 4, right)
    cp.hid.arrived(hpart(1, False), 2)
    cp.hid.go(hpart(1, False), hpart(1, False), 5, left)
    for k in range(1, 4):
        cp.ostage.go(outp, r.ostage.at[y], k - 1, near[k - 1])
    ring.turn(1)
    ring.turn(3)
    ring.turn(2)
    ring.pass_on(0)
    cp.hid.arrived(hpart(-1, False), 1)
    cp.cross.go(hid.at[hslot(-1, c)], hid.at[hslot(-1, c)], 1, mate)
    cp.hid.arrived(hpart(1, True), 3)
    cp.cross.go(hid.at[hslot(1, c)], hid.at[hslot(1, c)], 2, mate)
    ring.pass_on(1)
    ring.pass_on(3)
    oring = Plane(r.wo, cp.wo, 96, (0, 1, 3))
    cp.hid.arrived(hpart(2, True), 4)
    cp.hid.arrived(hpart(2, False), 5)
    cp.cross.go(hid.at[hslot(2, c)], hid.at[hslot(2, c)], 3, mate)
    for k, dy in enumerate((0, -1, 1, 2)):
        cp.cross.arrived(hid.at[hslot(dy, 1 - c)], k)
    cp.edge.go(hid.at[7, pl.ds(112, 16)], r.edge, 0, next_dev)
    for k in range(1, 4):
        cp.ostage.arrived(r.ostage.at[(y + 4 - k) % 4], k - 1)
    for j in range(0, d, 512):
        r.ounit[:, j : j + 512] = dot(
            pack(24), r.ostage[:, :, j : j + 512].reshape(128, 512)
        ).astype(BF)
    ring.pass_on(2)
    for k in range(4):
        ring.end(k)
    mine.wait()
    oring.first(r.ounit)
    mine = pltpu.make_async_copy(r.ounit, r.wo.at[g], local.at[1])
    mine.start()

    w, xs, bc, steps, sg = r.w, r.xs, r.bc, r.steps, r.sg

    def columns(a, z):
        return w[:, :, a:z].reshape(d, z - a)

    def project_bc(i, _):
        at = pl.multiple_of(i * 256, 256)
        got = dot(hid[pl.ds(i * 2, 2)].reshape(256, d), columns(2 * CH, UNIT)).astype(BF)
        bc[c, pl.ds(pl.multiple_of(at + 16, 16), 256), :] = got[:, :N]
        steps[pl.ds(at, 256), :] = got[:, N:]
        return 0

    lax.fori_loop(0, 4, project_bc, 0)
    mid = pl.ds(16, 1024)
    cp.bc.go(bc.at[c, mid], bc.at[c, mid], 0, mate)

    def project(i, _):
        at = pl.multiple_of(i * 256, 256)
        got = dot(hid[pl.ds(i * 2, 2)].reshape(256, d), columns(0, 2 * CH)).astype(BF)
        sg[pl.ds(at, 256), :] = got[:, :CH].astype(F32)
        xs[pl.ds(pl.multiple_of(at + 8, 8), 256), 0:CH] = got[:, CH:].astype(F32)
        return 0

    lax.fori_loop(0, 2, project, 0)
    cp.edge.arrived(r.edge, 0)
    bc[c, 0:16, :] = dot(r.edge[...], columns(2 * CH, 2 * CH + N)).astype(BF)
    cp.bc.go(bc.at[c, pl.ds(0, 16)], bc.at[c, pl.ds(0, 16)], 1, mate)
    xs[0:8, 0:CH] = dot(r.edge[...], columns(CH, 2 * CH))[8:16].astype(BF).astype(F32)
    lax.fori_loop(2, 4, project, 0)
    cp.bc.arrived(bc.at[1 - c, mid], 0)
    cp.bc.arrived(bc.at[1 - c, pl.ds(0, 16)], 1)
    for k in range(2):
        xs[0:8, CH + k * N : CH + k * N + N] = bc[k, 0:16, :].astype(F32)[8:16]
        xs[8:1032, CH + k * N : CH + k * N + N] = bc[k, 16:1040, :].astype(F32)

    hot = head_hot()
    starts = []
    total = jnp.int32(0)
    for k in range(8):
        starts.append(total)
        total = total + lens[k]
    row = lax.broadcasted_iota(jnp.int32, (128, 128), 0)
    col = lax.broadcasted_iota(jnp.int32, (128, 128), 1)
    head0 = c * 24 + y * MINE
    pick = jnp.where(col < MINE, (row == col + head0).astype(F32), 0.0).astype(BF)
    wrow = lax.broadcasted_iota(jnp.int32, (128, CH), 0)
    wcol = lax.broadcasted_iota(jnp.int32, (128, CH), 1)
    pickx = (wrow == wcol // HEAD + head0).astype(F32).astype(BF)
    hsplit = three(jnp.broadcast_to(params[:, 0:128], (8, 128)))

    def take(kind):
        at = jnp.where(col < MINE, (row == col + y * MINE + 24 * kind).astype(F32), 0.0).astype(BF)
        return sum(dot(part, at) for part in hsplit)[0:1]

    def takex(kind):
        at = (wrow == wcol // HEAD + y * MINE + 24 * kind).astype(F32).astype(BF)
        return sum(dot(part, at) for part in hsplit)[0:1]

    rate6 = jnp.where(col[0:1] < MINE, -jnp.exp(take(1)), 0.0)
    bias6, biasx, skipx = take(0), takex(0), takex(2)
    taps = cinner[...]
    biasc = r.binner[...]
    small, dps = r.small, r.dps
    small[0] = jnp.zeros((CH, N), BF)

    def find(pos):
        first = jnp.zeros(pos.shape, jnp.int32)
        for k in range(1, 8):
            first = jnp.where(pos >= starts[k], starts[k], first)
        return first

    def advance(i, held):
        old, dp, dprow = held
        at = pl.multiple_of(i * 256, 256)
        base = g * 1024 + i * 256
        first = find(base + lax.broadcasted_iota(jnp.int32, (256, 128), 0))
        off = base + lax.broadcasted_iota(jnp.int32, (256, 128), 0) - first
        xc = biasc + jnp.zeros((256, CH), F32)
        bcc = params[:, 256:512] + jnp.zeros((256, 2 * N), F32)
        window = xs[pl.ds(at, 264), :]
        for lag in range(CONV):
            ok = (off >= lag).astype(F32)
            part = window[8 - lag : 264 - lag, :]
            xc = xc + taps[lag : lag + 1, :] * part[:, :CH] * wide(ok)
            bcc = bcc + cshared[lag : lag + 1, :] * part[:, CH:] * jnp.concatenate([ok, ok], axis=1)
        xc = silu(xc)
        bcc = silu(bcc)
        b_all = bcc[:, :N].astype(BF)
        r.b[pl.ds(at, 256), :] = b_all
        r.c[pl.ds(at, 256), :] = bcc[:, N:].astype(BF)
        step = steps[pl.ds(at, 256), :]
        dt6 = softplus(dot(step, pick) + bias6)
        log6 = rate6 * dt6
        dtx = softplus(dot(step, pickx) + biasx)
        xdt_all = xc * dtx
        r.xdt[pl.ds(at, 256), :] = xdt_all.astype(BF)
        r.y[pl.ds(at, 256), :] = skipx * xc
        for sub in range(2):
            k = i * 2 + sub
            p0 = base + sub * 128
            rows = slice(sub * 128, sub * 128 + 128)
            f0 = first[rows, :]
            mask = (row >= col) & (f0 == find(p0 + col))
            maskb = mask.astype(F32).astype(BF)
            cum = sum(dot(maskb, part) for part in three(log6[rows, :]))
            there = pl.ds(pl.multiple_of(at + sub * 128, 128), 128)
            r.cum[there, :] = cum
            cumt = cum.T
            flast = jnp.int32(0)
            glast = grps[0]
            for j in range(1, 8):
                got = p0 + 127 >= starts[j]
                flast = jnp.where(got, starts[j], flast)
                glast = jnp.where(got, grps[j], glast)
            w6 = jnp.exp(jnp.where(f0 == flast, cum[127:128, :] - cum, NEG))
            xw = (xdt_all[rows, :] * expand(w6, hot)).astype(BF)
            summary = dot_tn(xw, b_all[rows, :])
            keep = (flast < p0).astype(F32)
            ecum = jnp.exp(cum)
            r.fx[there, :] = expand(
                jnp.where(f0 < p0, ecum, 0.0) * dprow, hot
            )
            scale = jnp.exp(jnp.broadcast_to(cumt[0:8, 127:128], (8, 128)))
            dp = dp * scale * keep
            dprow = dprow * jnp.exp(cum[127:128, :]) * keep
            dps[k] = dp
            start = r.initf[0]
            for j in range(1, 4):
                start = jnp.where(glast == j, r.initf[j], start)
            old = jnp.where(flast < p0, old, start)
            old = jnp.concatenate(
                [scale[h : h + 1, :] * old[h * HEAD : h * HEAD + HEAD, :] for h in range(MINE)], axis=0
            ) + summary
            small[k + 1] = old.astype(BF)
        return old, dp, dprow

    held = (jnp.zeros((CH, N), F32), jnp.ones((8, 128), F32), jnp.ones((1, 128), F32))
    held = lax.fori_loop(0, 2, advance, held)
    for k in (1, 3, 2):
        oring.turn(k)
    oring.pass_on(0)
    last, dplast, _ = lax.fori_loop(2, 4, advance, held)

    state, parts, befores, carry = r.state, r.parts, r.befores, r.carry
    for j in range(3):
        state[:, j] = last[j * 128 : j * 128 + 128].reshape(16, 8, N)
    state[:, 3] = jnp.broadcast_to(dplast[None], (16, 8, N))
    for k in range(1, 16):
        cp.part.go(state.at[(g + k) % 16], parts.at[g], k - 1, peers[k - 1])
    parts[g] = state[g]
    for k in range(1, 4):
        t = (y + k) % 4
        cp.page.go(small.at[pl.ds(t * 2 + 1, 2)], r.pages.at[y], k - 1, near[k - 1])
        cp.decay.go(dps.at[pl.ds(t * 2, 2)], r.rates.at[y], k - 1, near[k - 1])
    for k in range(2):
        r.pages[y, k] = small[y * 2 + 1 + k]
        r.rates[y, k] = dps[y * 2 + k]

    def inside(i, _):
        for sub in range(2):
            k = i * 2 + sub
            p0 = g * 1024 + k * 128
            at = pl.ds(pl.multiple_of(k * 128, 128), 128)
            f0 = find(p0 + row)
            mask = (row >= col) & (f0 == find(p0 + col))
            cum = r.cum[at, :]
            cumt = cum.T
            cb = r.c[at, :]
            cf = cb.astype(F32)
            scores = dot_nt(cb, r.b[at, :])
            gid = jnp.zeros((128, 128), jnp.int32) + grps[0]
            for j in range(1, 8):
                gid = jnp.where(p0 + row >= starts[j], grps[j], gid)
            gid = jnp.where(f0 < p0, 4, gid)
            chot = jnp.concatenate(
                [jnp.where(gid == j, cf, 0.0).astype(BF) for j in range(4)], axis=1
            )
            read = dot_nt(jnp.where(gid == 4, cf, 0.0).astype(BF), small[k])
            read = read + dot_nt(chot, r.initb[...])
            lane = col
            pieces = []
            for pair in range(3):
                xp = r.xdt[at, pair * 128 : pair * 128 + 128]
                got = []
                for h in (2 * pair, 2 * pair + 1):
                    diff = cum[:, h : h + 1] - cumt[h : h + 1, :]
                    mix = jnp.exp(jnp.where(mask, diff, NEG)) * scores
                    got.append(dot(mix.astype(BF), xp))
                pieces.append(jnp.where(lane < HEAD, got[0], got[1]))
            r.y[at, :] = (
                r.y[at, :] + expand(jnp.exp(cum), hot) * read + jnp.concatenate(pieces, axis=1)
            )
            sg[at, :] = silu(sg[at, :])
        return 0

    lax.fori_loop(0, 2, inside, 0)
    for k in range(1, 16):
        cp.part.arrived(parts.at[(g + 16 - k) % 16], k - 1)
    hb = g // 8
    run = [jnp.zeros((8, 128), F32) for _ in range(3)]
    for k in range(16):
        for j in range(3):
            befores[k, j] = run[j]
            run[j] = parts[k, 3, pl.ds(hb + 2 * j, 1), :] * run[j] + parts[k, j]
    for k in range(1, 16):
        cp.back.go(befores.at[(g + k) % 16], carry.at[g], k - 1, peers[k - 1])
    carry[g] = befores[g]
    oring.pass_on(1)
    oring.pass_on(3)
    lax.fori_loop(2, 4, inside, 0)
    for k in range(1, 16):
        cp.back.arrived(carry.at[(g + 16 - k) % 16], k - 1)

    cs = jnp.concatenate([carry[:, j].reshape(128, N) for j in range(3)], axis=0).astype(BF)
    carries = r.carries
    carries[y] = cs
    ones = jnp.ones((8, CH), BF)
    gain = r.ngain[...]
    gated, came, sq, sqin, acc = r.gated, r.came, r.sq, r.sqin, r.acc

    def gate(t):
        at = pl.ds(pl.multiple_of(t * 256, 256), 256)
        full = r.y[at, :] + r.fx[at, :] * dot_nt(r.c[at, :], cs)
        gv = full * sg[at, :]
        g2 = gv * gv
        top = g2.astype(BF)
        rest = (g2 - top.astype(F32)).astype(BF)
        sq[t] = dot_nt(ones, top) + dot_nt(ones, rest)
        gated[t] = (gv * gain).astype(BF)

    for k in (2, 1, 3):
        t = (y + k) % 4
        gate(t)
        cp.gated.go(gated.at[t], came.at[y], k - 1, near[k - 1])
        cp.square.go(sq.at[t], sqin.at[y], k - 1, near[k - 1])
    for k in range(1, 4):
        cp.state.go(carries.at[y], carries.at[y], k - 1, near[k - 1])
    gate(y)
    came[y] = gated[y]
    sqin[y] = sq[y]
    oring.pass_on(2)
    for k in range(4):
        oring.end(k)
    mine.wait()

    def multiply(t, fresh):
        lanes = pl.ds(pl.multiple_of(t * CH, CH), CH)
        for n in range(0, 16, 4):
            cols = slice(n * 96, n * 96 + 384)
            got = dot_nt(came[t], r.wo[n : n + 4, :, lanes].reshape(384, CH))
            acc[:, cols] = got if fresh else acc[:, cols] + got

    multiply(y, True)
    for k in (1, 3, 2):
        t = (y + 4 - k) % 4
        cp.gated.arrived(came.at[t], k - 1)
        cp.square.arrived(sqin.at[t], k - 1)
        multiply(t, False)
    r.sqown[...] = sqin[0] + sqin[1] + sqin[2] + sqin[3]
    r.pout[...] = acc[pl.ds(pl.multiple_of((1 - c) * 128, 128), 128), :].astype(BF)
    cp.mate.go(r.pout, r.pin, 0, mate)
    cp.mate.go(r.sqown, r.sqmate, 1, mate)

    swap = pt[0] != (g * 4 + y) * 2
    for k in range(4):
        t = (y + 4 - k) % 4
        if k:
            cp.state.arrived(carries.at[t], k - 1)
            cp.page.arrived(r.pages.at[t], k - 1)
            cp.decay.arrived(r.rates.at[t], k - 1)
        for h in range(MINE):
            at = slice(h * HEAD, h * HEAD + HEAD)
            into = carries[t, at, :].astype(F32)
            one, two = (
                r.pages[t, j, at, :].astype(F32) + r.rates[t, j, h : h + 1, :] * into
                for j in range(2)
            )
            r.snaps[0, t, at, :] = jnp.where(swap, two, one)
            r.snaps[1, t, at, :] = jnp.where(swap, one, two)
    snaps = pltpu.make_async_copy(r.snaps, page_o, local.at[0])
    snaps.start()

    cp.mate.arrived(r.pin, 0)
    cp.mate.arrived(r.sqmate, 1)
    mytoks = pl.ds(pl.multiple_of(c * 128, 128), 128)
    total = r.sqown[:, mytoks] + r.sqmate[:, mytoks]
    scale = lax.rsqrt(total / DI + EPS)
    scale = jnp.broadcast_to(scale[0:1, :], (128, 128)).T
    for n in range(0, 1536, 128):
        cols = slice(n, n + 128)
        r.res[:, cols] = ((acc[mytoks, cols] + r.pin[:, cols].astype(F32)) * scale).astype(BF)
    res = pltpu.make_async_copy(r.res, out_o, local.at[16])
    res.start()
    res.wait()
    snaps.wait()
    for part in vars(cp).values():
        part.close()


def on_device(
    hidden_in, gate_proj, inner_proj, small_proj, row_layout, conv_inner, conv_shared,
    bias_inner, bias_shared, dt_bias, decay_log, skip_gain, norm_gain, out_proj,
    prompt_lengths, group_map, init_states, page_table,
):
    d = hidden_in.shape[1]
    params = jnp.concatenate(
        [dt_bias, decay_log, skip_gain, jnp.zeros((56,), F32), row_layout.astype(F32), bias_shared]
    )
    hbm = pl.BlockSpec(memory_space=pltpu.HBM)
    dma = pltpu.SemaphoreType.DMA
    scratch = list(buffers(d).values())
    for count in COPY.values():
        scratch += [dma((count,)), dma((count,))]
    mixed, pages = pl.pallas_call(
        layer_kernel,
        in_specs=[hbm] * 14,
        out_specs=[hbm, hbm],
        out_shape=[
            jax.ShapeDtypeStruct((128, d), BF),
            jax.ShapeDtypeStruct((2, 4, CH, N), F32),
        ],
        scratch_shapes=scratch + [dma((18,))],
        compiler_params=pltpu.CompilerParams(
            collective_id=0, has_side_effects=True, vmem_limit_bytes=60 << 20
        ),
        name="layer",
    )(
        hidden_in, gate_proj, inner_proj, small_proj, conv_inner, conv_shared, bias_inner, norm_gain, params,
        out_proj.T, prompt_lengths, group_map, page_table, init_states.reshape(4, 24 * HEAD, N),
    )
    return (mixed, pages.reshape(2, 24, HEAD, N))


def solution(mesh):
    fine = Mesh(mesh.devices.reshape(4, 4, 4, 2), ("z", "x", "y", "tp"))
    seq = ("z", "x", "y")
    every = ("z", "x", "y", "tp")
    placed = (
        P(seq, None),
        P(every, None),
        P(every, None),
        P(every, None),
        P(),
        P(None, "tp"),
        P(),
        P("tp"),
        P(),
        P("tp"),
        P("tp"),
        P("tp"),
        P("tp"),
        P("tp", seq),
        P(),
        P(),
        P(None, "tp", None, None),
        P(seq),
    )
    return jax.shard_map(
        on_device,
        mesh=fine,
        in_specs=placed,
        out_specs=(P(every, None), P(seq, "tp", None, None)),
        check_vma=False,
    )
```

```python
from types import SimpleNamespace

import jax
import jax.numpy as jnp
from jax import lax
from jax.experimental import pallas as pl
from jax.experimental.pallas import tpu as pltpu
from jax.sharding import Mesh
from jax.sharding import PartitionSpec as P

N = 128
CONV = 4
PAGE = 128
DI = 3072
HEAD = 64
MINE = 6
CH = MINE * HEAD
EPS = 1e-05
BF = jnp.bfloat16
F32 = jnp.float32
NEG = -1e30


def dot(a, b):
    return jnp.dot(a, b, preferred_element_type=F32)


def dot_nt(a, b):
    return lax.dot_general(a, b, (((1,), (1,)), ((), ())), preferred_element_type=F32)


def dot_tn(a, b):
    return lax.dot_general(a, b, (((0,), (0,)), ((), ())), preferred_element_type=F32)


def silu(v):
    return v / (1.0 + jnp.exp(-v))


def softplus(v):
    return jnp.maximum(v, 0.0) + jnp.log1p(jnp.exp(-jnp.abs(v)))


def three(v):
    hi = v.astype(BF)
    rest = v - hi.astype(F32)
    mid = rest.astype(BF)
    return hi, mid, (rest - mid.astype(F32)).astype(BF)


def expand(v, hot):
    hi = v.astype(BF)
    lo = (v - hi.astype(F32)).astype(BF)
    return dot(hi, hot) + dot(lo, hot)


def head_hot():
    row = lax.broadcasted_iota(jnp.int32, (128, CH), 0)
    col = lax.broadcasted_iota(jnp.int32, (128, CH), 1)
    return (row == col // HEAD).astype(F32).astype(BF)


def wide(m):
    return jnp.concatenate([m, m, m], axis=1)


class Copies:
    def __init__(self, send, recv):
        self.send, self.recv, self.open = send, recv, []

    def go(self, src, dst, slot, device):
        copy = pltpu.make_async_remote_copy(
            src_ref=src,
            dst_ref=dst,
            send_sem=self.send.at[slot],
            recv_sem=self.recv.at[slot],
            device_id=device,
            device_id_type=pl.DeviceIdType.MESH,
        )
        copy.start()
        self.open.append(copy)

    def arrived(self, dst, slot):
        pltpu.make_async_remote_copy(
            src_ref=dst,
            dst_ref=dst,
            send_sem=self.send.at[slot],
            recv_sem=self.recv.at[slot],
            device_id=self.me,
            device_id_type=pl.DeviceIdType.MESH,
        ).wait_recv()

    def close(self):
        for copy in self.open:
            copy.wait_send()


def coords():
    return (
        lax.axis_index("z"),
        lax.axis_index("x"),
        lax.axis_index("y"),
        lax.axis_index("tp"),
    )


class Plane:
    def __init__(self, out, copies, rows, relay):
        self.out, self.copies, self.half, self.relay = out, copies, rows // 2, relay
        z, x, y, c = coords()
        self.y, self.c = y, c
        self.a = x * (1 - c) + z * c
        self.b = z * (1 - c) + x * c

    def at(self, da, db):
        a = (self.a + da + 8) % 4
        b = (self.b + db + 8) % 4
        c = self.c
        return b * (1 - c) + a * c, a * (1 - c) + b * c

    def device(self, da, db):
        z, x = self.at(da, db)
        return (z, x, self.y, self.c)

    def full(self, d, db=0):
        z, x = self.at(-d, db)
        return self.out.at[z * 4 + x]

    def low(self, d, db):
        z, x = self.at(-d, db)
        return self.out.at[z * 4 + x, pl.ds(0, self.half)]

    def high(self, d, db):
        z, x = self.at(-d, db)
        return self.out.at[z * 4 + x, pl.ds(self.half, self.half)]

    def first(self, own):
        for d in (1, 3, 2):
            self.copies.go(own, self.full(0), d - 1, self.device(d, 0))
        self.second(0, own)

    def second(self, d, src=None):
        src = self.full(d) if src is None else src
        self.copies.go(src, self.full(d), 3 + 4 * d, self.device(0, 1))
        self.copies.go(src, self.full(d), 4 + 4 * d, self.device(0, -1))
        if d not in self.relay:
            self.copies.go(src, self.full(d), 5 + 4 * d, self.device(0, 2))

    def turn(self, d):
        self.copies.arrived(self.full(d), d - 1)
        self.second(d)

    def pass_on(self, d):
        self.copies.arrived(self.full(d, -1), 3 + 4 * d)
        if d in self.relay:
            self.copies.go(self.low(d, -1), self.low(d, -1), 5 + 4 * d, self.device(0, 1))
        self.copies.arrived(self.full(d, 1), 4 + 4 * d)
        if d in self.relay:
            self.copies.go(self.high(d, 1), self.high(d, 1), 6 + 4 * d, self.device(0, -1))

    def end(self, d):
        if d in self.relay:
            self.copies.arrived(self.low(d, 2), 5 + 4 * d)
            self.copies.arrived(self.high(d, 2), 6 + 4 * d)
        else:
            self.copies.arrived(self.full(d, 2), 5 + 4 * d)


def pack(width):
    row = lax.broadcasted_iota(jnp.int32, (96, 128), 0)
    col = lax.broadcasted_iota(jnp.int32, (96, 128), 1)
    padded = 128 // (96 // width)
    return (col == row // width * padded + row % width).astype(F32).astype(BF)


UNIT = 1024
COPY = dict(
    stage=7, ostage=3, hid=6, cross=4, w=19, edge=1, wo=19, bc=2,
    part=15, back=15, page=3, decay=3, mate=4, ring=6, sum=7, state=3,
)


def buffers(d):
    vmem = pltpu.VMEM
    return dict(
        hidden=vmem((128, d), BF),
        gate_w=vmem((12, DI), F32),
        inner_w=vmem((12, DI), F32),
        small_w=vmem((12, 304), F32),
        cinner=vmem((4, CH), F32),
        cshared=vmem((4, 2 * N), F32),
        binner=vmem((1, CH), F32),
        ngain=vmem((1, CH), F32),
        params=vmem((1, 512), F32),
        out_w=vmem((24, d), F32),
        lens=pltpu.SMEM((8,), jnp.int32),
        grps=pltpu.SMEM((8,), jnp.int32),
        pt=pltpu.SMEM((2,), jnp.int32),
        pieces=vmem((8, 16, UNIT), BF),
        stage=vmem((8, 16, UNIT), BF),
        unit=vmem((96, UNIT), BF),
        half=vmem((128, d), BF),
        w=vmem((16, 96, UNIT), BF),
        hid=vmem((8, 128, d), BF),
        edge=vmem((16, d), BF),
        initf=vmem((4, CH, N), F32),
        initb=vmem((CH, 4 * N), BF),
        sg=vmem((1024, CH), F32),
        xs=vmem((1032, CH + 2 * N), F32),
        steps=vmem((1024, 128), BF),
        y=vmem((1024, CH), F32),
        xdt=vmem((1024, CH), BF),
        b=vmem((1024, N), BF),
        c=vmem((1024, N), BF),
        cum=vmem((1024, 128), F32),
        fx=vmem((1024, CH), F32),
        small=vmem((9, CH, N), BF),
        dps=vmem((8, 8, N), F32),
        carries=vmem((4, CH, N), BF),
        pages=vmem((4, 2, CH, N), BF),
        rates=vmem((4, 2, 8, N), F32),
        bc=vmem((2, 1040, N), BF),
        state=vmem((16, 4, 8, N), F32),
        parts=vmem((16, 4, 8, N), F32),
        befores=vmem((16, 3, 8, N), F32),
        carry=vmem((16, 3, 8, N), F32),
        outp=vmem((4, 32, CH), BF),
        ostage=vmem((4, 32, CH), BF),
        ounit=vmem((96, CH), BF),
        wo=vmem((16, 96, CH), BF),
        opp=vmem((128, d), BF),
        ahead=vmem((128, d), BF),
        behind=vmem((128, d), BF),
        own=vmem((128, d), BF),
        xs_out=vmem((4, 128, d), BF),
        xs_in=vmem((4, 128, d), BF),
        low=vmem((64, d), BF),
        high=vmem((64, d), BF),
        from_l=vmem((128, d), BF),
        from_r=vmem((128, d), BF),
        sq=vmem((8, 8, 128), F32),
        sqr=vmem((8, 8, 128), F32),
        snaps=vmem((2, 4, CH, N), F32),
        res=vmem((128, d), BF),
    )


def layer_kernel(
    hidden_h, gate_h, inner_h, small_h, cinner_h, cshared_h, binner_h, ngain_h, params_h, out_h,
    lens_h, grps_h, pt_h, init, out_o, page_o, *refs,
):
    d = hidden_h.shape[1]
    names = list(buffers(d))
    r = SimpleNamespace(**dict(zip(names, refs)))
    sems = refs[len(names):]
    z, x, y, c = coords()
    me_not = (z, x, y, 1 - c)
    cp = SimpleNamespace()
    for i, name in enumerate(COPY):
        setattr(cp, name, Copies(sems[2 * i], sems[2 * i + 1]))
        getattr(cp, name).me = me_not
    local = sems[2 * len(COPY)]
    q = y * 2 + c
    g = z * 4 + x
    mate = me_not
    right, left = (z, x, (y + 1) % 4, c), (z, x, (y + 3) % 4, c)
    near = [(z, x, (y + k) % 4, c) for k in range(1, 4)]
    group = [(z, x, ((q + k) % 8) // 2, (q + k) % 2) for k in range(1, 8)]
    peers = [(((g + k) % 16) // 4, ((g + k) % 16) % 4, y, c) for k in range(1, 16)]
    next_dev = peers[0]
    barrier = pltpu.get_barrier_semaphore()
    for device in group + peers:
        pl.semaphore_signal(
            barrier, inc=1, device_id=device, device_id_type=pl.DeviceIdType.MESH
        )

    mychan = pl.ds(pl.multiple_of(y * CH, CH), CH)
    loads = dict(
        gate_w=gate_h,
        inner_w=inner_h,
        small_w=small_h,
        hidden=hidden_h.at[pl.ds(pl.multiple_of(c * 128, 128), 128)],
        out_w=out_h,
        params=params_h,
        binner=binner_h.at[mychan],
        ngain=ngain_h.at[mychan],
        cinner=cinner_h.at[:, mychan],
        cshared=cshared_h,
        lens=lens_h,
        grps=grps_h,
        pt=pt_h,
        initf=init.at[:, mychan],
    )
    load = SimpleNamespace()
    for i, name in enumerate(loads):
        to = getattr(r, name)
        if loads[name].ndim == 1 and to.shape[0] == 1:
            to = to.at[0]
        setattr(load, name, pltpu.make_async_copy(loads[name], to, local.at[2 + i]))
        getattr(load, name).start()
    gate_w, inner_w, small_w, hidden = r.gate_w, r.inner_w, r.small_w, r.hidden
    params, cinner, cshared = r.params, r.cinner, r.cshared
    lens, grps, pt, outp = r.lens, r.grps, r.pt, r.outp
    pieces, stage = r.pieces, r.stage
    outp[...] = jnp.zeros_like(outp)
    pieces[...] = jnp.zeros_like(pieces)
    for one in (load.gate_w, load.inner_w, load.small_w, load.out_w):
        one.wait()
    for t in range(4):
        outp[t, 0:24, :] = r.out_w[:, t * CH : t * CH + CH].astype(BF)
    for t in range(8):
        a = 1536 * (t % 2) + CH * (t // 2)
        pieces[t, 0:12, 0:CH] = gate_w[:, a : a + CH].astype(BF)
        pieces[t, 0:12, CH : 2 * CH] = inner_w[:, a : a + CH].astype(BF)
        b = N * (t % 2)
        pieces[t, 0:12, 2 * CH : 2 * CH + N] = small_w[:, b : b + N].astype(BF)
        pieces[t, 0:12, 2 * CH + N : 2 * CH + N + 48] = small_w[:, 2 * N :].astype(BF)
    half = r.half
    load.params.wait()
    load.hidden.wait()
    lay = jnp.broadcast_to(params[:, 128:256], (8, 128)).astype(BF)
    rows = hidden[...]
    for j in range(0, d, CH):
        brow = lax.broadcasted_iota(jnp.int32, (128, CH), 0)
        bcol = lax.broadcasted_iota(jnp.int32, (128, CH), 1) + j
        block = dot(lay, (brow == bcol // 12).astype(F32).astype(BF))[0:1]
        want = block * 12.0 + (bcol[0:1] % 12).astype(F32)
        frow = lax.broadcasted_iota(jnp.int32, (d, CH), 0).astype(F32)
        pick = jnp.where(frow == want, 1.0, 0.0).astype(BF)
        half[:, j : j + CH] = dot(rows, pick).astype(BF)
    pl.semaphore_wait(barrier, len(group) + len(peers))

    for k in range(1, 8):
        cp.stage.go(pieces.at[(q + k) % 8], stage.at[q], k - 1, group[k - 1])
    stage[q] = pieces[q]
    r.ostage[y] = outp[y]

    hid = r.hid

    def hslot(dy, core):
        return ((y + dy + 4) % 4) * 2 + core

    def hpart(dy, low):
        return hid.at[hslot(dy, c), pl.ds(0 if low else 64, 64)]

    lo, hi = pl.ds(0, 64), pl.ds(64, 64)
    cp.hid.go(half.at[lo], hpart(0, True), 0, right)
    cp.hid.go(half.at[hi], hpart(0, False), 2, left)
    cp.hid.go(half.at[hi], hpart(0, False), 1, right)
    cp.hid.go(half.at[lo], hpart(0, True), 3, left)
    cp.cross.go(half, hid.at[hslot(0, c)], 0, mate)
    hid[q] = half[...]

    for k in range(1, 8):
        cp.stage.arrived(stage.at[(q + 8 - k) % 8], k - 1)
    packer = pack(12)
    for j in range(0, UNIT, 512):
        r.unit[:, j : j + 512] = dot(
            packer, stage[:, :, j : j + 512].reshape(128, 512)
        ).astype(BF)
    ring = Plane(r.w, cp.w, 96, (0, 1, 3))
    ring.first(r.unit)
    mine = pltpu.make_async_copy(r.unit, r.w.at[g], local.at[1])
    mine.start()
    for one in (load.initf, load.cinner, load.cshared, load.binner, load.ngain, load.lens, load.grps, load.pt):
        one.wait()
    for k in range(4):
        r.initb[:, k * N : k * N + N] = r.initf[k].astype(BF)

    cp.hid.arrived(hpart(-1, True), 0)
    cp.hid.go(hpart(-1, True), hpart(-1, True), 4, right)
    cp.hid.arrived(hpart(1, False), 2)
    cp.hid.go(hpart(1, False), hpart(1, False), 5, left)
    for k in range(1, 4):
        cp.ostage.go(outp.at[(y + k) % 4], r.ostage.at[y], k - 1, near[k - 1])
    ring.turn(1)
    ring.turn(3)
    ring.turn(2)
    ring.pass_on(0)
    cp.hid.arrived(hpart(-1, False), 1)
    cp.cross.go(hid.at[hslot(-1, c)], hid.at[hslot(-1, c)], 1, mate)
    cp.hid.arrived(hpart(1, True), 3)
    cp.cross.go(hid.at[hslot(1, c)], hid.at[hslot(1, c)], 2, mate)
    ring.pass_on(1)
    ring.pass_on(3)
    oring = Plane(r.wo, cp.wo, 96, ())
    cp.hid.arrived(hpart(2, True), 4)
    cp.hid.arrived(hpart(2, False), 5)
    cp.cross.go(hid.at[hslot(2, c)], hid.at[hslot(2, c)], 3, mate)
    for k, dy in enumerate((0, -1, 1, 2)):
        cp.cross.arrived(hid.at[hslot(dy, 1 - c)], k)
    cp.edge.go(hid.at[7, pl.ds(112, 16)], r.edge, 0, next_dev)
    for k in range(1, 4):
        cp.ostage.arrived(r.ostage.at[(y + 4 - k) % 4], k - 1)
    r.ounit[...] = dot(pack(24), r.ostage[...].reshape(128, CH)).astype(BF)
    ring.pass_on(2)
    for k in range(4):
        ring.end(k)
    mine.wait()
    oring.first(r.ounit)
    mine = pltpu.make_async_copy(r.ounit, r.wo.at[g], local.at[1])
    mine.start()

    w, xs, bc, steps, sg = r.w, r.xs, r.bc, r.steps, r.sg

    def columns(a, z):
        return w[:, :, a:z].reshape(d, z - a)

    def project_bc(i, _):
        at = pl.multiple_of(i * 256, 256)
        got = dot(hid[pl.ds(i * 2, 2)].reshape(256, d), columns(2 * CH, UNIT)).astype(BF)
        bc[c, pl.ds(pl.multiple_of(at + 16, 16), 256), :] = got[:, :N]
        steps[pl.ds(at, 256), :] = got[:, N:]
        return 0

    lax.fori_loop(0, 4, project_bc, 0)
    mid = pl.ds(16, 1024)
    cp.bc.go(bc.at[c, mid], bc.at[c, mid], 0, mate)

    def project(i, _):
        at = pl.multiple_of(i * 256, 256)
        got = dot(hid[pl.ds(i * 2, 2)].reshape(256, d), columns(0, 2 * CH)).astype(BF)
        sg[pl.ds(at, 256), :] = got[:, :CH].astype(F32)
        xs[pl.ds(pl.multiple_of(at + 8, 8), 256), 0:CH] = got[:, CH:].astype(F32)
        return 0

    lax.fori_loop(0, 2, project, 0)
    cp.edge.arrived(r.edge, 0)
    bc[c, 0:16, :] = dot(r.edge[...], columns(2 * CH, 2 * CH + N)).astype(BF)
    cp.bc.go(bc.at[c, pl.ds(0, 16)], bc.at[c, pl.ds(0, 16)], 1, mate)
    xs[0:8, 0:CH] = dot(r.edge[...], columns(CH, 2 * CH))[8:16].astype(BF).astype(F32)
    lax.fori_loop(2, 4, project, 0)
    for k in (1, 3, 2):
        oring.turn(k)
    cp.bc.arrived(bc.at[1 - c, mid], 0)
    cp.bc.arrived(bc.at[1 - c, pl.ds(0, 16)], 1)
    for k in range(2):
        xs[0:8, CH + k * N : CH + k * N + N] = bc[k, 0:16, :].astype(F32)[8:16]
        xs[8:1032, CH + k * N : CH + k * N + N] = bc[k, 16:1040, :].astype(F32)

    hot = head_hot()
    starts = []
    total = jnp.int32(0)
    for k in range(8):
        starts.append(total)
        total = total + lens[k]
    row = lax.broadcasted_iota(jnp.int32, (128, 128), 0)
    col = lax.broadcasted_iota(jnp.int32, (128, 128), 1)
    head0 = c * 24 + y * MINE
    pick = jnp.where(col < MINE, (row == col + head0).astype(F32), 0.0).astype(BF)
    wrow = lax.broadcasted_iota(jnp.int32, (128, CH), 0)
    wcol = lax.broadcasted_iota(jnp.int32, (128, CH), 1)
    pickx = (wrow == wcol // HEAD + head0).astype(F32).astype(BF)
    hsplit = three(jnp.broadcast_to(params[:, 0:128], (8, 128)))

    def take(kind):
        at = jnp.where(col < MINE, (row == col + y * MINE + 24 * kind).astype(F32), 0.0).astype(BF)
        return sum(dot(part, at) for part in hsplit)[0:1]

    def takex(kind):
        at = (wrow == wcol // HEAD + y * MINE + 24 * kind).astype(F32).astype(BF)
        return sum(dot(part, at) for part in hsplit)[0:1]

    rate6 = jnp.where(col[0:1] < MINE, -jnp.exp(take(1)), 0.0)
    bias6, biasx, skipx = take(0), takex(0), takex(2)
    taps = cinner[...]
    biasc = r.binner[...]
    small, dps = r.small, r.dps
    small[0] = jnp.zeros((CH, N), BF)

    def find(pos):
        first = jnp.zeros(pos.shape, jnp.int32)
        for k in range(1, 8):
            first = jnp.where(pos >= starts[k], starts[k], first)
        return first

    def advance(i, held):
        old, dp, dprow = held
        at = pl.multiple_of(i * 256, 256)
        base = g * 1024 + i * 256
        first = find(base + lax.broadcasted_iota(jnp.int32, (256, 128), 0))
        off = base + lax.broadcasted_iota(jnp.int32, (256, 128), 0) - first
        xc = biasc + jnp.zeros((256, CH), F32)
        bcc = params[:, 256:512] + jnp.zeros((256, 2 * N), F32)
        window = xs[pl.ds(at, 264), :]
        for lag in range(CONV):
            ok = (off >= lag).astype(F32)
            part = window[8 - lag : 264 - lag, :]
            xc = xc + taps[lag : lag + 1, :] * part[:, :CH] * wide(ok)
            bcc = bcc + cshared[lag : lag + 1, :] * part[:, CH:] * jnp.concatenate([ok, ok], axis=1)
        xc = silu(xc)
        bcc = silu(bcc)
        b_all = bcc[:, :N].astype(BF)
        r.b[pl.ds(at, 256), :] = b_all
        r.c[pl.ds(at, 256), :] = bcc[:, N:].astype(BF)
        step = steps[pl.ds(at, 256), :]
        dt6 = softplus(dot(step, pick) + bias6)
        log6 = rate6 * dt6
        dtx = softplus(dot(step, pickx) + biasx)
        xdt_all = xc * dtx
        r.xdt[pl.ds(at, 256), :] = xdt_all.astype(BF)
        r.y[pl.ds(at, 256), :] = skipx * xc
        for sub in range(2):
            k = i * 2 + sub
            p0 = base + sub * 128
            rows = slice(sub * 128, sub * 128 + 128)
            f0 = first[rows, :]
            mask = (row >= col) & (f0 == find(p0 + col))
            maskb = mask.astype(F32).astype(BF)
            cum = sum(dot(maskb, part) for part in three(log6[rows, :]))
            there = pl.ds(pl.multiple_of(at + sub * 128, 128), 128)
            r.cum[there, :] = cum
            cumt = cum.T
            flast = jnp.int32(0)
            glast = grps[0]
            for j in range(1, 8):
                got = p0 + 127 >= starts[j]
                flast = jnp.where(got, starts[j], flast)
                glast = jnp.where(got, grps[j], glast)
            w6 = jnp.exp(jnp.where(f0 == flast, cum[127:128, :] - cum, NEG))
            xw = (xdt_all[rows, :] * expand(w6, hot)).astype(BF)
            summary = dot_tn(xw, b_all[rows, :])
            keep = (flast < p0).astype(F32)
            ecum = jnp.exp(cum)
            r.fx[there, :] = expand(
                jnp.where(f0 < p0, ecum, 0.0) * dprow, hot
            )
            scale = jnp.exp(jnp.broadcast_to(cumt[0:8, 127:128], (8, 128)))
            dp = dp * scale * keep
            dprow = dprow * jnp.exp(cum[127:128, :]) * keep
            dps[k] = dp
            start = r.initf[0]
            for j in range(1, 4):
                start = jnp.where(glast == j, r.initf[j], start)
            old = jnp.where(flast < p0, old, start)
            old = jnp.concatenate(
                [scale[h : h + 1, :] * old[h * HEAD : h * HEAD + HEAD, :] for h in range(MINE)], axis=0
            ) + summary
            small[k + 1] = old.astype(BF)
        return old, dp, dprow

    held = (jnp.zeros((CH, N), F32), jnp.ones((8, 128), F32), jnp.ones((1, 128), F32))
    last, dplast, _ = lax.fori_loop(0, 4, advance, held)

    state, parts, befores, carry = r.state, r.parts, r.befores, r.carry
    for j in range(3):
        state[:, j] = last[j * 128 : j * 128 + 128].reshape(16, 8, N)
    state[:, 3] = jnp.broadcast_to(dplast[None], (16, 8, N))
    for k in range(1, 16):
        cp.part.go(state.at[(g + k) % 16], parts.at[g], k - 1, peers[k - 1])
    parts[g] = state[g]
    for k in range(1, 4):
        t = (y + k) % 4
        cp.page.go(small.at[pl.ds(t * 2 + 1, 2)], r.pages.at[y], k - 1, near[k - 1])
        cp.decay.go(dps.at[pl.ds(t * 2, 2)], r.rates.at[y], k - 1, near[k - 1])
    for k in range(2):
        r.pages[y, k] = small[y * 2 + 1 + k]
        r.rates[y, k] = dps[y * 2 + k]

    def inside(i, _):
        for sub in range(2):
            k = i * 2 + sub
            p0 = g * 1024 + k * 128
            at = pl.ds(pl.multiple_of(k * 128, 128), 128)
            f0 = find(p0 + row)
            mask = (row >= col) & (f0 == find(p0 + col))
            cum = r.cum[at, :]
            cumt = cum.T
            cb = r.c[at, :]
            cf = cb.astype(F32)
            scores = dot_nt(cb, r.b[at, :])
            gid = jnp.zeros((128, 128), jnp.int32) + grps[0]
            for j in range(1, 8):
                gid = jnp.where(p0 + row >= starts[j], grps[j], gid)
            gid = jnp.where(f0 < p0, 4, gid)
            chot = jnp.concatenate(
                [jnp.where(gid == j, cf, 0.0).astype(BF) for j in range(4)], axis=1
            )
            read = dot_nt(jnp.where(gid == 4, cf, 0.0).astype(BF), small[k])
            read = read + dot_nt(chot, r.initb[...])
            lane = col
            pieces = []
            for pair in range(3):
                xp = r.xdt[at, pair * 128 : pair * 128 + 128]
                got = []
                for h in (2 * pair, 2 * pair + 1):
                    diff = cum[:, h : h + 1] - cumt[h : h + 1, :]
                    mix = jnp.exp(jnp.where(mask, diff, NEG)) * scores
                    got.append(dot(mix.astype(BF), xp))
                pieces.append(jnp.where(lane < HEAD, got[0], got[1]))
            r.y[at, :] = (
                r.y[at, :] + expand(jnp.exp(cum), hot) * read + jnp.concatenate(pieces, axis=1)
            )
            sg[at, :] = silu(sg[at, :])
        return 0

    lax.fori_loop(0, 2, inside, 0)
    for k in range(1, 16):
        cp.part.arrived(parts.at[(g + 16 - k) % 16], k - 1)
    hb = g // 8
    run = [jnp.zeros((8, 128), F32) for _ in range(3)]
    for k in range(16):
        for j in range(3):
            befores[k, j] = run[j]
            run[j] = parts[k, 3, pl.ds(hb + 2 * j, 1), :] * run[j] + parts[k, j]
    for k in range(1, 16):
        cp.back.go(befores.at[(g + k) % 16], carry.at[g], k - 1, peers[k - 1])
    carry[g] = befores[g]
    lax.fori_loop(2, 4, inside, 0)
    for k in range(4):
        oring.pass_on(k)
        oring.end(k)
    mine.wait()
    for k in range(1, 16):
        cp.back.arrived(carry.at[(g + 16 - k) % 16], k - 1)

    carries = r.carries
    cs = jnp.concatenate([carry[:, j].reshape(128, N) for j in range(3)], axis=0).astype(BF)
    carries[y] = cs
    for k in range(1, 4):
        cp.state.go(carries.at[y], carries.at[y], k - 1, near[k - 1])
    ones = jnp.ones((8, CH), BF)
    gain = r.ngain[...]
    xs_out, xs_in, sq, sqr = r.xs_out, r.xs_in, r.sq, r.sqr

    def partial(dy, k, keep):
        t = (y + dy) % 4
        for part in range(2):
            core = c if part else 1 - c
            at = pl.ds(pl.multiple_of(t * 256 + core * 128, 128), 128)
            full = r.y[at, :] + r.fx[at, :] * dot_nt(r.c[at, :], cs)
            gv = full * sg[at, :]
            g2 = gv * gv
            top = g2.astype(BF)
            rest = (g2 - top.astype(F32)).astype(BF)
            sq[t * 2 + core] = dot_nt(ones, top) + dot_nt(ones, rest)
            gg = (gv * gain).astype(BF)
            for n in range(0, 1536, CH):
                got = dot_nt(gg, r.wo[n // 96 : n // 96 + 4].reshape(CH, CH)).astype(BF)
                if part:
                    keep[:, n : n + CH] = got
                else:
                    xs_out[k, :, n : n + CH] = got
            if not part:
                cp.mate.go(xs_out.at[k], xs_in.at[k], k, mate)

    def join(k, keep):
        cp.mate.arrived(xs_in.at[k], k)
        keep[...] = (keep[...].astype(F32) + xs_in[k].astype(F32)).astype(BF)

    opp, ahead, behind, own = r.opp, r.ahead, r.behind, r.own
    from_l, from_r = r.from_l, r.from_r
    partial(2, 0, opp)
    partial(1, 1, ahead)
    join(0, opp)
    cp.ring.go(opp.at[lo], r.low, 0, right)
    cp.ring.go(opp.at[hi], r.high, 1, left)
    partial(3, 2, behind)
    join(1, ahead)
    cp.ring.go(ahead.at[hi], from_l.at[hi], 2, right)
    join(2, behind)
    cp.ring.go(behind.at[lo], from_r.at[lo], 3, left)
    cp.ring.arrived(r.low, 0)
    ahead[0:64, :] = (ahead[0:64, :].astype(F32) + r.low[...].astype(F32)).astype(BF)
    cp.ring.go(ahead.at[lo], from_l.at[lo], 4, right)
    cp.ring.arrived(r.high, 1)
    behind[64:128, :] = (behind[64:128, :].astype(F32) + r.high[...].astype(F32)).astype(BF)
    cp.ring.go(behind.at[hi], from_r.at[hi], 5, left)
    partial(0, 3, own)
    for k in range(1, 8):
        cp.sum.go(sq.at[(q + k) % 8], sqr.at[q], k - 1, group[k - 1])
    sqr[q] = sq[q]
    join(3, own)

    swap = pt[0] != (g * 4 + y) * 2
    for k in range(4):
        t = (y + 4 - k) % 4
        if k:
            cp.state.arrived(carries.at[t], k - 1)
            cp.page.arrived(r.pages.at[t], k - 1)
            cp.decay.arrived(r.rates.at[t], k - 1)
        for h in range(MINE):
            at = slice(h * HEAD, h * HEAD + HEAD)
            into = carries[t, at, :].astype(F32)
            one, two = (
                r.pages[t, j, at, :].astype(F32) + r.rates[t, j, h : h + 1, :] * into
                for j in range(2)
            )
            r.snaps[0, t, at, :] = jnp.where(swap, two, one)
            r.snaps[1, t, at, :] = jnp.where(swap, one, two)
    snaps = pltpu.make_async_copy(r.snaps, page_o, local.at[0])
    snaps.start()

    for k in range(1, 8):
        cp.sum.arrived(sqr.at[(q + 8 - k) % 8], k - 1)
    total = sqr[0]
    for k in range(1, 8):
        total = total + sqr[k]
    scale = lax.rsqrt(total / DI + EPS)
    scale = jnp.broadcast_to(scale[0:1, :], (128, 128)).T
    cp.ring.arrived(from_l.at[hi], 2)
    cp.ring.arrived(from_r.at[lo], 3)
    cp.ring.arrived(from_l.at[lo], 4)
    cp.ring.arrived(from_r.at[hi], 5)
    for n in range(0, 1536, 128):
        cols = slice(n, n + 128)
        whole = sum(v[:, cols].astype(F32) for v in (own, from_l, from_r))
        r.res[:, cols] = (whole * scale).astype(BF)
    res = pltpu.make_async_copy(r.res, out_o, local.at[16])
    res.start()
    res.wait()
    snaps.wait()
    for part in vars(cp).values():
        part.close()


def on_device(
    hidden_in, gate_proj, inner_proj, small_proj, row_layout, conv_inner, conv_shared,
    bias_inner, bias_shared, dt_bias, decay_log, skip_gain, norm_gain, out_proj,
    prompt_lengths, group_map, init_states, page_table,
):
    d = hidden_in.shape[1]
    params = jnp.concatenate(
        [dt_bias, decay_log, skip_gain, jnp.zeros((56,), F32), row_layout.astype(F32), bias_shared]
    )
    hbm = pl.BlockSpec(memory_space=pltpu.HBM)
    dma = pltpu.SemaphoreType.DMA
    scratch = list(buffers(d).values())
    for count in COPY.values():
        scratch += [dma((count,)), dma((count,))]
    mixed, pages = pl.pallas_call(
        layer_kernel,
        in_specs=[hbm] * 14,
        out_specs=[hbm, hbm],
        out_shape=[
            jax.ShapeDtypeStruct((128, d), BF),
            jax.ShapeDtypeStruct((2, 4, CH, N), F32),
        ],
        scratch_shapes=scratch + [dma((18,))],
        compiler_params=pltpu.CompilerParams(
            collective_id=0, has_side_effects=True, vmem_limit_bytes=60 << 20
        ),
        name="layer",
    )(
        hidden_in, gate_proj, inner_proj, small_proj, conv_inner, conv_shared, bias_inner, norm_gain, params,
        out_proj.T, prompt_lengths, group_map, page_table, init_states.reshape(4, 24 * HEAD, N),
    )
    return (mixed, pages.reshape(2, 24, HEAD, N))


def solution(mesh):
    fine = Mesh(mesh.devices.reshape(4, 4, 4, 2), ("z", "x", "y", "tp"))
    seq = ("z", "x", "y")
    every = ("z", "x", "y", "tp")
    placed = (
        P(seq, None),
        P(every, None),
        P(every, None),
        P(every, None),
        P(),
        P(None, "tp"),
        P(),
        P("tp"),
        P(),
        P("tp"),
        P("tp"),
        P("tp"),
        P("tp"),
        P("tp", seq),
        P(),
        P(),
        P(None, "tp", None, None),
        P(seq),
    )
    return jax.shard_map(
        on_device,
        mesh=fine,
        in_specs=placed,
        out_specs=(P(every, None), P(seq, "tp", None, None)),
        check_vma=False,
    )
```

```python
from types import SimpleNamespace

import jax
import jax.numpy as jnp
from jax import lax
from jax.experimental import pallas as pl
from jax.experimental.pallas import tpu as pltpu
from jax.sharding import Mesh
from jax.sharding import PartitionSpec as P

N = 128
CONV = 4
PAGE = 128
DI = 3072
HEAD = 64
MINE = 6
CH = MINE * HEAD
EPS = 1e-05
BF = jnp.bfloat16
F32 = jnp.float32
NEG = -1e30


def dot(a, b):
    return jnp.dot(a, b, preferred_element_type=F32)


def dot_nt(a, b):
    return lax.dot_general(a, b, (((1,), (1,)), ((), ())), preferred_element_type=F32)


def dot_tn(a, b):
    return lax.dot_general(a, b, (((0,), (0,)), ((), ())), preferred_element_type=F32)


def silu(v):
    return v / (1.0 + jnp.exp(-v))


def softplus(v):
    return jnp.maximum(v, 0.0) + jnp.log1p(jnp.exp(-jnp.abs(v)))


def three(v):
    hi = v.astype(BF)
    rest = v - hi.astype(F32)
    mid = rest.astype(BF)
    return hi, mid, (rest - mid.astype(F32)).astype(BF)


def expand(v, hot):
    hi = v.astype(BF)
    lo = (v - hi.astype(F32)).astype(BF)
    return dot(hi, hot) + dot(lo, hot)


def head_hot():
    row = lax.broadcasted_iota(jnp.int32, (128, CH), 0)
    col = lax.broadcasted_iota(jnp.int32, (128, CH), 1)
    return (row == col // HEAD).astype(F32).astype(BF)


def wide(m):
    return jnp.concatenate([m, m, m], axis=1)


class Copies:
    def __init__(self, send, recv):
        self.send, self.recv, self.open = send, recv, []

    def go(self, src, dst, slot, device):
        copy = pltpu.make_async_remote_copy(
            src_ref=src,
            dst_ref=dst,
            send_sem=self.send.at[slot],
            recv_sem=self.recv.at[slot],
            device_id=device,
            device_id_type=pl.DeviceIdType.MESH,
        )
        copy.start()
        self.open.append(copy)

    def arrived(self, dst, slot):
        pltpu.make_async_remote_copy(
            src_ref=dst,
            dst_ref=dst,
            send_sem=self.send.at[slot],
            recv_sem=self.recv.at[slot],
            device_id=self.me,
            device_id_type=pl.DeviceIdType.MESH,
        ).wait_recv()

    def close(self):
        for copy in self.open:
            copy.wait_send()


def coords():
    return (
        lax.axis_index("z"),
        lax.axis_index("x"),
        lax.axis_index("y"),
        lax.axis_index("tp"),
    )


class Plane:
    def __init__(self, out, copies, rows, relay):
        self.out, self.copies, self.half, self.relay = out, copies, rows // 2, relay
        z, x, y, c = coords()
        self.y, self.c = y, c
        self.a = x * (1 - c) + z * c
        self.b = z * (1 - c) + x * c

    def at(self, da, db):
        a = (self.a + da + 8) % 4
        b = (self.b + db + 8) % 4
        c = self.c
        return b * (1 - c) + a * c, a * (1 - c) + b * c

    def device(self, da, db):
        z, x = self.at(da, db)
        return (z, x, self.y, self.c)

    def full(self, d, db=0):
        z, x = self.at(-d, db)
        return self.out.at[z * 4 + x]

    def low(self, d, db):
        z, x = self.at(-d, db)
        return self.out.at[z * 4 + x, pl.ds(0, self.half)]

    def high(self, d, db):
        z, x = self.at(-d, db)
        return self.out.at[z * 4 + x, pl.ds(self.half, self.half)]

    def first(self, own):
        for d in (1, 3, 2):
            self.copies.go(own, self.full(0), d - 1, self.device(d, 0))
        self.second(0, own)

    def second(self, d, src=None):
        src = self.full(d) if src is None else src
        self.copies.go(src, self.full(d), 3 + 4 * d, self.device(0, 1))
        self.copies.go(src, self.full(d), 4 + 4 * d, self.device(0, -1))
        if d not in self.relay:
            self.copies.go(src, self.full(d), 5 + 4 * d, self.device(0, 2))

    def turn(self, d):
        self.copies.arrived(self.full(d), d - 1)
        self.second(d)

    def pass_on(self, d):
        self.copies.arrived(self.full(d, -1), 3 + 4 * d)
        if d in self.relay:
            self.copies.go(self.low(d, -1), self.low(d, -1), 5 + 4 * d, self.device(0, 1))
        self.copies.arrived(self.full(d, 1), 4 + 4 * d)
        if d in self.relay:
            self.copies.go(self.high(d, 1), self.high(d, 1), 6 + 4 * d, self.device(0, -1))

    def end(self, d):
        if d in self.relay:
            self.copies.arrived(self.low(d, 2), 5 + 4 * d)
            self.copies.arrived(self.high(d, 2), 6 + 4 * d)
        else:
            self.copies.arrived(self.full(d, 2), 5 + 4 * d)


def pack(width):
    row = lax.broadcasted_iota(jnp.int32, (96, 128), 0)
    col = lax.broadcasted_iota(jnp.int32, (96, 128), 1)
    padded = 128 // (96 // width)
    return (col == row // width * padded + row % width).astype(F32).astype(BF)


UNIT = 1024
COPY = dict(
    stage=7, ostage=3, hid=6, cross=4, w=19, edge=1, wo=19, bc=2,
    part=15, back=15, page=3, decay=3, mate=4, ring=6, sum=7, state=3,
)


def buffers(d):
    vmem = pltpu.VMEM
    return dict(
        hidden=vmem((128, d), BF),
        gate_w=vmem((12, DI), F32),
        inner_w=vmem((12, DI), F32),
        small_w=vmem((12, 304), F32),
        cinner=vmem((4, CH), F32),
        cshared=vmem((4, 2 * N), F32),
        binner=vmem((1, CH), F32),
        ngain=vmem((1, CH), F32),
        dtb=vmem((1, 24), F32),
        rates_log=vmem((1, 24), F32),
        skip=vmem((1, 24), F32),
        layout=vmem((1, 128), jnp.int32),
        bshared=vmem((1, 2 * N), F32),
        out_w=vmem((24, d), F32),
        lens=pltpu.SMEM((8,), jnp.int32),
        grps=pltpu.SMEM((8,), jnp.int32),
        pieces=vmem((8, 16, UNIT), BF),
        stage=vmem((8, 16, UNIT), BF),
        unit=vmem((96, UNIT), BF),
        half=vmem((128, d), BF),
        w=vmem((16, 96, UNIT), BF),
        hid=vmem((8, 128, d), BF),
        edge=vmem((16, d), BF),
        initf=vmem((4, CH, N), F32),
        initb=vmem((CH, 4 * N), BF),
        sg=vmem((1024, CH), F32),
        xs=vmem((1032, CH + 2 * N), F32),
        steps=vmem((1024, 128), BF),
        y=vmem((1024, CH), F32),
        xdt=vmem((1024, CH), BF),
        b=vmem((1024, N), BF),
        c=vmem((1024, N), BF),
        cum=vmem((1024, 128), F32),
        fx=vmem((1024, CH), F32),
        fac=vmem((1024, 128), F32),
        small=vmem((9, CH, N), BF),
        dps=vmem((8, 8, N), F32),
        carries=vmem((4, CH, N), BF),
        pages=vmem((4, 2, CH, N), BF),
        rates=vmem((4, 2, 8, N), F32),
        bc=vmem((2, 1040, N), BF),
        state=vmem((16, 4, 8, N), F32),
        parts=vmem((16, 4, 8, N), F32),
        befores=vmem((16, 3, 8, N), F32),
        carry=vmem((16, 3, 8, N), F32),
        outp=vmem((4, 32, CH), BF),
        ostage=vmem((4, 32, CH), BF),
        ounit=vmem((96, CH), BF),
        wo=vmem((16, 96, CH), BF),
        opp=vmem((128, d), BF),
        ahead=vmem((128, d), BF),
        behind=vmem((128, d), BF),
        own=vmem((128, d), BF),
        xs_out=vmem((4, 128, d), BF),
        xs_in=vmem((4, 128, d), BF),
        low=vmem((64, d), BF),
        high=vmem((64, d), BF),
        from_l=vmem((128, d), BF),
        from_r=vmem((128, d), BF),
        sq=vmem((8, 8, 128), F32),
        sqr=vmem((8, 8, 128), F32),
        snaps=vmem((2, 4, CH, N), F32),
        res=vmem((128, d), F32),
    )


def layer_kernel(
    hidden_h, gate_h, inner_h, small_h, cinner_h, cshared_h, binner_h, ngain_h, out_h,
    dtb_h, rates_h, skip_h, layout_h, bshared_h,
    lens_h, grps_h, init, out_o, page_o, *refs,
):
    d = hidden_h.shape[1]
    names = list(buffers(d))
    r = SimpleNamespace(**dict(zip(names, refs)))
    sems = refs[len(names):]
    z, x, y, c = coords()
    me_not = (z, x, y, 1 - c)
    cp = SimpleNamespace()
    for i, name in enumerate(COPY):
        setattr(cp, name, Copies(sems[2 * i], sems[2 * i + 1]))
        getattr(cp, name).me = me_not
    local = sems[2 * len(COPY)]
    q = y * 2 + c
    g = z * 4 + x
    mate = me_not
    right, left = (z, x, (y + 1) % 4, c), (z, x, (y + 3) % 4, c)
    near = [(z, x, (y + k) % 4, c) for k in range(1, 4)]
    group = [(z, x, ((q + k) % 8) // 2, (q + k) % 2) for k in range(1, 8)]
    peers = [(((g + k) % 16) // 4, ((g + k) % 16) % 4, y, c) for k in range(1, 16)]
    next_dev = peers[0]
    barrier = pltpu.get_barrier_semaphore()
    for device in group + peers:
        pl.semaphore_signal(
            barrier, inc=1, device_id=device, device_id_type=pl.DeviceIdType.MESH
        )

    mychan = pl.ds(pl.multiple_of(y * CH, CH), CH)
    loads = dict(
        gate_w=gate_h,
        inner_w=inner_h,
        small_w=small_h,
        hidden=hidden_h.at[pl.ds(pl.multiple_of(c * 128, 128), 128)],
        out_w=out_h,
        dtb=dtb_h,
        rates_log=rates_h,
        skip=skip_h,
        layout=layout_h,
        bshared=bshared_h,
        binner=binner_h.at[mychan],
        ngain=ngain_h.at[mychan],
        cinner=cinner_h.at[:, mychan],
        cshared=cshared_h,
        lens=lens_h,
        grps=grps_h,
        initf=init.at[:, mychan],
    )
    load = SimpleNamespace()
    for i, name in enumerate(loads):
        to = getattr(r, name)
        if loads[name].ndim == 1 and to.shape[0] == 1:
            to = to.at[0]
        setattr(load, name, pltpu.make_async_copy(loads[name], to, local.at[2 + i]))
        getattr(load, name).start()
    gate_w, inner_w, small_w, hidden = r.gate_w, r.inner_w, r.small_w, r.hidden
    cinner, cshared = r.cinner, r.cshared
    lens, grps, outp = r.lens, r.grps, r.outp
    pieces, stage = r.pieces, r.stage
    outp[...] = jnp.zeros_like(outp)
    pieces[...] = jnp.zeros_like(pieces)
    for one in (load.gate_w, load.inner_w, load.small_w, load.out_w):
        one.wait()
    for t in range(4):
        outp[t, 0:24, :] = r.out_w[:, t * CH : t * CH + CH].astype(BF)
    for t in range(8):
        a = 1536 * (t % 2) + CH * (t // 2)
        pieces[t, 0:12, 0:CH] = gate_w[:, a : a + CH].astype(BF)
        pieces[t, 0:12, CH : 2 * CH] = inner_w[:, a : a + CH].astype(BF)
        b = N * (t % 2)
        pieces[t, 0:12, 2 * CH : 2 * CH + N] = small_w[:, b : b + N].astype(BF)
        pieces[t, 0:12, 2 * CH + N : 2 * CH + N + 48] = small_w[:, 2 * N :].astype(BF)
    half = r.half
    load.layout.wait()
    load.hidden.wait()
    lay = jnp.broadcast_to(r.layout[...], (8, 128)).astype(F32).astype(BF)
    rows = hidden[...]
    for j in range(0, d, CH):
        brow = lax.broadcasted_iota(jnp.int32, (128, CH), 0)
        bcol = lax.broadcasted_iota(jnp.int32, (128, CH), 1) + j
        block = dot(lay, (brow == bcol // 12).astype(F32).astype(BF))[0:1]
        want = block * 12.0 + (bcol[0:1] % 12).astype(F32)
        frow = lax.broadcasted_iota(jnp.int32, (d, CH), 0).astype(F32)
        pick = jnp.where(frow == want, 1.0, 0.0).astype(BF)
        half[:, j : j + CH] = dot(rows, pick).astype(BF)
    pl.semaphore_wait(barrier, len(group) + len(peers))

    for k in range(1, 8):
        cp.stage.go(pieces.at[(q + k) % 8], stage.at[q], k - 1, group[k - 1])
    stage[q] = pieces[q]
    r.ostage[y] = outp[y]

    hid = r.hid

    def hslot(dy, core):
        return ((y + dy + 4) % 4) * 2 + core

    def hpart(dy, low):
        return hid.at[hslot(dy, c), pl.ds(0 if low else 64, 64)]

    lo, hi = pl.ds(0, 64), pl.ds(64, 64)
    cp.hid.go(half.at[lo], hpart(0, True), 0, right)
    cp.hid.go(half.at[hi], hpart(0, False), 2, left)
    cp.hid.go(half.at[hi], hpart(0, False), 1, right)
    cp.hid.go(half.at[lo], hpart(0, True), 3, left)
    cp.cross.go(half, hid.at[hslot(0, c)], 0, mate)
    hid[q] = half[...]

    for k in range(1, 8):
        cp.stage.arrived(stage.at[(q + 8 - k) % 8], k - 1)
    packer = pack(12)
    for j in range(0, UNIT, 512):
        r.unit[:, j : j + 512] = dot(
            packer, stage[:, :, j : j + 512].reshape(128, 512)
        ).astype(BF)
    ring = Plane(r.w, cp.w, 96, (0, 1, 3))
    ring.first(r.unit)
    mine = pltpu.make_async_copy(r.unit, r.w.at[g], local.at[1])
    mine.start()
    for one in (load.dtb, load.rates_log, load.skip, load.bshared):
        one.wait()
    for one in (load.initf, load.cinner, load.cshared, load.binner, load.ngain, load.lens, load.grps):
        one.wait()
    for k in range(4):
        r.initb[:, k * N : k * N + N] = r.initf[k].astype(BF)

    cp.hid.arrived(hpart(-1, True), 0)
    cp.hid.go(hpart(-1, True), hpart(-1, True), 4, right)
    cp.hid.arrived(hpart(1, False), 2)
    cp.hid.go(hpart(1, False), hpart(1, False), 5, left)
    for k in range(1, 4):
        cp.ostage.go(outp.at[(y + k) % 4], r.ostage.at[y], k - 1, near[k - 1])
    ring.turn(1)
    ring.turn(3)
    ring.turn(2)
    ring.pass_on(0)
    cp.hid.arrived(hpart(-1, False), 1)
    cp.cross.go(hid.at[hslot(-1, c)], hid.at[hslot(-1, c)], 1, mate)
    cp.hid.arrived(hpart(1, True), 3)
    cp.cross.go(hid.at[hslot(1, c)], hid.at[hslot(1, c)], 2, mate)
    ring.pass_on(1)
    ring.pass_on(3)
    oring = Plane(r.wo, cp.wo, 96, ())
    cp.hid.arrived(hpart(2, True), 4)
    cp.hid.arrived(hpart(2, False), 5)
    cp.cross.go(hid.at[hslot(2, c)], hid.at[hslot(2, c)], 3, mate)
    for k, dy in enumerate((0, -1, 1, 2)):
        cp.cross.arrived(hid.at[hslot(dy, 1 - c)], k)
    cp.edge.go(hid.at[7, pl.ds(112, 16)], r.edge, 0, next_dev)
    for k in range(1, 4):
        cp.ostage.arrived(r.ostage.at[(y + 4 - k) % 4], k - 1)
    r.ounit[...] = dot(pack(24), r.ostage[...].reshape(128, CH)).astype(BF)
    ring.pass_on(2)
    for k in range(4):
        ring.end(k)
    mine.wait()
    oring.first(r.ounit)
    mine = pltpu.make_async_copy(r.ounit, r.wo.at[g], local.at[1])
    mine.start()

    w, xs, bc, steps, sg = r.w, r.xs, r.bc, r.steps, r.sg

    def columns(a, z):
        return w[:, :, a:z].reshape(d, z - a)

    def project_bc(i, _):
        at = pl.multiple_of(i * 256, 256)
        got = dot(hid[pl.ds(i * 2, 2)].reshape(256, d), columns(2 * CH, UNIT)).astype(BF)
        bc[c, pl.ds(pl.multiple_of(at + 16, 16), 256), :] = got[:, :N]
        steps[pl.ds(at, 256), :] = got[:, N:]
        return 0

    lax.fori_loop(0, 4, project_bc, 0)
    mid = pl.ds(16, 1024)
    cp.bc.go(bc.at[c, mid], bc.at[c, mid], 0, mate)

    def project(i, _):
        at = pl.multiple_of(i * 256, 256)
        got = dot(hid[pl.ds(i * 2, 2)].reshape(256, d), columns(0, 2 * CH)).astype(BF)
        sg[pl.ds(at, 256), :] = got[:, :CH].astype(F32)
        xs[pl.ds(pl.multiple_of(at + 8, 8), 256), 0:CH] = got[:, CH:].astype(F32)
        return 0

    lax.fori_loop(0, 2, project, 0)
    cp.edge.arrived(r.edge, 0)
    bc[c, 0:16, :] = dot(r.edge[...], columns(2 * CH, 2 * CH + N)).astype(BF)
    cp.bc.go(bc.at[c, pl.ds(0, 16)], bc.at[c, pl.ds(0, 16)], 1, mate)
    xs[0:8, 0:CH] = dot(r.edge[...], columns(CH, 2 * CH))[8:16].astype(BF).astype(F32)
    lax.fori_loop(2, 4, project, 0)
    for k in (1, 3, 2):
        oring.turn(k)
    cp.bc.arrived(bc.at[1 - c, mid], 0)
    cp.bc.arrived(bc.at[1 - c, pl.ds(0, 16)], 1)
    for k in range(2):
        xs[0:8, CH + k * N : CH + k * N + N] = bc[k, 0:16, :].astype(F32)[8:16]
        xs[8:1032, CH + k * N : CH + k * N + N] = bc[k, 16:1040, :].astype(F32)

    hot = head_hot()
    starts = []
    total = jnp.int32(0)
    for k in range(8):
        starts.append(total)
        total = total + lens[k]
    row = lax.broadcasted_iota(jnp.int32, (128, 128), 0)
    col = lax.broadcasted_iota(jnp.int32, (128, 128), 1)
    head0 = c * 24 + y * MINE
    pick = jnp.where(col < MINE, (row == col + head0).astype(F32), 0.0).astype(BF)
    wrow = lax.broadcasted_iota(jnp.int32, (128, CH), 0)
    wcol = lax.broadcasted_iota(jnp.int32, (128, CH), 1)
    pickx = (wrow == wcol // HEAD + head0).astype(F32).astype(BF)

    def take(ref):
        at = jnp.where(col < MINE, (row == col + y * MINE).astype(F32), 0.0).astype(BF)[0:32]
        wide_v = jnp.concatenate([jnp.broadcast_to(ref[...], (8, 24)), jnp.zeros((8, 8), F32)], axis=1)
        return sum(dot(part, at) for part in three(wide_v))[0:1]

    def takex(ref):
        at = (wrow == wcol // HEAD + y * MINE).astype(F32).astype(BF)[0:32]
        wide_v = jnp.concatenate([jnp.broadcast_to(ref[...], (8, 24)), jnp.zeros((8, 8), F32)], axis=1)
        return sum(dot(part, at) for part in three(wide_v))[0:1]

    rate6 = jnp.where(col[0:1] < MINE, -jnp.exp(take(r.rates_log)), 0.0)
    bias6, biasx, skipx = take(r.dtb), takex(r.dtb), takex(r.skip)
    taps = cinner[...]
    biasc = r.binner[...]
    small, dps = r.small, r.dps
    small[0] = jnp.zeros((CH, N), BF)

    def find(pos):
        first = jnp.zeros(pos.shape, jnp.int32)
        for k in range(1, 8):
            first = jnp.where(pos >= starts[k], starts[k], first)
        return first

    def advance(i, held):
        old, dp, dprow = held
        at = pl.multiple_of(i * 256, 256)
        base = g * 1024 + i * 256
        first = find(base + lax.broadcasted_iota(jnp.int32, (256, 128), 0))
        off = base + lax.broadcasted_iota(jnp.int32, (256, 128), 0) - first
        xc = biasc + jnp.zeros((256, CH), F32)
        bv = r.bshared[:, :N] + jnp.zeros((256, N), F32)
        window = xs[pl.ds(at, 264), : CH + N]
        for lag in range(CONV):
            ok = (off >= lag).astype(F32)
            part = window[8 - lag : 264 - lag, :]
            xc = xc + taps[lag : lag + 1, :] * part[:, :CH] * wide(ok)
            bv = bv + cshared[lag : lag + 1, :N] * part[:, CH : CH + N] * ok
        xc = silu(xc)
        b_all = silu(bv).astype(BF)
        r.b[pl.ds(at, 256), :] = b_all
        step = steps[pl.ds(at, 256), :]
        dt6 = softplus(dot(step, pick) + bias6)
        log6 = rate6 * dt6
        dtx = softplus(dot(step, pickx) + biasx)
        xdt_all = xc * dtx
        r.xdt[pl.ds(at, 256), :] = xdt_all.astype(BF)
        r.y[pl.ds(at, 256), :] = skipx * xc
        for sub in range(2):
            k = i * 2 + sub
            p0 = base + sub * 128
            rows = slice(sub * 128, sub * 128 + 128)
            f0 = first[rows, :]
            mask = (row >= col) & (f0 == find(p0 + col))
            maskb = mask.astype(F32).astype(BF)
            cum = sum(dot(maskb, part) for part in three(log6[rows, :]))
            there = pl.ds(pl.multiple_of(at + sub * 128, 128), 128)
            r.cum[there, :] = cum
            cumt = cum.T
            flast = jnp.int32(0)
            glast = grps[0]
            for j in range(1, 8):
                got = p0 + 127 >= starts[j]
                flast = jnp.where(got, starts[j], flast)
                glast = jnp.where(got, grps[j], glast)
            w6 = jnp.exp(jnp.where(f0 == flast, cum[127:128, :] - cum, NEG))
            xw = (xdt_all[rows, :] * expand(w6, hot)).astype(BF)
            summary = dot_tn(xw, b_all[rows, :])
            keep = (flast < p0).astype(F32)
            ecum = jnp.exp(cum)
            r.fac[there, :] = jnp.where(f0 < p0, ecum, 0.0) * dprow
            scale = jnp.exp(jnp.broadcast_to(cumt[0:8, 127:128], (8, 128)))
            dp = dp * scale * keep
            dprow = dprow * jnp.exp(cum[127:128, :]) * keep
            dps[k] = dp
            start = r.initf[0]
            for j in range(1, 4):
                start = jnp.where(glast == j, r.initf[j], start)
            old = jnp.where(flast < p0, old, start)
            old = jnp.concatenate(
                [scale[h : h + 1, :] * old[h * HEAD : h * HEAD + HEAD, :] for h in range(MINE)], axis=0
            ) + summary
            small[k + 1] = old.astype(BF)
        return old, dp, dprow

    held = (jnp.zeros((CH, N), F32), jnp.ones((8, 128), F32), jnp.ones((1, 128), F32))
    last, dplast, _ = lax.fori_loop(0, 4, advance, held)

    state, parts, befores, carry = r.state, r.parts, r.befores, r.carry
    for j in range(3):
        state[:, j] = last[j * 128 : j * 128 + 128].reshape(16, 8, N)
    state[:, 3] = jnp.broadcast_to(dplast[None], (16, 8, N))
    for k in range(1, 16):
        cp.part.go(state.at[(g + k) % 16], parts.at[g], k - 1, peers[k - 1])
    parts[g] = state[g]
    for k in range(1, 4):
        t = (y + k) % 4
        cp.page.go(small.at[pl.ds(t * 2 + 1, 2)], r.pages.at[y], k - 1, near[k - 1])
        cp.decay.go(dps.at[pl.ds(t * 2, 2)], r.rates.at[y], k - 1, near[k - 1])
    for k in range(2):
        r.pages[y, k] = small[y * 2 + 1 + k]
        r.rates[y, k] = dps[y * 2 + k]

    def inside(i, _):
        first_at = pl.multiple_of(i * 256, 256)
        pos = g * 1024 + i * 256 + lax.broadcasted_iota(jnp.int32, (256, 128), 0)
        off = pos - find(pos)
        cv = r.bshared[:, N:] + jnp.zeros((256, N), F32)
        window = xs[pl.ds(first_at, 264), CH + N :]
        for lag in range(CONV):
            ok = (off >= lag).astype(F32)
            cv = cv + cshared[lag : lag + 1, N:] * window[8 - lag : 264 - lag, :] * ok
        c_all = silu(cv).astype(BF)
        r.c[pl.ds(first_at, 256), :] = c_all
        for sub in range(2):
            k = i * 2 + sub
            p0 = g * 1024 + k * 128
            at = pl.ds(pl.multiple_of(k * 128, 128), 128)
            f0 = find(p0 + row)
            mask = (row >= col) & (f0 == find(p0 + col))
            cum = r.cum[at, :]
            cumt = cum.T
            cb = c_all[sub * 128 : sub * 128 + 128, :]
            r.fx[at, :] = expand(r.fac[at, :], hot)
            cf = cb.astype(F32)
            scores = dot_nt(cb, r.b[at, :])
            gid = jnp.zeros((128, 128), jnp.int32) + grps[0]
            for j in range(1, 8):
                gid = jnp.where(p0 + row >= starts[j], grps[j], gid)
            gid = jnp.where(f0 < p0, 4, gid)
            chot = jnp.concatenate(
                [jnp.where(gid == j, cf, 0.0).astype(BF) for j in range(4)], axis=1
            )
            read = dot_nt(jnp.where(gid == 4, cf, 0.0).astype(BF), small[k])
            read = read + dot_nt(chot, r.initb[...])
            lane = col
            pieces = []
            for pair in range(3):
                xp = r.xdt[at, pair * 128 : pair * 128 + 128]
                got = []
                for h in (2 * pair, 2 * pair + 1):
                    diff = cum[:, h : h + 1] - cumt[h : h + 1, :]
                    mix = jnp.exp(jnp.where(mask, diff, NEG)) * scores
                    got.append(dot(mix.astype(BF), xp))
                pieces.append(jnp.where(lane < HEAD, got[0], got[1]))
            r.y[at, :] = (
                r.y[at, :] + expand(jnp.exp(cum), hot) * read + jnp.concatenate(pieces, axis=1)
            )
            sg[at, :] = silu(sg[at, :])
        return 0

    lax.fori_loop(0, 2, inside, 0)
    for k in range(1, 16):
        cp.part.arrived(parts.at[(g + 16 - k) % 16], k - 1)
    hb = g // 8
    run = [jnp.zeros((8, 128), F32) for _ in range(3)]
    for k in range(16):
        for j in range(3):
            befores[k, j] = run[j]
            run[j] = parts[k, 3, pl.ds(hb + 2 * j, 1), :] * run[j] + parts[k, j]
    for k in range(1, 16):
        cp.back.go(befores.at[(g + k) % 16], carry.at[g], k - 1, peers[k - 1])
    carry[g] = befores[g]
    lax.fori_loop(2, 4, inside, 0)
    for k in range(4):
        oring.pass_on(k)
        oring.end(k)
    mine.wait()
    for k in range(1, 16):
        cp.back.arrived(carry.at[(g + 16 - k) % 16], k - 1)

    carries = r.carries
    cs = jnp.concatenate([carry[:, j].reshape(128, N) for j in range(3)], axis=0).astype(BF)
    carries[y] = cs
    for k in range(1, 4):
        cp.state.go(carries.at[y], carries.at[y], k - 1, near[k - 1])
    ones = jnp.ones((8, CH), BF)
    gain = r.ngain[...]
    xs_out, xs_in, sq, sqr = r.xs_out, r.xs_in, r.sq, r.sqr

    def partial(dy, k, keep):
        t = (y + dy) % 4
        for part in range(2):
            core = c if part else 1 - c
            at = pl.ds(pl.multiple_of(t * 256 + core * 128, 128), 128)
            full = r.y[at, :] + r.fx[at, :] * dot_nt(r.c[at, :], cs)
            gv = full * sg[at, :]
            g2 = gv * gv
            top = g2.astype(BF)
            rest = (g2 - top.astype(F32)).astype(BF)
            sq[t * 2 + core] = dot_nt(ones, top) + dot_nt(ones, rest)
            gg = (gv * gain).astype(BF)
            for n in range(0, 1536, CH):
                got = dot_nt(gg, r.wo[n // 96 : n // 96 + 4].reshape(CH, CH)).astype(BF)
                if part:
                    keep[:, n : n + CH] = got
                else:
                    xs_out[k, :, n : n + CH] = got
            if not part:
                cp.mate.go(xs_out.at[k], xs_in.at[k], k, mate)

    def join(k, keep):
        cp.mate.arrived(xs_in.at[k], k)
        keep[...] = (keep[...].astype(F32) + xs_in[k].astype(F32)).astype(BF)

    opp, ahead, behind, own = r.opp, r.ahead, r.behind, r.own
    from_l, from_r = r.from_l, r.from_r
    partial(2, 0, opp)
    partial(1, 1, ahead)
    join(0, opp)
    cp.ring.go(opp.at[lo], r.low, 0, right)
    cp.ring.go(opp.at[hi], r.high, 1, left)
    partial(3, 2, behind)
    join(1, ahead)
    cp.ring.go(ahead.at[hi], from_l.at[hi], 2, right)
    join(2, behind)
    cp.ring.go(behind.at[lo], from_r.at[lo], 3, left)
    cp.ring.arrived(r.low, 0)
    ahead[0:64, :] = (ahead[0:64, :].astype(F32) + r.low[...].astype(F32)).astype(BF)
    cp.ring.go(ahead.at[lo], from_l.at[lo], 4, right)
    cp.ring.arrived(r.high, 1)
    behind[64:128, :] = (behind[64:128, :].astype(F32) + r.high[...].astype(F32)).astype(BF)
    cp.ring.go(behind.at[hi], from_r.at[hi], 5, left)
    partial(0, 3, own)
    for k in range(1, 8):
        cp.sum.go(sq.at[(q + k) % 8], sqr.at[q], k - 1, group[k - 1])
    sqr[q] = sq[q]
    join(3, own)

    for k in range(4):
        t = (y + 4 - k) % 4
        if k:
            cp.state.arrived(carries.at[t], k - 1)
            cp.page.arrived(r.pages.at[t], k - 1)
            cp.decay.arrived(r.rates.at[t], k - 1)
        for h in range(MINE):
            at = slice(h * HEAD, h * HEAD + HEAD)
            into = carries[t, at, :].astype(F32)
            one, two = (
                r.pages[t, j, at, :].astype(F32) + r.rates[t, j, h : h + 1, :] * into
                for j in range(2)
            )
            r.snaps[0, t, at, :] = one
            r.snaps[1, t, at, :] = two

    snaps = pltpu.make_async_copy(r.snaps, page_o, local.at[0])
    snaps.start()

    for k in range(1, 8):
        cp.sum.arrived(sqr.at[(q + 8 - k) % 8], k - 1)
    total = sqr[0]
    for k in range(1, 8):
        total = total + sqr[k]
    scale = lax.rsqrt(total / DI + EPS)
    scale = jnp.broadcast_to(scale[0:1, :], (128, 128)).T
    cp.ring.arrived(from_l.at[hi], 2)
    cp.ring.arrived(from_r.at[lo], 3)
    cp.ring.arrived(from_l.at[lo], 4)
    cp.ring.arrived(from_r.at[hi], 5)
    for n in range(0, 1536, 128):
        cols = slice(n, n + 128)
        r.res[:, cols] = sum(v[:, cols].astype(F32) for v in (own, from_l, from_r)) * scale
    res = pltpu.make_async_copy(r.res, out_o, local.at[21])
    res.start()
    for part in vars(cp).values():
        part.close()
    for one in (snaps, res):
        one.wait()


def on_device(
    hidden_in, gate_proj, inner_proj, small_proj, row_layout, conv_inner, conv_shared,
    bias_inner, bias_shared, dt_bias, decay_log, skip_gain, norm_gain, out_proj,
    prompt_lengths, group_map, init_states, page_table,
):
    d = hidden_in.shape[1]
    hbm = pl.BlockSpec(memory_space=pltpu.HBM)
    dma = pltpu.SemaphoreType.DMA
    scratch = list(buffers(d).values())
    for count in COPY.values():
        scratch += [dma((count,)), dma((count,))]
    mixed, pages = pl.pallas_call(
        layer_kernel,
        in_specs=[hbm] * 17,
        out_specs=[hbm, hbm],
        out_shape=[
            jax.ShapeDtypeStruct((128, d), F32),
            jax.ShapeDtypeStruct((2, 4, CH, N), F32),
        ],
        scratch_shapes=scratch + [dma((22,))],
        compiler_params=pltpu.CompilerParams(
            collective_id=0, has_side_effects=True, vmem_limit_bytes=60 << 20
        ),
        name="layer",
    )(
        hidden_in, gate_proj, inner_proj, small_proj, conv_inner, conv_shared, bias_inner, norm_gain, out_proj.T,
        dt_bias, decay_log, skip_gain, row_layout, bias_shared, prompt_lengths, group_map, init_states.reshape(4, 24 * HEAD, N),
    )
    mixed = mixed.astype(BF)
    seq = (lax.axis_index("z") * 4 + lax.axis_index("x")) * 4 + lax.axis_index("y")
    pages = pages.reshape(2, 24, HEAD, N)
    return (mixed, jnp.where(page_table[0] == seq * 2, pages, pages[::-1]))


def solution(mesh):
    fine = Mesh(mesh.devices.reshape(4, 4, 4, 2), ("z", "x", "y", "tp"))
    seq = ("z", "x", "y")
    every = ("z", "x", "y", "tp")
    placed = (
        P(seq, None),
        P(every, None),
        P(every, None),
        P(every, None),
        P(),
        P(None, "tp"),
        P(),
        P("tp"),
        P(),
        P("tp"),
        P("tp"),
        P("tp"),
        P("tp"),
        P("tp", seq),
        P(),
        P(),
        P(None, "tp", None, None),
        P(seq),
    )
    return jax.shard_map(
        on_device,
        mesh=fine,
        in_specs=placed,
        out_specs=(P(every, None), P(seq, "tp", None, None)),
        check_vma=False,
    )
```

```python
from types import SimpleNamespace

import jax
import jax.numpy as jnp
from jax import lax
from jax.experimental import pallas as pl
from jax.experimental.pallas import tpu as pltpu
from jax.sharding import Mesh
from jax.sharding import PartitionSpec as P

N = 128
CONV = 4
PAGE = 128
DI = 3072
HEAD = 64
MINE = 6
CH = MINE * HEAD
EPS = 1e-05
BF = jnp.bfloat16
F32 = jnp.float32
NEG = -1e30


def dot(a, b):
    return jnp.dot(a, b, preferred_element_type=F32)


def dot_nt(a, b):
    return lax.dot_general(a, b, (((1,), (1,)), ((), ())), preferred_element_type=F32)


def dot_tn(a, b):
    return lax.dot_general(a, b, (((0,), (0,)), ((), ())), preferred_element_type=F32)


def silu(v):
    return v / (1.0 + jnp.exp(-v))


def softplus(v):
    return jnp.maximum(v, 0.0) + jnp.log1p(jnp.exp(-jnp.abs(v)))


def three(v):
    hi = v.astype(BF)
    rest = v - hi.astype(F32)
    mid = rest.astype(BF)
    return hi, mid, (rest - mid.astype(F32)).astype(BF)


def expand(v, hot):
    hi = v.astype(BF)
    lo = (v - hi.astype(F32)).astype(BF)
    return dot(hi, hot) + dot(lo, hot)


def head_hot():
    row = lax.broadcasted_iota(jnp.int32, (128, CH), 0)
    col = lax.broadcasted_iota(jnp.int32, (128, CH), 1)
    return (row == col // HEAD).astype(F32).astype(BF)


def wide(m):
    return jnp.concatenate([m, m, m], axis=1)


class Copies:
    def __init__(self, send, recv):
        self.send, self.recv, self.open = send, recv, []

    def go(self, src, dst, slot, device):
        copy = pltpu.make_async_remote_copy(
            src_ref=src,
            dst_ref=dst,
            send_sem=self.send.at[slot],
            recv_sem=self.recv.at[slot],
            device_id=device,
            device_id_type=pl.DeviceIdType.MESH,
        )
        copy.start()
        self.open.append(copy)

    def arrived(self, dst, slot):
        pltpu.make_async_remote_copy(
            src_ref=dst,
            dst_ref=dst,
            send_sem=self.send.at[slot],
            recv_sem=self.recv.at[slot],
            device_id=self.me,
            device_id_type=pl.DeviceIdType.MESH,
        ).wait_recv()

    def close(self):
        for copy in self.open:
            copy.wait_send()


def coords():
    return (
        lax.axis_index("z"),
        lax.axis_index("x"),
        lax.axis_index("y"),
        lax.axis_index("tp"),
    )


class Plane:
    def __init__(self, out, copies, rows, relay):
        self.out, self.copies, self.half, self.relay = out, copies, rows // 2, relay
        z, x, y, c = coords()
        self.y, self.c = y, c
        self.a = x * (1 - c) + z * c
        self.b = z * (1 - c) + x * c

    def at(self, da, db):
        a = (self.a + da + 8) % 4
        b = (self.b + db + 8) % 4
        c = self.c
        return b * (1 - c) + a * c, a * (1 - c) + b * c

    def device(self, da, db):
        z, x = self.at(da, db)
        return (z, x, self.y, self.c)

    def full(self, d, db=0):
        z, x = self.at(-d, db)
        return self.out.at[z * 4 + x]

    def low(self, d, db):
        z, x = self.at(-d, db)
        return self.out.at[z * 4 + x, pl.ds(0, self.half)]

    def high(self, d, db):
        z, x = self.at(-d, db)
        return self.out.at[z * 4 + x, pl.ds(self.half, self.half)]

    def first(self, own):
        for d in (1, 3, 2):
            self.copies.go(own, self.full(0), d - 1, self.device(d, 0))
        self.second(0, own)

    def second(self, d, src=None):
        src = self.full(d) if src is None else src
        self.copies.go(src, self.full(d), 3 + 4 * d, self.device(0, 1))
        self.copies.go(src, self.full(d), 4 + 4 * d, self.device(0, -1))
        if d not in self.relay:
            self.copies.go(src, self.full(d), 5 + 4 * d, self.device(0, 2))

    def turn(self, d):
        self.copies.arrived(self.full(d), d - 1)
        self.second(d)

    def pass_on(self, d):
        self.copies.arrived(self.full(d, -1), 3 + 4 * d)
        if d in self.relay:
            self.copies.go(self.low(d, -1), self.low(d, -1), 5 + 4 * d, self.device(0, 1))
        self.copies.arrived(self.full(d, 1), 4 + 4 * d)
        if d in self.relay:
            self.copies.go(self.high(d, 1), self.high(d, 1), 6 + 4 * d, self.device(0, -1))

    def end(self, d):
        if d in self.relay:
            self.copies.arrived(self.low(d, 2), 5 + 4 * d)
            self.copies.arrived(self.high(d, 2), 6 + 4 * d)
        else:
            self.copies.arrived(self.full(d, 2), 5 + 4 * d)


def pack(width):
    row = lax.broadcasted_iota(jnp.int32, (96, 128), 0)
    col = lax.broadcasted_iota(jnp.int32, (96, 128), 1)
    padded = 128 // (96 // width)
    return (col == row // width * padded + row % width).astype(F32).astype(BF)


UNIT = 1024
COPY = dict(
    stage=7, ostage=3, hid=6, cross=4, w=19, edge=1, wo=19, bc=2,
    part=15, back=15, page=3, decay=3, mate=4, ring=6, sum=7, state=3,
)


def buffers(d):
    vmem = pltpu.VMEM
    return dict(
        hidden=vmem((128, d), BF),
        gate_w=vmem((12, DI), F32),
        inner_w=vmem((12, DI), F32),
        small_w=vmem((12, 304), F32),
        cinner=vmem((4, CH), F32),
        cshared=vmem((4, 2 * N), F32),
        binner=vmem((1, CH), F32),
        ngain=vmem((1, CH), F32),
        dtb=vmem((1, 24), F32),
        rates_log=vmem((1, 24), F32),
        skip=vmem((1, 24), F32),
        layout=vmem((1, 128), jnp.int32),
        bshared=vmem((1, 2 * N), F32),
        out_w=vmem((24, d), F32),
        lens=pltpu.SMEM((8,), jnp.int32),
        grps=pltpu.SMEM((8,), jnp.int32),
        pt=pltpu.SMEM((2,), jnp.int32),
        pieces=vmem((8, 16, UNIT), BF),
        stage=vmem((8, 16, UNIT), BF),
        unit=vmem((96, UNIT), BF),
        half=vmem((128, d), BF),
        w=vmem((16, 96, UNIT), BF),
        hid=vmem((8, 128, d), BF),
        edge=vmem((16, d), BF),
        initf=vmem((4, CH, N), F32),
        initb=vmem((CH, 4 * N), BF),
        sg=vmem((1024, CH), F32),
        xs=vmem((1032, CH + 2 * N), F32),
        steps=vmem((1024, 128), BF),
        y=vmem((1024, CH), F32),
        xdt=vmem((1024, CH), BF),
        b=vmem((1024, N), BF),
        c=vmem((1024, N), BF),
        cum=vmem((1024, 128), F32),
        fx=vmem((1024, CH), F32),
        fac=vmem((1024, 128), F32),
        small=vmem((9, CH, N), BF),
        dps=vmem((8, 8, N), F32),
        carries=vmem((4, CH, N), BF),
        pages=vmem((4, 2, CH, N), BF),
        rates=vmem((4, 2, 8, N), F32),
        bc=vmem((2, 1040, N), BF),
        state=vmem((16, 4, 8, N), F32),
        parts=vmem((16, 4, 8, N), F32),
        befores=vmem((16, 3, 8, N), F32),
        carry=vmem((16, 3, 8, N), F32),
        outp=vmem((4, 32, CH), BF),
        ostage=vmem((4, 32, CH), BF),
        ounit=vmem((96, CH), BF),
        wo=vmem((16, 96, CH), BF),
        opp=vmem((128, d), BF),
        ahead=vmem((128, d), BF),
        behind=vmem((128, d), BF),
        own=vmem((128, d), BF),
        xs_out=vmem((4, 128, d), BF),
        xs_in=vmem((4, 128, d), BF),
        low=vmem((64, d), BF),
        high=vmem((64, d), BF),
        from_l=vmem((128, d), BF),
        from_r=vmem((128, d), BF),
        sq=vmem((8, 8, 128), F32),
        sqr=vmem((8, 8, 128), F32),
        snaps=vmem((2, 4, CH, N), F32),
        res=vmem((128, d), BF),
    )


def layer_kernel(
    hidden_h, gate_h, inner_h, small_h, cinner_h, cshared_h, binner_h, ngain_h, out_h,
    dtb_h, rates_h, skip_h, layout_h, bshared_h,
    lens_h, grps_h, pt_h, init, out_o, page_o, *refs,
):
    d = hidden_h.shape[1]
    names = list(buffers(d))
    r = SimpleNamespace(**dict(zip(names, refs)))
    sems = refs[len(names):]
    z, x, y, c = coords()
    me_not = (z, x, y, 1 - c)
    cp = SimpleNamespace()
    for i, name in enumerate(COPY):
        setattr(cp, name, Copies(sems[2 * i], sems[2 * i + 1]))
        getattr(cp, name).me = me_not
    local = sems[2 * len(COPY)]
    q = y * 2 + c
    g = z * 4 + x
    mate = me_not
    right, left = (z, x, (y + 1) % 4, c), (z, x, (y + 3) % 4, c)
    near = [(z, x, (y + k) % 4, c) for k in range(1, 4)]
    group = [(z, x, ((q + k) % 8) // 2, (q + k) % 2) for k in range(1, 8)]
    peers = [(((g + k) % 16) // 4, ((g + k) % 16) % 4, y, c) for k in range(1, 16)]
    next_dev = peers[0]
    barrier = pltpu.get_barrier_semaphore()
    for device in group + peers:
        pl.semaphore_signal(
            barrier, inc=1, device_id=device, device_id_type=pl.DeviceIdType.MESH
        )

    mychan = pl.ds(pl.multiple_of(y * CH, CH), CH)
    loads = dict(
        gate_w=gate_h,
        inner_w=inner_h,
        small_w=small_h,
        hidden=hidden_h.at[pl.ds(pl.multiple_of(c * 128, 128), 128)],
        out_w=out_h,
        dtb=dtb_h,
        rates_log=rates_h,
        skip=skip_h,
        layout=layout_h,
        bshared=bshared_h,
        binner=binner_h.at[mychan],
        ngain=ngain_h.at[mychan],
        cinner=cinner_h.at[:, mychan],
        cshared=cshared_h,
        lens=lens_h,
        grps=grps_h,
        pt=pt_h,
        initf=init.at[:, mychan],
    )
    load = SimpleNamespace()
    for i, name in enumerate(loads):
        to = getattr(r, name)
        if loads[name].ndim == 1 and to.shape[0] == 1:
            to = to.at[0]
        setattr(load, name, pltpu.make_async_copy(loads[name], to, local.at[2 + i]))
        getattr(load, name).start()
    gate_w, inner_w, small_w, hidden = r.gate_w, r.inner_w, r.small_w, r.hidden
    cinner, cshared = r.cinner, r.cshared
    lens, grps, outp = r.lens, r.grps, r.outp
    pieces, stage = r.pieces, r.stage
    outp[...] = jnp.zeros_like(outp)
    pieces[...] = jnp.zeros_like(pieces)
    for one in (load.gate_w, load.inner_w, load.small_w, load.out_w):
        one.wait()
    for t in range(4):
        outp[t, 0:24, :] = r.out_w[:, t * CH : t * CH + CH].astype(BF)
    for t in range(8):
        a = 1536 * (t % 2) + CH * (t // 2)
        pieces[t, 0:12, 0:CH] = gate_w[:, a : a + CH].astype(BF)
        pieces[t, 0:12, CH : 2 * CH] = inner_w[:, a : a + CH].astype(BF)
        b = N * (t % 2)
        pieces[t, 0:12, 2 * CH : 2 * CH + N] = small_w[:, b : b + N].astype(BF)
        pieces[t, 0:12, 2 * CH + N : 2 * CH + N + 48] = small_w[:, 2 * N :].astype(BF)
    half = r.half
    load.layout.wait()
    load.hidden.wait()
    lay = jnp.broadcast_to(r.layout[...], (8, 128)).astype(F32).astype(BF)
    rows = hidden[...]
    for j in range(0, d, CH):
        brow = lax.broadcasted_iota(jnp.int32, (128, CH), 0)
        bcol = lax.broadcasted_iota(jnp.int32, (128, CH), 1) + j
        block = dot(lay, (brow == bcol // 12).astype(F32).astype(BF))[0:1]
        want = block * 12.0 + (bcol[0:1] % 12).astype(F32)
        frow = lax.broadcasted_iota(jnp.int32, (d, CH), 0).astype(F32)
        pick = jnp.where(frow == want, 1.0, 0.0).astype(BF)
        half[:, j : j + CH] = dot(rows, pick).astype(BF)
    pl.semaphore_wait(barrier, len(group) + len(peers))

    for k in range(1, 8):
        cp.stage.go(pieces.at[(q + k) % 8], stage.at[q], k - 1, group[k - 1])
    stage[q] = pieces[q]
    r.ostage[y] = outp[y]

    hid = r.hid

    def hslot(dy, core):
        return ((y + dy + 4) % 4) * 2 + core

    def hpart(dy, low):
        return hid.at[hslot(dy, c), pl.ds(0 if low else 64, 64)]

    lo, hi = pl.ds(0, 64), pl.ds(64, 64)
    cp.hid.go(half.at[lo], hpart(0, True), 0, right)
    cp.hid.go(half.at[hi], hpart(0, False), 2, left)
    cp.hid.go(half.at[hi], hpart(0, False), 1, right)
    cp.hid.go(half.at[lo], hpart(0, True), 3, left)
    cp.cross.go(half, hid.at[hslot(0, c)], 0, mate)
    hid[q] = half[...]

    for k in range(1, 8):
        cp.stage.arrived(stage.at[(q + 8 - k) % 8], k - 1)
    packer = pack(12)
    for j in range(0, UNIT, 512):
        r.unit[:, j : j + 512] = dot(
            packer, stage[:, :, j : j + 512].reshape(128, 512)
        ).astype(BF)
    ring = Plane(r.w, cp.w, 96, (0, 1, 3))
    ring.first(r.unit)
    mine = pltpu.make_async_copy(r.unit, r.w.at[g], local.at[1])
    mine.start()
    for one in (load.dtb, load.rates_log, load.skip, load.bshared):
        one.wait()
    for one in (load.initf, load.cinner, load.cshared, load.binner, load.ngain, load.lens, load.grps, load.pt):
        one.wait()
    for k in range(4):
        r.initb[:, k * N : k * N + N] = r.initf[k].astype(BF)

    cp.hid.arrived(hpart(-1, True), 0)
    cp.hid.go(hpart(-1, True), hpart(-1, True), 4, right)
    cp.hid.arrived(hpart(1, False), 2)
    cp.hid.go(hpart(1, False), hpart(1, False), 5, left)
    for k in range(1, 4):
        cp.ostage.go(outp.at[(y + k) % 4], r.ostage.at[y], k - 1, near[k - 1])
    ring.turn(1)
    ring.turn(3)
    ring.turn(2)
    ring.pass_on(0)
    cp.hid.arrived(hpart(-1, False), 1)
    cp.cross.go(hid.at[hslot(-1, c)], hid.at[hslot(-1, c)], 1, mate)
    cp.hid.arrived(hpart(1, True), 3)
    cp.cross.go(hid.at[hslot(1, c)], hid.at[hslot(1, c)], 2, mate)
    ring.pass_on(1)
    ring.pass_on(3)
    oring = Plane(r.wo, cp.wo, 96, ())
    cp.hid.arrived(hpart(2, True), 4)
    cp.hid.arrived(hpart(2, False), 5)
    cp.cross.go(hid.at[hslot(2, c)], hid.at[hslot(2, c)], 3, mate)
    for k, dy in enumerate((0, -1, 1, 2)):
        cp.cross.arrived(hid.at[hslot(dy, 1 - c)], k)
    cp.edge.go(hid.at[7, pl.ds(112, 16)], r.edge, 0, next_dev)
    for k in range(1, 4):
        cp.ostage.arrived(r.ostage.at[(y + 4 - k) % 4], k - 1)
    r.ounit[...] = dot(pack(24), r.ostage[...].reshape(128, CH)).astype(BF)
    ring.pass_on(2)
    for k in range(4):
        ring.end(k)
    mine.wait()
    oring.first(r.ounit)
    mine = pltpu.make_async_copy(r.ounit, r.wo.at[g], local.at[1])
    mine.start()

    w, xs, bc, steps, sg = r.w, r.xs, r.bc, r.steps, r.sg

    def columns(a, z):
        return w[:, :, a:z].reshape(d, z - a)

    def project_bc(i, _):
        at = pl.multiple_of(i * 256, 256)
        got = dot(hid[pl.ds(i * 2, 2)].reshape(256, d), columns(2 * CH, UNIT)).astype(BF)
        bc[c, pl.ds(pl.multiple_of(at + 16, 16), 256), :] = got[:, :N]
        steps[pl.ds(at, 256), :] = got[:, N:]
        return 0

    lax.fori_loop(0, 4, project_bc, 0)
    mid = pl.ds(16, 1024)
    cp.bc.go(bc.at[c, mid], bc.at[c, mid], 0, mate)

    def project(i, _):
        at = pl.multiple_of(i * 256, 256)
        got = dot(hid[pl.ds(i * 2, 2)].reshape(256, d), columns(0, 2 * CH)).astype(BF)
        sg[pl.ds(at, 256), :] = got[:, :CH].astype(F32)
        xs[pl.ds(pl.multiple_of(at + 8, 8), 256), 0:CH] = got[:, CH:].astype(F32)
        return 0

    lax.fori_loop(0, 2, project, 0)
    cp.edge.arrived(r.edge, 0)
    bc[c, 0:16, :] = dot(r.edge[...], columns(2 * CH, 2 * CH + N)).astype(BF)
    cp.bc.go(bc.at[c, pl.ds(0, 16)], bc.at[c, pl.ds(0, 16)], 1, mate)
    xs[0:8, 0:CH] = dot(r.edge[...], columns(CH, 2 * CH))[8:16].astype(BF).astype(F32)
    lax.fori_loop(2, 4, project, 0)
    for k in (1, 3, 2):
        oring.turn(k)
    cp.bc.arrived(bc.at[1 - c, mid], 0)
    cp.bc.arrived(bc.at[1 - c, pl.ds(0, 16)], 1)
    for k in range(2):
        xs[0:8, CH + k * N : CH + k * N + N] = bc[k, 0:16, :].astype(F32)[8:16]
        xs[8:1032, CH + k * N : CH + k * N + N] = bc[k, 16:1040, :].astype(F32)

    hot = head_hot()
    starts = []
    total = jnp.int32(0)
    for k in range(8):
        starts.append(total)
        total = total + lens[k]
    row = lax.broadcasted_iota(jnp.int32, (128, 128), 0)
    col = lax.broadcasted_iota(jnp.int32, (128, 128), 1)
    head0 = c * 24 + y * MINE
    pick = jnp.where(col < MINE, (row == col + head0).astype(F32), 0.0).astype(BF)
    wrow = lax.broadcasted_iota(jnp.int32, (128, CH), 0)
    wcol = lax.broadcasted_iota(jnp.int32, (128, CH), 1)
    pickx = (wrow == wcol // HEAD + head0).astype(F32).astype(BF)

    def take(ref):
        at = jnp.where(col < MINE, (row == col + y * MINE).astype(F32), 0.0).astype(BF)[0:32]
        wide_v = jnp.concatenate([jnp.broadcast_to(ref[...], (8, 24)), jnp.zeros((8, 8), F32)], axis=1)
        return sum(dot(part, at) for part in three(wide_v))[0:1]

    def takex(ref):
        at = (wrow == wcol // HEAD + y * MINE).astype(F32).astype(BF)[0:32]
        wide_v = jnp.concatenate([jnp.broadcast_to(ref[...], (8, 24)), jnp.zeros((8, 8), F32)], axis=1)
        return sum(dot(part, at) for part in three(wide_v))[0:1]

    rate6 = jnp.where(col[0:1] < MINE, -jnp.exp(take(r.rates_log)), 0.0)
    bias6, biasx, skipx = take(r.dtb), takex(r.dtb), takex(r.skip)
    taps = cinner[...]
    biasc = r.binner[...]
    small, dps = r.small, r.dps
    small[0] = jnp.zeros((CH, N), BF)

    def find(pos):
        first = jnp.zeros(pos.shape, jnp.int32)
        for k in range(1, 8):
            first = jnp.where(pos >= starts[k], starts[k], first)
        return first

    def advance(i, held):
        old, dp, dprow = held
        at = pl.multiple_of(i * 256, 256)
        base = g * 1024 + i * 256
        first = find(base + lax.broadcasted_iota(jnp.int32, (256, 128), 0))
        off = base + lax.broadcasted_iota(jnp.int32, (256, 128), 0) - first
        xc = biasc + jnp.zeros((256, CH), F32)
        bv = r.bshared[:, :N] + jnp.zeros((256, N), F32)
        window = xs[pl.ds(at, 264), : CH + N]
        for lag in range(CONV):
            ok = (off >= lag).astype(F32)
            part = window[8 - lag : 264 - lag, :]
            xc = xc + taps[lag : lag + 1, :] * part[:, :CH] * wide(ok)
            bv = bv + cshared[lag : lag + 1, :N] * part[:, CH : CH + N] * ok
        xc = silu(xc)
        b_all = silu(bv).astype(BF)
        r.b[pl.ds(at, 256), :] = b_all
        step = steps[pl.ds(at, 256), :]
        dt6 = softplus(dot(step, pick) + bias6)
        log6 = rate6 * dt6
        dtx = softplus(dot(step, pickx) + biasx)
        xdt_all = xc * dtx
        r.xdt[pl.ds(at, 256), :] = xdt_all.astype(BF)
        r.y[pl.ds(at, 256), :] = skipx * xc
        for sub in range(2):
            k = i * 2 + sub
            p0 = base + sub * 128
            rows = slice(sub * 128, sub * 128 + 128)
            f0 = first[rows, :]
            mask = (row >= col) & (f0 == find(p0 + col))
            maskb = mask.astype(F32).astype(BF)
            cum = sum(dot(maskb, part) for part in three(log6[rows, :]))
            there = pl.ds(pl.multiple_of(at + sub * 128, 128), 128)
            r.cum[there, :] = cum
            cumt = cum.T
            flast = jnp.int32(0)
            glast = grps[0]
            for j in range(1, 8):
                got = p0 + 127 >= starts[j]
                flast = jnp.where(got, starts[j], flast)
                glast = jnp.where(got, grps[j], glast)
            w6 = jnp.exp(jnp.where(f0 == flast, cum[127:128, :] - cum, NEG))
            xw = (xdt_all[rows, :] * expand(w6, hot)).astype(BF)
            summary = dot_tn(xw, b_all[rows, :])
            keep = (flast < p0).astype(F32)
            ecum = jnp.exp(cum)
            r.fac[there, :] = jnp.where(f0 < p0, ecum, 0.0) * dprow
            scale = jnp.exp(jnp.broadcast_to(cumt[0:8, 127:128], (8, 128)))
            dp = dp * scale * keep
            dprow = dprow * jnp.exp(cum[127:128, :]) * keep
            dps[k] = dp
            start = r.initf[0]
            for j in range(1, 4):
                start = jnp.where(glast == j, r.initf[j], start)
            old = jnp.where(flast < p0, old, start)
            old = jnp.concatenate(
                [scale[h : h + 1, :] * old[h * HEAD : h * HEAD + HEAD, :] for h in range(MINE)], axis=0
            ) + summary
            small[k + 1] = old.astype(BF)
        return old, dp, dprow

    held = (jnp.zeros((CH, N), F32), jnp.ones((8, 128), F32), jnp.ones((1, 128), F32))
    last, dplast, _ = lax.fori_loop(0, 4, advance, held)

    state, parts, befores, carry = r.state, r.parts, r.befores, r.carry
    for j in range(3):
        state[:, j] = last[j * 128 : j * 128 + 128].reshape(16, 8, N)
    state[:, 3] = jnp.broadcast_to(dplast[None], (16, 8, N))
    for k in range(1, 16):
        cp.part.go(state.at[(g + k) % 16], parts.at[g], k - 1, peers[k - 1])
    parts[g] = state[g]
    for k in range(1, 4):
        t = (y + k) % 4
        cp.page.go(small.at[pl.ds(t * 2 + 1, 2)], r.pages.at[y], k - 1, near[k - 1])
        cp.decay.go(dps.at[pl.ds(t * 2, 2)], r.rates.at[y], k - 1, near[k - 1])
    for k in range(2):
        r.pages[y, k] = small[y * 2 + 1 + k]
        r.rates[y, k] = dps[y * 2 + k]

    def inside(i, _):
        first_at = pl.multiple_of(i * 256, 256)
        pos = g * 1024 + i * 256 + lax.broadcasted_iota(jnp.int32, (256, 128), 0)
        off = pos - find(pos)
        cv = r.bshared[:, N:] + jnp.zeros((256, N), F32)
        window = xs[pl.ds(first_at, 264), CH + N :]
        for lag in range(CONV):
            ok = (off >= lag).astype(F32)
            cv = cv + cshared[lag : lag + 1, N:] * window[8 - lag : 264 - lag, :] * ok
        c_all = silu(cv).astype(BF)
        r.c[pl.ds(first_at, 256), :] = c_all
        for sub in range(2):
            k = i * 2 + sub
            p0 = g * 1024 + k * 128
            at = pl.ds(pl.multiple_of(k * 128, 128), 128)
            f0 = find(p0 + row)
            mask = (row >= col) & (f0 == find(p0 + col))
            cum = r.cum[at, :]
            cumt = cum.T
            cb = c_all[sub * 128 : sub * 128 + 128, :]
            r.fx[at, :] = expand(r.fac[at, :], hot)
            cf = cb.astype(F32)
            scores = dot_nt(cb, r.b[at, :])
            gid = jnp.zeros((128, 128), jnp.int32) + grps[0]
            for j in range(1, 8):
                gid = jnp.where(p0 + row >= starts[j], grps[j], gid)
            gid = jnp.where(f0 < p0, 4, gid)
            chot = jnp.concatenate(
                [jnp.where(gid == j, cf, 0.0).astype(BF) for j in range(4)], axis=1
            )
            read = dot_nt(jnp.where(gid == 4, cf, 0.0).astype(BF), small[k])
            read = read + dot_nt(chot, r.initb[...])
            lane = col
            pieces = []
            for pair in range(3):
                xp = r.xdt[at, pair * 128 : pair * 128 + 128]
                got = []
                for h in (2 * pair, 2 * pair + 1):
                    diff = cum[:, h : h + 1] - cumt[h : h + 1, :]
                    mix = jnp.exp(jnp.where(mask, diff, NEG)) * scores
                    got.append(dot(mix.astype(BF), xp))
                pieces.append(jnp.where(lane < HEAD, got[0], got[1]))
            r.y[at, :] = (
                r.y[at, :] + expand(jnp.exp(cum), hot) * read + jnp.concatenate(pieces, axis=1)
            )
            sg[at, :] = silu(sg[at, :])
        return 0

    lax.fori_loop(0, 2, inside, 0)
    for k in range(1, 16):
        cp.part.arrived(parts.at[(g + 16 - k) % 16], k - 1)
    hb = g // 8
    run = [jnp.zeros((8, 128), F32) for _ in range(3)]
    for k in range(16):
        for j in range(3):
            befores[k, j] = run[j]
            run[j] = parts[k, 3, pl.ds(hb + 2 * j, 1), :] * run[j] + parts[k, j]
    for k in range(1, 16):
        cp.back.go(befores.at[(g + k) % 16], carry.at[g], k - 1, peers[k - 1])
    carry[g] = befores[g]
    lax.fori_loop(2, 4, inside, 0)
    for k in range(4):
        oring.pass_on(k)
        oring.end(k)
    mine.wait()
    for k in range(1, 16):
        cp.back.arrived(carry.at[(g + 16 - k) % 16], k - 1)

    carries = r.carries
    cs = jnp.concatenate([carry[:, j].reshape(128, N) for j in range(3)], axis=0).astype(BF)
    carries[y] = cs
    for k in range(1, 4):
        cp.state.go(carries.at[y], carries.at[y], k - 1, near[k - 1])
    ones = jnp.ones((8, CH), BF)
    gain = r.ngain[...]
    xs_out, xs_in, sq, sqr = r.xs_out, r.xs_in, r.sq, r.sqr

    def partial(dy, k, keep):
        t = (y + dy) % 4
        for part in range(2):
            core = c if part else 1 - c
            at = pl.ds(pl.multiple_of(t * 256 + core * 128, 128), 128)
            full = r.y[at, :] + r.fx[at, :] * dot_nt(r.c[at, :], cs)
            gv = full * sg[at, :]
            g2 = gv * gv
            top = g2.astype(BF)
            rest = (g2 - top.astype(F32)).astype(BF)
            sq[t * 2 + core] = dot_nt(ones, top) + dot_nt(ones, rest)
            gg = (gv * gain).astype(BF)
            for n in range(0, 1536, CH):
                got = dot_nt(gg, r.wo[n // 96 : n // 96 + 4].reshape(CH, CH)).astype(BF)
                if part:
                    keep[:, n : n + CH] = got
                else:
                    xs_out[k, :, n : n + CH] = got
            if not part:
                cp.mate.go(xs_out.at[k], xs_in.at[k], k, mate)

    def join(k, keep):
        cp.mate.arrived(xs_in.at[k], k)
        keep[...] = (keep[...].astype(F32) + xs_in[k].astype(F32)).astype(BF)

    opp, ahead, behind, own = r.opp, r.ahead, r.behind, r.own
    from_l, from_r = r.from_l, r.from_r
    partial(2, 0, opp)
    partial(1, 1, ahead)
    join(0, opp)
    cp.ring.go(opp.at[lo], r.low, 0, right)
    cp.ring.go(opp.at[hi], r.high, 1, left)
    partial(3, 2, behind)
    join(1, ahead)
    cp.ring.go(ahead.at[hi], from_l.at[hi], 2, right)
    join(2, behind)
    cp.ring.go(behind.at[lo], from_r.at[lo], 3, left)
    cp.ring.arrived(r.low, 0)
    ahead[0:64, :] = (ahead[0:64, :].astype(F32) + r.low[...].astype(F32)).astype(BF)
    cp.ring.go(ahead.at[lo], from_l.at[lo], 4, right)
    cp.ring.arrived(r.high, 1)
    behind[64:128, :] = (behind[64:128, :].astype(F32) + r.high[...].astype(F32)).astype(BF)
    cp.ring.go(behind.at[hi], from_r.at[hi], 5, left)
    partial(0, 3, own)
    for k in range(1, 8):
        cp.sum.go(sq.at[(q + k) % 8], sqr.at[q], k - 1, group[k - 1])
    sqr[q] = sq[q]
    join(3, own)

    swap = r.pt[0] != (g * 4 + y) * 2
    for k in range(4):
        t = (y + 4 - k) % 4
        if k:
            cp.state.arrived(carries.at[t], k - 1)
            cp.page.arrived(r.pages.at[t], k - 1)
            cp.decay.arrived(r.rates.at[t], k - 1)
        for h in range(MINE):
            at = slice(h * HEAD, h * HEAD + HEAD)
            into = carries[t, at, :].astype(F32)
            one, two = (
                r.pages[t, j, at, :].astype(F32) + r.rates[t, j, h : h + 1, :] * into
                for j in range(2)
            )
            r.snaps[0, t, at, :] = jnp.where(swap, two, one)
            r.snaps[1, t, at, :] = jnp.where(swap, one, two)

    snaps = pltpu.make_async_copy(r.snaps, page_o, local.at[0])
    snaps.start()

    for k in range(1, 8):
        cp.sum.arrived(sqr.at[(q + 8 - k) % 8], k - 1)
    total = sqr[0]
    for k in range(1, 8):
        total = total + sqr[k]
    scale = lax.rsqrt(total / DI + EPS)
    scale = jnp.broadcast_to(scale[0:1, :], (128, 128)).T
    cp.ring.arrived(from_l.at[hi], 2)
    cp.ring.arrived(from_r.at[lo], 3)
    cp.ring.arrived(from_l.at[lo], 4)
    cp.ring.arrived(from_r.at[hi], 5)
    for n in range(0, 1536, 128):
        cols = slice(n, n + 128)
        whole = sum(v[:, cols].astype(F32) for v in (own, from_l, from_r))
        r.res[:, cols] = (whole * scale).astype(BF)
    res = pltpu.make_async_copy(r.res, out_o, local.at[21])
    res.start()
    for part in vars(cp).values():
        part.close()
    for one in (snaps, res):
        one.wait()


def place_kernel(mixed, pages, mixed_o, pages_o, sems):
    copies = []
    for k in range(8):
        part = (k // 4, k % 4)
        copies.append(pltpu.make_async_copy(pages.at[part], pages_o.at[part], sems.at[k]))
    for k in range(4):
        part = pl.ds(k * 32, 32)
        copies.append(pltpu.make_async_copy(mixed.at[part], mixed_o.at[part], sems.at[8 + k]))
    for copy in copies:
        copy.start()
    for copy in copies:
        copy.wait()


def on_device(
    hidden_in, gate_proj, inner_proj, small_proj, row_layout, conv_inner, conv_shared,
    bias_inner, bias_shared, dt_bias, decay_log, skip_gain, norm_gain, out_proj,
    prompt_lengths, group_map, init_states, page_table,
):
    d = hidden_in.shape[1]
    hbm = pl.BlockSpec(memory_space=pltpu.HBM)
    dma = pltpu.SemaphoreType.DMA
    scratch = list(buffers(d).values())
    for count in COPY.values():
        scratch += [dma((count,)), dma((count,))]
    mixed, pages = pl.pallas_call(
        layer_kernel,
        in_specs=[hbm] * 18,
        out_specs=[hbm, hbm],
        out_shape=[
            jax.ShapeDtypeStruct((128, d), BF),
            jax.ShapeDtypeStruct((2, 4, CH, N), F32),
        ],
        scratch_shapes=scratch + [dma((22,))],
        compiler_params=pltpu.CompilerParams(
            collective_id=0, has_side_effects=True, vmem_limit_bytes=60 << 20
        ),
        name="layer",
    )(
        hidden_in, gate_proj, inner_proj, small_proj, conv_inner, conv_shared, bias_inner, norm_gain, out_proj.T,
        dt_bias, decay_log, skip_gain, row_layout, bias_shared, prompt_lengths, group_map, page_table, init_states.reshape(4, 24 * HEAD, N),
    )
    mixed, pages = pl.pallas_call(
        place_kernel,
        in_specs=[hbm, hbm],
        out_specs=[hbm, hbm],
        out_shape=[
            jax.ShapeDtypeStruct((128, d), BF),
            jax.ShapeDtypeStruct((2, 4, CH, N), F32),
        ],
        scratch_shapes=[dma((12,))],
        compiler_params=pltpu.CompilerParams(vmem_limit_bytes=60 << 20),
        name="place",
    )(mixed, pages)
    return (mixed, pages.reshape(2, 24, HEAD, N))


def solution(mesh):
    fine = Mesh(mesh.devices.reshape(4, 4, 4, 2), ("z", "x", "y", "tp"))
    seq = ("z", "x", "y")
    every = ("z", "x", "y", "tp")
    placed = (
        P(seq, None),
        P(every, None),
        P(every, None),
        P(every, None),
        P(),
        P(None, "tp"),
        P(),
        P("tp"),
        P(),
        P("tp"),
        P("tp"),
        P("tp"),
        P("tp"),
        P("tp", seq),
        P(),
        P(),
        P(None, "tp", None, None),
        P(seq),
    )
    return jax.shard_map(
        on_device,
        mesh=fine,
        in_specs=placed,
        out_specs=(P(every, None), P(seq, "tp", None, None)),
        check_vma=False,
    )
```

```python
from types import SimpleNamespace

import jax
import jax.numpy as jnp
from jax import lax
from jax.experimental import pallas as pl
from jax.experimental.pallas import tpu as pltpu
from jax.sharding import Mesh
from jax.sharding import PartitionSpec as P

N = 128
CONV = 4
PAGE = 128
DI = 3072
HEAD = 64
MINE = 6
CH = MINE * HEAD
EPS = 1e-05
BF = jnp.bfloat16
F32 = jnp.float32
NEG = -1e30


def dot(a, b):
    return jnp.dot(a, b, preferred_element_type=F32)


def dot_nt(a, b):
    return lax.dot_general(a, b, (((1,), (1,)), ((), ())), preferred_element_type=F32)


def dot_tn(a, b):
    return lax.dot_general(a, b, (((0,), (0,)), ((), ())), preferred_element_type=F32)


def silu(v):
    return v / (1.0 + jnp.exp(-v))


def softplus(v):
    return jnp.maximum(v, 0.0) + jnp.log1p(jnp.exp(-jnp.abs(v)))


def three(v):
    hi = v.astype(BF)
    rest = v - hi.astype(F32)
    mid = rest.astype(BF)
    return hi, mid, (rest - mid.astype(F32)).astype(BF)


def expand(v, hot):
    hi = v.astype(BF)
    lo = (v - hi.astype(F32)).astype(BF)
    return dot(hi, hot) + dot(lo, hot)


def head_hot():
    row = lax.broadcasted_iota(jnp.int32, (128, CH), 0)
    col = lax.broadcasted_iota(jnp.int32, (128, CH), 1)
    return (row == col // HEAD).astype(F32).astype(BF)


def wide(m):
    return jnp.concatenate([m, m, m], axis=1)


class Copies:
    def __init__(self, send, recv):
        self.send, self.recv, self.open = send, recv, []

    def go(self, src, dst, slot, device):
        copy = pltpu.make_async_remote_copy(
            src_ref=src,
            dst_ref=dst,
            send_sem=self.send.at[slot],
            recv_sem=self.recv.at[slot],
            device_id=device,
            device_id_type=pl.DeviceIdType.MESH,
        )
        copy.start()
        self.open.append(copy)

    def arrived(self, dst, slot):
        pltpu.make_async_remote_copy(
            src_ref=dst,
            dst_ref=dst,
            send_sem=self.send.at[slot],
            recv_sem=self.recv.at[slot],
            device_id=self.me,
            device_id_type=pl.DeviceIdType.MESH,
        ).wait_recv()

    def close(self):
        for copy in self.open:
            copy.wait_send()


def coords():
    return (
        lax.axis_index("z"),
        lax.axis_index("x"),
        lax.axis_index("y"),
        lax.axis_index("tp"),
    )


class Plane:
    def __init__(self, out, copies, rows, relay):
        self.out, self.copies, self.half, self.relay = out, copies, rows // 2, relay
        z, x, y, c = coords()
        self.y, self.c = y, c
        self.a = x * (1 - c) + z * c
        self.b = z * (1 - c) + x * c

    def at(self, da, db):
        a = (self.a + da + 8) % 4
        b = (self.b + db + 8) % 4
        c = self.c
        return b * (1 - c) + a * c, a * (1 - c) + b * c

    def device(self, da, db):
        z, x = self.at(da, db)
        return (z, x, self.y, self.c)

    def full(self, d, db=0):
        z, x = self.at(-d, db)
        return self.out.at[z * 4 + x]

    def low(self, d, db):
        z, x = self.at(-d, db)
        return self.out.at[z * 4 + x, pl.ds(0, self.half)]

    def high(self, d, db):
        z, x = self.at(-d, db)
        return self.out.at[z * 4 + x, pl.ds(self.half, self.half)]

    def first(self, own):
        for d in (1, 3, 2):
            self.copies.go(own, self.full(0), d - 1, self.device(d, 0))
        self.second(0, own)

    def second(self, d, src=None):
        src = self.full(d) if src is None else src
        self.copies.go(src, self.full(d), 3 + 4 * d, self.device(0, 1))
        self.copies.go(src, self.full(d), 4 + 4 * d, self.device(0, -1))
        if d not in self.relay:
            self.copies.go(src, self.full(d), 5 + 4 * d, self.device(0, 2))

    def turn(self, d):
        self.copies.arrived(self.full(d), d - 1)
        self.second(d)

    def pass_on(self, d):
        self.copies.arrived(self.full(d, -1), 3 + 4 * d)
        if d in self.relay:
            self.copies.go(self.low(d, -1), self.low(d, -1), 5 + 4 * d, self.device(0, 1))
        self.copies.arrived(self.full(d, 1), 4 + 4 * d)
        if d in self.relay:
            self.copies.go(self.high(d, 1), self.high(d, 1), 6 + 4 * d, self.device(0, -1))

    def end(self, d):
        if d in self.relay:
            self.copies.arrived(self.low(d, 2), 5 + 4 * d)
            self.copies.arrived(self.high(d, 2), 6 + 4 * d)
        else:
            self.copies.arrived(self.full(d, 2), 5 + 4 * d)


def pack(width):
    row = lax.broadcasted_iota(jnp.int32, (96, 128), 0)
    col = lax.broadcasted_iota(jnp.int32, (96, 128), 1)
    padded = 128 // (96 // width)
    return (col == row // width * padded + row % width).astype(F32).astype(BF)


UNIT = 1024
COPY = dict(
    stage=7, ostage=3, hid=6, cross=4, w=19, edge=1, wo=19, bc=2,
    part=15, back=15, page=3, decay=3, mate=4, ring=6, sum=7, state=3,
)


def buffers(d):
    vmem = pltpu.VMEM
    return dict(
        hidden=vmem((128, d), BF),
        gate_w=vmem((12, DI), F32),
        inner_w=vmem((12, DI), F32),
        small_w=vmem((12, 304), F32),
        cinner=vmem((4, CH), F32),
        cshared=vmem((4, 2 * N), F32),
        binner=vmem((1, CH), F32),
        ngain=vmem((1, CH), F32),
        dtb=vmem((1, 24), F32),
        rates_log=vmem((1, 24), F32),
        skip=vmem((1, 24), F32),
        layout=vmem((1, 128), jnp.int32),
        bshared=vmem((1, 2 * N), F32),
        out_w=vmem((24, d), F32),
        lens=pltpu.SMEM((8,), jnp.int32),
        grps=pltpu.SMEM((8,), jnp.int32),
        pt=pltpu.SMEM((2,), jnp.int32),
        pieces=vmem((8, 16, UNIT), BF),
        stage=vmem((8, 16, UNIT), BF),
        unit=vmem((96, UNIT), BF),
        half=vmem((128, d), BF),
        w=vmem((16, 96, UNIT), BF),
        hid=vmem((8, 128, d), BF),
        edge=vmem((16, d), BF),
        initf=vmem((4, CH, N), F32),
        initb=vmem((CH, 4 * N), BF),
        sg=vmem((1024, CH), F32),
        xs=vmem((1032, CH + 2 * N), F32),
        steps=vmem((1024, 128), BF),
        y=vmem((1024, CH), F32),
        xdt=vmem((1024, CH), BF),
        b=vmem((1024, N), BF),
        c=vmem((1024, N), BF),
        cum=vmem((1024, 128), F32),
        fx=vmem((1024, CH), F32),
        fac=vmem((1024, 128), F32),
        small=vmem((9, CH, N), BF),
        dps=vmem((8, 8, N), F32),
        carries=vmem((4, CH, N), BF),
        pages=vmem((4, 2, CH, N), BF),
        rates=vmem((4, 2, 8, N), F32),
        bc=vmem((2, 1040, N), BF),
        state=vmem((16, 4, 8, N), F32),
        parts=vmem((16, 4, 8, N), F32),
        befores=vmem((16, 3, 8, N), F32),
        carry=vmem((16, 3, 8, N), F32),
        outp=vmem((4, 32, CH), BF),
        ostage=vmem((4, 32, CH), BF),
        ounit=vmem((96, CH), BF),
        wo=vmem((16, 96, CH), BF),
        opp=vmem((128, d), BF),
        ahead=vmem((128, d), BF),
        behind=vmem((128, d), BF),
        own=vmem((128, d), BF),
        xs_out=vmem((4, 128, d), BF),
        xs_in=vmem((4, 128, d), BF),
        low=vmem((64, d), BF),
        high=vmem((64, d), BF),
        from_l=vmem((128, d), BF),
        from_r=vmem((128, d), BF),
        sq=vmem((8, 8, 128), F32),
        sqr=vmem((8, 8, 128), F32),
        snaps=vmem((2, 4, CH, N), F32),
        res=vmem((128, d), BF),
    )


def layer_kernel(
    hidden_h, gate_h, inner_h, small_h, cinner_h, cshared_h, binner_h, ngain_h, out_h,
    dtb_h, rates_h, skip_h, layout_h, bshared_h,
    lens_h, grps_h, pt_h, init, out_o, page_o, *refs,
):
    d = hidden_h.shape[1]
    names = list(buffers(d))
    r = SimpleNamespace(**dict(zip(names, refs)))
    sems = refs[len(names):]
    z, x, y, c = coords()
    me_not = (z, x, y, 1 - c)
    cp = SimpleNamespace()
    for i, name in enumerate(COPY):
        setattr(cp, name, Copies(sems[2 * i], sems[2 * i + 1]))
        getattr(cp, name).me = me_not
    local = sems[2 * len(COPY)]
    q = y * 2 + c
    g = z * 4 + x
    mate = me_not
    right, left = (z, x, (y + 1) % 4, c), (z, x, (y + 3) % 4, c)
    near = [(z, x, (y + k) % 4, c) for k in range(1, 4)]
    group = [(z, x, ((q + k) % 8) // 2, (q + k) % 2) for k in range(1, 8)]
    peers = [(((g + k) % 16) // 4, ((g + k) % 16) % 4, y, c) for k in range(1, 16)]
    next_dev = peers[0]
    barrier = pltpu.get_barrier_semaphore()
    for device in group + peers:
        pl.semaphore_signal(
            barrier, inc=1, device_id=device, device_id_type=pl.DeviceIdType.MESH
        )

    mychan = pl.ds(pl.multiple_of(y * CH, CH), CH)
    loads = dict(
        gate_w=gate_h,
        inner_w=inner_h,
        small_w=small_h,
        hidden=hidden_h.at[pl.ds(pl.multiple_of(c * 128, 128), 128)],
        out_w=out_h,
        dtb=dtb_h,
        rates_log=rates_h,
        skip=skip_h,
        layout=layout_h,
        bshared=bshared_h,
        binner=binner_h.at[mychan],
        ngain=ngain_h.at[mychan],
        cinner=cinner_h.at[:, mychan],
        cshared=cshared_h,
        lens=lens_h,
        grps=grps_h,
        pt=pt_h,
        initf=init.at[:, mychan],
    )
    load = SimpleNamespace()
    for i, name in enumerate(loads):
        to = getattr(r, name)
        if loads[name].ndim == 1 and to.shape[0] == 1:
            to = to.at[0]
        setattr(load, name, pltpu.make_async_copy(loads[name], to, local.at[2 + i]))
        getattr(load, name).start()
    gate_w, inner_w, small_w, hidden = r.gate_w, r.inner_w, r.small_w, r.hidden
    cinner, cshared = r.cinner, r.cshared
    lens, grps, outp = r.lens, r.grps, r.outp
    pieces, stage = r.pieces, r.stage
    outp[...] = jnp.zeros_like(outp)
    pieces[...] = jnp.zeros_like(pieces)
    for one in (load.gate_w, load.inner_w, load.small_w, load.out_w):
        one.wait()
    for t in range(4):
        outp[t, 0:24, :] = r.out_w[:, t * CH : t * CH + CH].astype(BF)
    for t in range(8):
        a = 1536 * (t % 2) + CH * (t // 2)
        pieces[t, 0:12, 0:CH] = gate_w[:, a : a + CH].astype(BF)
        pieces[t, 0:12, CH : 2 * CH] = inner_w[:, a : a + CH].astype(BF)
        b = N * (t % 2)
        pieces[t, 0:12, 2 * CH : 2 * CH + N] = small_w[:, b : b + N].astype(BF)
        pieces[t, 0:12, 2 * CH + N : 2 * CH + N + 48] = small_w[:, 2 * N :].astype(BF)
    half = r.half
    load.layout.wait()
    load.hidden.wait()
    lay = jnp.broadcast_to(r.layout[...], (8, 128)).astype(F32).astype(BF)
    rows = hidden[...]
    for j in range(0, d, CH):
        brow = lax.broadcasted_iota(jnp.int32, (128, CH), 0)
        bcol = lax.broadcasted_iota(jnp.int32, (128, CH), 1) + j
        block = dot(lay, (brow == bcol // 12).astype(F32).astype(BF))[0:1]
        want = block * 12.0 + (bcol[0:1] % 12).astype(F32)
        frow = lax.broadcasted_iota(jnp.int32, (d, CH), 0).astype(F32)
        pick = jnp.where(frow == want, 1.0, 0.0).astype(BF)
        half[:, j : j + CH] = dot(rows, pick).astype(BF)
    pl.semaphore_wait(barrier, len(group) + len(peers))

    for k in range(1, 8):
        cp.stage.go(pieces.at[(q + k) % 8], stage.at[q], k - 1, group[k - 1])
    stage[q] = pieces[q]
    r.ostage[y] = outp[y]

    hid = r.hid

    def hslot(dy, core):
        return ((y + dy + 4) % 4) * 2 + core

    def hpart(dy, low):
        return hid.at[hslot(dy, c), pl.ds(0 if low else 64, 64)]

    lo, hi = pl.ds(0, 64), pl.ds(64, 64)
    cp.hid.go(half.at[lo], hpart(0, True), 0, right)
    cp.hid.go(half.at[hi], hpart(0, False), 2, left)
    cp.hid.go(half.at[hi], hpart(0, False), 1, right)
    cp.hid.go(half.at[lo], hpart(0, True), 3, left)
    cp.cross.go(half, hid.at[hslot(0, c)], 0, mate)
    hid[q] = half[...]

    for k in range(1, 8):
        cp.stage.arrived(stage.at[(q + 8 - k) % 8], k - 1)
    packer = pack(12)
    for j in range(0, UNIT, 512):
        r.unit[:, j : j + 512] = dot(
            packer, stage[:, :, j : j + 512].reshape(128, 512)
        ).astype(BF)
    ring = Plane(r.w, cp.w, 96, (0, 1, 3))
    ring.first(r.unit)
    mine = pltpu.make_async_copy(r.unit, r.w.at[g], local.at[1])
    mine.start()
    for one in (load.dtb, load.rates_log, load.skip, load.bshared):
        one.wait()
    for one in (load.initf, load.cinner, load.cshared, load.binner, load.ngain, load.lens, load.grps, load.pt):
        one.wait()
    for k in range(4):
        r.initb[:, k * N : k * N + N] = r.initf[k].astype(BF)

    cp.hid.arrived(hpart(-1, True), 0)
    cp.hid.go(hpart(-1, True), hpart(-1, True), 4, right)
    cp.hid.arrived(hpart(1, False), 2)
    cp.hid.go(hpart(1, False), hpart(1, False), 5, left)
    for k in range(1, 4):
        cp.ostage.go(outp.at[(y + k) % 4], r.ostage.at[y], k - 1, near[k - 1])
    ring.turn(1)
    ring.turn(3)
    ring.turn(2)
    ring.pass_on(0)
    cp.hid.arrived(hpart(-1, False), 1)
    cp.cross.go(hid.at[hslot(-1, c)], hid.at[hslot(-1, c)], 1, mate)
    cp.hid.arrived(hpart(1, True), 3)
    cp.cross.go(hid.at[hslot(1, c)], hid.at[hslot(1, c)], 2, mate)
    ring.pass_on(1)
    ring.pass_on(3)
    oring = Plane(r.wo, cp.wo, 96, ())
    cp.hid.arrived(hpart(2, True), 4)
    cp.hid.arrived(hpart(2, False), 5)
    cp.cross.go(hid.at[hslot(2, c)], hid.at[hslot(2, c)], 3, mate)
    for k, dy in enumerate((0, -1, 1, 2)):
        cp.cross.arrived(hid.at[hslot(dy, 1 - c)], k)
    cp.edge.go(hid.at[7, pl.ds(112, 16)], r.edge, 0, next_dev)
    for k in range(1, 4):
        cp.ostage.arrived(r.ostage.at[(y + 4 - k) % 4], k - 1)
    r.ounit[...] = dot(pack(24), r.ostage[...].reshape(128, CH)).astype(BF)
    ring.pass_on(2)
    for k in range(4):
        ring.end(k)
    mine.wait()
    oring.first(r.ounit)
    mine = pltpu.make_async_copy(r.ounit, r.wo.at[g], local.at[1])
    mine.start()

    w, xs, bc, steps, sg = r.w, r.xs, r.bc, r.steps, r.sg

    def columns(a, z):
        return w[:, :, a:z].reshape(d, z - a)

    def project_bc(i, _):
        at = pl.multiple_of(i * 256, 256)
        got = dot(hid[pl.ds(i * 2, 2)].reshape(256, d), columns(2 * CH, UNIT)).astype(BF)
        bc[c, pl.ds(pl.multiple_of(at + 16, 16), 256), :] = got[:, :N]
        steps[pl.ds(at, 256), :] = got[:, N:]
        return 0

    lax.fori_loop(0, 4, project_bc, 0)
    mid = pl.ds(16, 1024)
    cp.bc.go(bc.at[c, mid], bc.at[c, mid], 0, mate)

    def project(i, _):
        at = pl.multiple_of(i * 256, 256)
        got = dot(hid[pl.ds(i * 2, 2)].reshape(256, d), columns(0, 2 * CH)).astype(BF)
        sg[pl.ds(at, 256), :] = got[:, :CH].astype(F32)
        xs[pl.ds(pl.multiple_of(at + 8, 8), 256), 0:CH] = got[:, CH:].astype(F32)
        return 0

    lax.fori_loop(0, 2, project, 0)
    cp.edge.arrived(r.edge, 0)
    bc[c, 0:16, :] = dot(r.edge[...], columns(2 * CH, 2 * CH + N)).astype(BF)
    cp.bc.go(bc.at[c, pl.ds(0, 16)], bc.at[c, pl.ds(0, 16)], 1, mate)
    xs[0:8, 0:CH] = dot(r.edge[...], columns(CH, 2 * CH))[8:16].astype(BF).astype(F32)
    lax.fori_loop(2, 4, project, 0)
    for k in (1, 3, 2):
        oring.turn(k)
    cp.bc.arrived(bc.at[1 - c, mid], 0)
    cp.bc.arrived(bc.at[1 - c, pl.ds(0, 16)], 1)
    for k in range(2):
        xs[0:8, CH + k * N : CH + k * N + N] = bc[k, 0:16, :].astype(F32)[8:16]
        xs[8:1032, CH + k * N : CH + k * N + N] = bc[k, 16:1040, :].astype(F32)

    hot = head_hot()
    starts = []
    total = jnp.int32(0)
    for k in range(8):
        starts.append(total)
        total = total + lens[k]
    row = lax.broadcasted_iota(jnp.int32, (128, 128), 0)
    col = lax.broadcasted_iota(jnp.int32, (128, 128), 1)
    head0 = c * 24 + y * MINE
    pick = jnp.where(col < MINE, (row == col + head0).astype(F32), 0.0).astype(BF)
    wrow = lax.broadcasted_iota(jnp.int32, (128, CH), 0)
    wcol = lax.broadcasted_iota(jnp.int32, (128, CH), 1)
    pickx = (wrow == wcol // HEAD + head0).astype(F32).astype(BF)

    def take(ref):
        at = jnp.where(col < MINE, (row == col + y * MINE).astype(F32), 0.0).astype(BF)[0:32]
        wide_v = jnp.concatenate([jnp.broadcast_to(ref[...], (8, 24)), jnp.zeros((8, 8), F32)], axis=1)
        return sum(dot(part, at) for part in three(wide_v))[0:1]

    def takex(ref):
        at = (wrow == wcol // HEAD + y * MINE).astype(F32).astype(BF)[0:32]
        wide_v = jnp.concatenate([jnp.broadcast_to(ref[...], (8, 24)), jnp.zeros((8, 8), F32)], axis=1)
        return sum(dot(part, at) for part in three(wide_v))[0:1]

    rate6 = jnp.where(col[0:1] < MINE, -jnp.exp(take(r.rates_log)), 0.0)
    bias6, biasx, skipx = take(r.dtb), takex(r.dtb), takex(r.skip)
    taps = cinner[...]
    biasc = r.binner[...]
    small, dps = r.small, r.dps
    small[0] = jnp.zeros((CH, N), BF)

    def find(pos):
        first = jnp.zeros(pos.shape, jnp.int32)
        for k in range(1, 8):
            first = jnp.where(pos >= starts[k], starts[k], first)
        return first

    def advance(i, held):
        old, dp, dprow = held
        at = pl.multiple_of(i * 256, 256)
        base = g * 1024 + i * 256
        first = find(base + lax.broadcasted_iota(jnp.int32, (256, 128), 0))
        off = base + lax.broadcasted_iota(jnp.int32, (256, 128), 0) - first
        xc = biasc + jnp.zeros((256, CH), F32)
        bv = r.bshared[:, :N] + jnp.zeros((256, N), F32)
        window = xs[pl.ds(at, 264), : CH + N]
        for lag in range(CONV):
            ok = (off >= lag).astype(F32)
            part = window[8 - lag : 264 - lag, :]
            xc = xc + taps[lag : lag + 1, :] * part[:, :CH] * wide(ok)
            bv = bv + cshared[lag : lag + 1, :N] * part[:, CH : CH + N] * ok
        xc = silu(xc)
        b_all = silu(bv).astype(BF)
        r.b[pl.ds(at, 256), :] = b_all
        step = steps[pl.ds(at, 256), :]
        dt6 = softplus(dot(step, pick) + bias6)
        log6 = rate6 * dt6
        dtx = softplus(dot(step, pickx) + biasx)
        xdt_all = xc * dtx
        r.xdt[pl.ds(at, 256), :] = xdt_all.astype(BF)
        r.y[pl.ds(at, 256), :] = skipx * xc
        for sub in range(2):
            k = i * 2 + sub
            p0 = base + sub * 128
            rows = slice(sub * 128, sub * 128 + 128)
            f0 = first[rows, :]
            mask = (row >= col) & (f0 == find(p0 + col))
            maskb = mask.astype(F32).astype(BF)
            cum = sum(dot(maskb, part) for part in three(log6[rows, :]))
            there = pl.ds(pl.multiple_of(at + sub * 128, 128), 128)
            r.cum[there, :] = cum
            cumt = cum.T
            flast = jnp.int32(0)
            glast = grps[0]
            for j in range(1, 8):
                got = p0 + 127 >= starts[j]
                flast = jnp.where(got, starts[j], flast)
                glast = jnp.where(got, grps[j], glast)
            w6 = jnp.exp(jnp.where(f0 == flast, cum[127:128, :] - cum, NEG))
            xw = (xdt_all[rows, :] * expand(w6, hot)).astype(BF)
            summary = dot_tn(xw, b_all[rows, :])
            keep = (flast < p0).astype(F32)
            ecum = jnp.exp(cum)
            r.fac[there, :] = jnp.where(f0 < p0, ecum, 0.0) * dprow
            scale = jnp.exp(jnp.broadcast_to(cumt[0:8, 127:128], (8, 128)))
            dp = dp * scale * keep
            dprow = dprow * jnp.exp(cum[127:128, :]) * keep
            dps[k] = dp
            start = r.initf[0]
            for j in range(1, 4):
                start = jnp.where(glast == j, r.initf[j], start)
            old = jnp.where(flast < p0, old, start)
            old = jnp.concatenate(
                [scale[h : h + 1, :] * old[h * HEAD : h * HEAD + HEAD, :] for h in range(MINE)], axis=0
            ) + summary
            small[k + 1] = old.astype(BF)
        return old, dp, dprow

    held = (jnp.zeros((CH, N), F32), jnp.ones((8, 128), F32), jnp.ones((1, 128), F32))
    last, dplast, _ = lax.fori_loop(0, 4, advance, held)

    state, parts, befores, carry = r.state, r.parts, r.befores, r.carry
    for j in range(3):
        state[:, j] = last[j * 128 : j * 128 + 128].reshape(16, 8, N)
    state[:, 3] = jnp.broadcast_to(dplast[None], (16, 8, N))
    for k in range(1, 16):
        cp.part.go(state.at[(g + k) % 16], parts.at[g], k - 1, peers[k - 1])
    parts[g] = state[g]
    for k in range(1, 4):
        t = (y + k) % 4
        cp.page.go(small.at[pl.ds(t * 2 + 1, 2)], r.pages.at[y], k - 1, near[k - 1])
        cp.decay.go(dps.at[pl.ds(t * 2, 2)], r.rates.at[y], k - 1, near[k - 1])
    for k in range(2):
        r.pages[y, k] = small[y * 2 + 1 + k]
        r.rates[y, k] = dps[y * 2 + k]

    def inside(i, _):
        first_at = pl.multiple_of(i * 256, 256)
        pos = g * 1024 + i * 256 + lax.broadcasted_iota(jnp.int32, (256, 128), 0)
        off = pos - find(pos)
        cv = r.bshared[:, N:] + jnp.zeros((256, N), F32)
        window = xs[pl.ds(first_at, 264), CH + N :]
        for lag in range(CONV):
            ok = (off >= lag).astype(F32)
            cv = cv + cshared[lag : lag + 1, N:] * window[8 - lag : 264 - lag, :] * ok
        c_all = silu(cv).astype(BF)
        r.c[pl.ds(first_at, 256), :] = c_all
        for sub in range(2):
            k = i * 2 + sub
            p0 = g * 1024 + k * 128
            at = pl.ds(pl.multiple_of(k * 128, 128), 128)
            f0 = find(p0 + row)
            mask = (row >= col) & (f0 == find(p0 + col))
            cum = r.cum[at, :]
            cumt = cum.T
            cb = c_all[sub * 128 : sub * 128 + 128, :]
            r.fx[at, :] = expand(r.fac[at, :], hot)
            cf = cb.astype(F32)
            scores = dot_nt(cb, r.b[at, :])
            gid = jnp.zeros((128, 128), jnp.int32) + grps[0]
            for j in range(1, 8):
                gid = jnp.where(p0 + row >= starts[j], grps[j], gid)
            gid = jnp.where(f0 < p0, 4, gid)
            chot = jnp.concatenate(
                [jnp.where(gid == j, cf, 0.0).astype(BF) for j in range(4)], axis=1
            )
            read = dot_nt(jnp.where(gid == 4, cf, 0.0).astype(BF), small[k])
            read = read + dot_nt(chot, r.initb[...])
            lane = col
            pieces = []
            for pair in range(3):
                xp = r.xdt[at, pair * 128 : pair * 128 + 128]
                got = []
                for h in (2 * pair, 2 * pair + 1):
                    diff = cum[:, h : h + 1] - cumt[h : h + 1, :]
                    mix = jnp.exp(jnp.where(mask, diff, NEG)) * scores
                    got.append(dot(mix.astype(BF), xp))
                pieces.append(jnp.where(lane < HEAD, got[0], got[1]))
            r.y[at, :] = (
                r.y[at, :] + expand(jnp.exp(cum), hot) * read + jnp.concatenate(pieces, axis=1)
            )
            sg[at, :] = silu(sg[at, :])
        return 0

    lax.fori_loop(0, 2, inside, 0)
    for k in range(1, 16):
        cp.part.arrived(parts.at[(g + 16 - k) % 16], k - 1)
    hb = g // 8
    run = [jnp.zeros((8, 128), F32) for _ in range(3)]
    for k in range(16):
        for j in range(3):
            befores[k, j] = run[j]
            run[j] = parts[k, 3, pl.ds(hb + 2 * j, 1), :] * run[j] + parts[k, j]
    for k in range(1, 16):
        cp.back.go(befores.at[(g + k) % 16], carry.at[g], k - 1, peers[k - 1])
    carry[g] = befores[g]
    lax.fori_loop(2, 4, inside, 0)
    for k in range(4):
        oring.pass_on(k)
        oring.end(k)
    mine.wait()
    for k in range(1, 16):
        cp.back.arrived(carry.at[(g + 16 - k) % 16], k - 1)

    carries = r.carries
    cs = jnp.concatenate([carry[:, j].reshape(128, N) for j in range(3)], axis=0).astype(BF)
    carries[y] = cs
    for k in range(1, 4):
        cp.state.go(carries.at[y], carries.at[y], k - 1, near[k - 1])
    ones = jnp.ones((8, CH), BF)
    gain = r.ngain[...]
    xs_out, xs_in, sq, sqr = r.xs_out, r.xs_in, r.sq, r.sqr

    def partial(dy, k, keep):
        t = (y + dy) % 4
        for part in range(2):
            core = c if part else 1 - c
            at = pl.ds(pl.multiple_of(t * 256 + core * 128, 128), 128)
            full = r.y[at, :] + r.fx[at, :] * dot_nt(r.c[at, :], cs)
            gv = full * sg[at, :]
            g2 = gv * gv
            top = g2.astype(BF)
            rest = (g2 - top.astype(F32)).astype(BF)
            sq[t * 2 + core] = dot_nt(ones, top) + dot_nt(ones, rest)
            gg = (gv * gain).astype(BF)
            for n in range(0, 1536, CH):
                got = dot_nt(gg, r.wo[n // 96 : n // 96 + 4].reshape(CH, CH)).astype(BF)
                if part:
                    keep[:, n : n + CH] = got
                else:
                    xs_out[k, :, n : n + CH] = got
            if not part:
                cp.mate.go(xs_out.at[k], xs_in.at[k], k, mate)

    def join(k, keep):
        cp.mate.arrived(xs_in.at[k], k)
        keep[...] = (keep[...].astype(F32) + xs_in[k].astype(F32)).astype(BF)

    opp, ahead, behind, own = r.opp, r.ahead, r.behind, r.own
    from_l, from_r = r.from_l, r.from_r
    partial(2, 0, opp)
    partial(1, 1, ahead)
    join(0, opp)
    cp.ring.go(opp.at[lo], r.low, 0, right)
    cp.ring.go(opp.at[hi], r.high, 1, left)
    partial(3, 2, behind)
    join(1, ahead)
    cp.ring.go(ahead.at[hi], from_l.at[hi], 2, right)
    join(2, behind)
    cp.ring.go(behind.at[lo], from_r.at[lo], 3, left)
    cp.ring.arrived(r.low, 0)
    ahead[0:64, :] = (ahead[0:64, :].astype(F32) + r.low[...].astype(F32)).astype(BF)
    cp.ring.go(ahead.at[lo], from_l.at[lo], 4, right)
    cp.ring.arrived(r.high, 1)
    behind[64:128, :] = (behind[64:128, :].astype(F32) + r.high[...].astype(F32)).astype(BF)
    cp.ring.go(behind.at[hi], from_r.at[hi], 5, left)
    partial(0, 3, own)
    for k in range(1, 8):
        cp.sum.go(sq.at[(q + k) % 8], sqr.at[q], k - 1, group[k - 1])
    sqr[q] = sq[q]
    join(3, own)

    swap = r.pt[0] != (g * 4 + y) * 2
    for k in range(4):
        t = (y + 4 - k) % 4
        if k:
            cp.state.arrived(carries.at[t], k - 1)
            cp.page.arrived(r.pages.at[t], k - 1)
            cp.decay.arrived(r.rates.at[t], k - 1)
        for h in range(MINE):
            at = slice(h * HEAD, h * HEAD + HEAD)
            into = carries[t, at, :].astype(F32)
            one, two = (
                r.pages[t, j, at, :].astype(F32) + r.rates[t, j, h : h + 1, :] * into
                for j in range(2)
            )
            r.snaps[0, t, at, :] = jnp.where(swap, two, one)
            r.snaps[1, t, at, :] = jnp.where(swap, one, two)

    snaps = pltpu.make_async_copy(r.snaps, page_o, local.at[0])
    snaps.start()

    for k in range(1, 8):
        cp.sum.arrived(sqr.at[(q + 8 - k) % 8], k - 1)
    total = sqr[0]
    for k in range(1, 8):
        total = total + sqr[k]
    scale = lax.rsqrt(total / DI + EPS)
    scale = jnp.broadcast_to(scale[0:1, :], (128, 128)).T
    cp.ring.arrived(from_l.at[hi], 2)
    cp.ring.arrived(from_r.at[lo], 3)
    cp.ring.arrived(from_l.at[lo], 4)
    cp.ring.arrived(from_r.at[hi], 5)
    for n in range(0, 1536, 128):
        cols = slice(n, n + 128)
        whole = sum(v[:, cols].astype(F32) for v in (own, from_l, from_r))
        r.res[:, cols] = (whole * scale).astype(BF)
    res = pltpu.make_async_copy(r.res, out_o, local.at[21])
    res.start()
    for part in vars(cp).values():
        part.close()
    for one in (snaps, res):
        one.wait()


def place_kernel(mixed, pages, mixed_o, pages_o, block, snaps, came, gone):
    moves = []
    for k in range(4):
        part = pl.ds(k * 32, 32)
        moves.append((mixed.at[part], block.at[part], mixed_o.at[part]))
    for k in range(8):
        part = (k // 4, k % 4)
        moves.append((pages.at[part], snaps.at[part], pages_o.at[part]))
    ins = [pltpu.make_async_copy(a, b, came.at[k]) for k, (a, b, _) in enumerate(moves)]
    outs = [pltpu.make_async_copy(b, o, gone.at[k]) for k, (_, b, o) in enumerate(moves)]
    for copy in ins:
        copy.start()
    for one, two in zip(ins, outs):
        one.wait()
        two.start()
    for copy in outs:
        copy.wait()


def on_device(
    hidden_in, gate_proj, inner_proj, small_proj, row_layout, conv_inner, conv_shared,
    bias_inner, bias_shared, dt_bias, decay_log, skip_gain, norm_gain, out_proj,
    prompt_lengths, group_map, init_states, page_table,
):
    d = hidden_in.shape[1]
    hbm = pl.BlockSpec(memory_space=pltpu.HBM)
    dma = pltpu.SemaphoreType.DMA
    scratch = list(buffers(d).values())
    for count in COPY.values():
        scratch += [dma((count,)), dma((count,))]
    mixed, pages = pl.pallas_call(
        layer_kernel,
        in_specs=[hbm] * 18,
        out_specs=[hbm, hbm],
        out_shape=[
            jax.ShapeDtypeStruct((128, d), BF),
            jax.ShapeDtypeStruct((2, 4, CH, N), F32),
        ],
        scratch_shapes=scratch + [dma((22,))],
        compiler_params=pltpu.CompilerParams(
            collective_id=0, has_side_effects=True, vmem_limit_bytes=60 << 20
        ),
        name="layer",
    )(
        hidden_in, gate_proj, inner_proj, small_proj, conv_inner, conv_shared, bias_inner, norm_gain, out_proj.T,
        dt_bias, decay_log, skip_gain, row_layout, bias_shared, prompt_lengths, group_map, page_table, init_states.reshape(4, 24 * HEAD, N),
    )
    mixed, pages = pl.pallas_call(
        place_kernel,
        in_specs=[hbm, hbm],
        out_specs=[hbm, hbm],
        out_shape=[
            jax.ShapeDtypeStruct((128, d), BF),
            jax.ShapeDtypeStruct((2, 4, CH, N), F32),
        ],
        scratch_shapes=[
            pltpu.VMEM((128, d), BF),
            pltpu.VMEM((2, 4, CH, N), F32),
            dma((12,)), dma((12,)),
        ],
        compiler_params=pltpu.CompilerParams(vmem_limit_bytes=60 << 20),
        name="place",
    )(mixed, pages)
    return (mixed, pages.reshape(2, 24, HEAD, N))


def solution(mesh):
    fine = Mesh(mesh.devices.reshape(4, 4, 4, 2), ("z", "x", "y", "tp"))
    seq = ("z", "x", "y")
    every = ("z", "x", "y", "tp")
    placed = (
        P(seq, None),
        P(every, None),
        P(every, None),
        P(every, None),
        P(),
        P(None, "tp"),
        P(),
        P("tp"),
        P(),
        P("tp"),
        P("tp"),
        P("tp"),
        P("tp"),
        P("tp", seq),
        P(),
        P(),
        P(None, "tp", None, None),
        P(seq),
    )
    return jax.shard_map(
        on_device,
        mesh=fine,
        in_specs=placed,
        out_specs=(P(every, None), P(seq, "tp", None, None)),
        check_vma=False,
    )
```

```python
from types import SimpleNamespace

import jax
import jax.numpy as jnp
from jax import lax
from jax.experimental import pallas as pl
from jax.experimental.pallas import tpu as pltpu
from jax.sharding import Mesh
from jax.sharding import PartitionSpec as P

N = 128
CONV = 4
PAGE = 128
DI = 3072
HEAD = 64
MINE = 6
CH = MINE * HEAD
EPS = 1e-05
BF = jnp.bfloat16
F32 = jnp.float32
NEG = -1e30


def dot(a, b):
    return jnp.dot(a, b, preferred_element_type=F32)


def dot_nt(a, b):
    return lax.dot_general(a, b, (((1,), (1,)), ((), ())), preferred_element_type=F32)


def dot_tn(a, b):
    return lax.dot_general(a, b, (((0,), (0,)), ((), ())), preferred_element_type=F32)


def silu(v):
    return v / (1.0 + jnp.exp(-v))


def softplus(v):
    return jnp.maximum(v, 0.0) + jnp.log1p(jnp.exp(-jnp.abs(v)))


def three(v):
    hi = v.astype(BF)
    rest = v - hi.astype(F32)
    mid = rest.astype(BF)
    return hi, mid, (rest - mid.astype(F32)).astype(BF)


def expand(v, hot):
    hi = v.astype(BF)
    lo = (v - hi.astype(F32)).astype(BF)
    return dot(hi, hot) + dot(lo, hot)


def head_hot():
    row = lax.broadcasted_iota(jnp.int32, (128, CH), 0)
    col = lax.broadcasted_iota(jnp.int32, (128, CH), 1)
    return (row == col // HEAD).astype(F32).astype(BF)


def wide(m):
    return jnp.concatenate([m, m, m], axis=1)


class Copies:
    def __init__(self, send, recv):
        self.send, self.recv, self.open = send, recv, []

    def go(self, src, dst, slot, device):
        copy = pltpu.make_async_remote_copy(
            src_ref=src,
            dst_ref=dst,
            send_sem=self.send.at[slot],
            recv_sem=self.recv.at[slot],
            device_id=device,
            device_id_type=pl.DeviceIdType.MESH,
        )
        copy.start()
        self.open.append(copy)

    def arrived(self, dst, slot):
        pltpu.make_async_remote_copy(
            src_ref=dst,
            dst_ref=dst,
            send_sem=self.send.at[slot],
            recv_sem=self.recv.at[slot],
            device_id=self.me,
            device_id_type=pl.DeviceIdType.MESH,
        ).wait_recv()

    def close(self):
        for copy in self.open:
            copy.wait_send()


def coords():
    return (
        lax.axis_index("z"),
        lax.axis_index("x"),
        lax.axis_index("y"),
        lax.axis_index("tp"),
    )


class Plane:
    def __init__(self, out, copies, rows, relay):
        self.out, self.copies, self.half, self.relay = out, copies, rows // 2, relay
        z, x, y, c = coords()
        self.y, self.c = y, c
        self.a = x * (1 - c) + z * c
        self.b = z * (1 - c) + x * c

    def at(self, da, db):
        a = (self.a + da + 8) % 4
        b = (self.b + db + 8) % 4
        c = self.c
        return b * (1 - c) + a * c, a * (1 - c) + b * c

    def device(self, da, db):
        z, x = self.at(da, db)
        return (z, x, self.y, self.c)

    def full(self, d, db=0):
        z, x = self.at(-d, db)
        return self.out.at[z * 4 + x]

    def low(self, d, db):
        z, x = self.at(-d, db)
        return self.out.at[z * 4 + x, pl.ds(0, self.half)]

    def high(self, d, db):
        z, x = self.at(-d, db)
        return self.out.at[z * 4 + x, pl.ds(self.half, self.half)]

    def first(self, own):
        for d in (1, 3, 2):
            self.copies.go(own, self.full(0), d - 1, self.device(d, 0))
        self.second(0, own)

    def second(self, d, src=None):
        src = self.full(d) if src is None else src
        self.copies.go(src, self.full(d), 3 + 4 * d, self.device(0, 1))
        self.copies.go(src, self.full(d), 4 + 4 * d, self.device(0, -1))
        if d not in self.relay:
            self.copies.go(src, self.full(d), 5 + 4 * d, self.device(0, 2))

    def turn(self, d):
        self.copies.arrived(self.full(d), d - 1)
        self.second(d)

    def pass_on(self, d):
        self.copies.arrived(self.full(d, -1), 3 + 4 * d)
        if d in self.relay:
            self.copies.go(self.low(d, -1), self.low(d, -1), 5 + 4 * d, self.device(0, 1))
        self.copies.arrived(self.full(d, 1), 4 + 4 * d)
        if d in self.relay:
            self.copies.go(self.high(d, 1), self.high(d, 1), 6 + 4 * d, self.device(0, -1))

    def end(self, d):
        if d in self.relay:
            self.copies.arrived(self.low(d, 2), 5 + 4 * d)
            self.copies.arrived(self.high(d, 2), 6 + 4 * d)
        else:
            self.copies.arrived(self.full(d, 2), 5 + 4 * d)


def pack(width):
    row = lax.broadcasted_iota(jnp.int32, (96, 128), 0)
    col = lax.broadcasted_iota(jnp.int32, (96, 128), 1)
    padded = 128 // (96 // width)
    return (col == row // width * padded + row % width).astype(F32).astype(BF)


UNIT = 1024
COPY = dict(
    stage=7, ostage=3, hid=6, cross=4, w=19, edge=1, wo=19, bc=2,
    part=15, back=15, page=3, decay=3, mate=4, ring=6, sum=7, state=3,
)


def buffers(d):
    vmem = pltpu.VMEM
    return dict(
        hidden=vmem((128, d), BF),
        gate_w=vmem((12, DI), F32),
        inner_w=vmem((12, DI), F32),
        small_w=vmem((12, 304), F32),
        cinner=vmem((4, CH), F32),
        cshared=vmem((4, 2 * N), F32),
        binner=vmem((1, CH), F32),
        ngain=vmem((1, CH), F32),
        dtb=vmem((1, 24), F32),
        rates_log=vmem((1, 24), F32),
        skip=vmem((1, 24), F32),
        layout=vmem((1, 128), jnp.int32),
        bshared=vmem((1, 2 * N), F32),
        out_w=vmem((24, d), F32),
        lens=pltpu.SMEM((8,), jnp.int32),
        grps=pltpu.SMEM((8,), jnp.int32),
        pt=pltpu.SMEM((2,), jnp.int32),
        pieces=vmem((8, 16, UNIT), BF),
        stage=vmem((8, 16, UNIT), BF),
        unit=vmem((96, UNIT), BF),
        half=vmem((128, d), BF),
        w=vmem((16, 96, UNIT), BF),
        hid=vmem((8, 128, d), BF),
        edge=vmem((16, d), BF),
        initf=vmem((4, CH, N), F32),
        initb=vmem((CH, 4 * N), BF),
        sg=vmem((1024, CH), F32),
        xs=vmem((1032, CH + 2 * N), F32),
        steps=vmem((1024, 128), BF),
        y=vmem((1024, CH), F32),
        xdt=vmem((1024, CH), BF),
        b=vmem((1024, N), BF),
        c=vmem((1024, N), BF),
        cum=vmem((1024, 128), F32),
        fx=vmem((1024, CH), F32),
        fac=vmem((1024, 128), F32),
        small=vmem((9, CH, N), BF),
        dps=vmem((8, 8, N), F32),
        carries=vmem((4, CH, N), BF),
        pages=vmem((4, 2, CH, N), BF),
        rates=vmem((4, 2, 8, N), F32),
        bc=vmem((2, 1040, N), BF),
        state=vmem((16, 4, 8, N), F32),
        parts=vmem((16, 4, 8, N), F32),
        befores=vmem((16, 3, 8, N), F32),
        carry=vmem((16, 3, 8, N), F32),
        outp=vmem((4, 32, CH), BF),
        ostage=vmem((4, 32, CH), BF),
        ounit=vmem((96, CH), BF),
        wo=vmem((16, 96, CH), BF),
        opp=vmem((128, d), BF),
        ahead=vmem((128, d), BF),
        behind=vmem((128, d), BF),
        own=vmem((128, d), BF),
        xs_out=vmem((4, 128, d), BF),
        xs_in=vmem((4, 128, d), BF),
        low=vmem((64, d), BF),
        high=vmem((64, d), BF),
        from_l=vmem((128, d), BF),
        from_r=vmem((128, d), BF),
        sq=vmem((8, 8, 128), F32),
        sqr=vmem((8, 8, 128), F32),
        snaps=vmem((2, 4, CH, N), F32),
        res=vmem((128, d), BF),
    )


def layer_kernel(
    hidden_h, gate_h, inner_h, small_h, cinner_h, cshared_h, binner_h, ngain_h, out_h,
    dtb_h, rates_h, skip_h, layout_h, bshared_h,
    lens_h, grps_h, pt_h, init, out_o, page_o, *refs,
):
    d = hidden_h.shape[1]
    names = list(buffers(d))
    r = SimpleNamespace(**dict(zip(names, refs)))
    sems = refs[len(names):]
    z, x, y, c = coords()
    me_not = (z, x, y, 1 - c)
    cp = SimpleNamespace()
    for i, name in enumerate(COPY):
        setattr(cp, name, Copies(sems[2 * i], sems[2 * i + 1]))
        getattr(cp, name).me = me_not
    local = sems[2 * len(COPY)]
    q = y * 2 + c
    g = z * 4 + x
    mate = me_not
    right, left = (z, x, (y + 1) % 4, c), (z, x, (y + 3) % 4, c)
    near = [(z, x, (y + k) % 4, c) for k in range(1, 4)]
    group = [(z, x, ((q + k) % 8) // 2, (q + k) % 2) for k in range(1, 8)]
    peers = [(((g + k) % 16) // 4, ((g + k) % 16) % 4, y, c) for k in range(1, 16)]
    next_dev = peers[0]
    barrier = pltpu.get_barrier_semaphore()
    for device in group + peers:
        pl.semaphore_signal(
            barrier, inc=1, device_id=device, device_id_type=pl.DeviceIdType.MESH
        )

    mychan = pl.ds(pl.multiple_of(y * CH, CH), CH)
    loads = dict(
        gate_w=gate_h,
        inner_w=inner_h,
        small_w=small_h,
        hidden=hidden_h.at[pl.ds(pl.multiple_of(c * 128, 128), 128)],
        out_w=out_h,
        dtb=dtb_h,
        rates_log=rates_h,
        skip=skip_h,
        layout=layout_h,
        bshared=bshared_h,
        binner=binner_h.at[mychan],
        ngain=ngain_h.at[mychan],
        cinner=cinner_h.at[:, mychan],
        cshared=cshared_h,
        lens=lens_h,
        grps=grps_h,
        pt=pt_h,
        initf=init.at[:, mychan],
    )
    load = SimpleNamespace()
    for i, name in enumerate(loads):
        to = getattr(r, name)
        if loads[name].ndim == 1 and to.shape[0] == 1:
            to = to.at[0]
        setattr(load, name, pltpu.make_async_copy(loads[name], to, local.at[2 + i]))
        getattr(load, name).start()
    gate_w, inner_w, small_w, hidden = r.gate_w, r.inner_w, r.small_w, r.hidden
    cinner, cshared = r.cinner, r.cshared
    lens, grps, outp = r.lens, r.grps, r.outp
    pieces, stage = r.pieces, r.stage
    outp[...] = jnp.zeros_like(outp)
    pieces[...] = jnp.zeros_like(pieces)
    for one in (load.gate_w, load.inner_w, load.small_w, load.out_w):
        one.wait()
    for t in range(4):
        outp[t, 0:24, :] = r.out_w[:, t * CH : t * CH + CH].astype(BF)
    for t in range(8):
        a = 1536 * (t % 2) + CH * (t // 2)
        pieces[t, 0:12, 0:CH] = gate_w[:, a : a + CH].astype(BF)
        pieces[t, 0:12, CH : 2 * CH] = inner_w[:, a : a + CH].astype(BF)
        b = N * (t % 2)
        pieces[t, 0:12, 2 * CH : 2 * CH + N] = small_w[:, b : b + N].astype(BF)
        pieces[t, 0:12, 2 * CH + N : 2 * CH + N + 48] = small_w[:, 2 * N :].astype(BF)
    half = r.half
    load.layout.wait()
    load.hidden.wait()
    lay = jnp.broadcast_to(r.layout[...], (8, 128)).astype(F32).astype(BF)
    rows = hidden[...]
    for j in range(0, d, CH):
        brow = lax.broadcasted_iota(jnp.int32, (128, CH), 0)
        bcol = lax.broadcasted_iota(jnp.int32, (128, CH), 1) + j
        block = dot(lay, (brow == bcol // 12).astype(F32).astype(BF))[0:1]
        want = block * 12.0 + (bcol[0:1] % 12).astype(F32)
        frow = lax.broadcasted_iota(jnp.int32, (d, CH), 0).astype(F32)
        pick = jnp.where(frow == want, 1.0, 0.0).astype(BF)
        half[:, j : j + CH] = dot(rows, pick).astype(BF)
    pl.semaphore_wait(barrier, len(group) + len(peers))

    for k in range(1, 8):
        cp.stage.go(pieces.at[(q + k) % 8], stage.at[q], k - 1, group[k - 1])
    stage[q] = pieces[q]
    r.ostage[y] = outp[y]

    hid = r.hid

    def hslot(dy, core):
        return ((y + dy + 4) % 4) * 2 + core

    def hpart(dy, low):
        return hid.at[hslot(dy, c), pl.ds(0 if low else 64, 64)]

    lo, hi = pl.ds(0, 64), pl.ds(64, 64)
    cp.hid.go(half.at[lo], hpart(0, True), 0, right)
    cp.hid.go(half.at[hi], hpart(0, False), 2, left)
    cp.hid.go(half.at[hi], hpart(0, False), 1, right)
    cp.hid.go(half.at[lo], hpart(0, True), 3, left)
    cp.cross.go(half, hid.at[hslot(0, c)], 0, mate)
    hid[q] = half[...]

    for k in range(1, 8):
        cp.stage.arrived(stage.at[(q + 8 - k) % 8], k - 1)
    packer = pack(12)
    for j in range(0, UNIT, 512):
        r.unit[:, j : j + 512] = dot(
            packer, stage[:, :, j : j + 512].reshape(128, 512)
        ).astype(BF)
    ring = Plane(r.w, cp.w, 96, (0, 1, 3))
    ring.first(r.unit)
    mine = pltpu.make_async_copy(r.unit, r.w.at[g], local.at[1])
    mine.start()
    for one in (load.dtb, load.rates_log, load.skip, load.bshared):
        one.wait()
    for one in (load.initf, load.cinner, load.cshared, load.binner, load.ngain, load.lens, load.grps, load.pt):
        one.wait()
    for k in range(4):
        r.initb[:, k * N : k * N + N] = r.initf[k].astype(BF)

    cp.hid.arrived(hpart(-1, True), 0)
    cp.hid.go(hpart(-1, True), hpart(-1, True), 4, right)
    cp.hid.arrived(hpart(1, False), 2)
    cp.hid.go(hpart(1, False), hpart(1, False), 5, left)
    for k in range(1, 4):
        cp.ostage.go(outp.at[(y + k) % 4], r.ostage.at[y], k - 1, near[k - 1])
    ring.turn(1)
    ring.turn(3)
    ring.turn(2)
    ring.pass_on(0)
    cp.hid.arrived(hpart(-1, False), 1)
    cp.cross.go(hid.at[hslot(-1, c)], hid.at[hslot(-1, c)], 1, mate)
    cp.hid.arrived(hpart(1, True), 3)
    cp.cross.go(hid.at[hslot(1, c)], hid.at[hslot(1, c)], 2, mate)
    ring.pass_on(1)
    ring.pass_on(3)
    oring = Plane(r.wo, cp.wo, 96, ())
    cp.hid.arrived(hpart(2, True), 4)
    cp.hid.arrived(hpart(2, False), 5)
    cp.cross.go(hid.at[hslot(2, c)], hid.at[hslot(2, c)], 3, mate)
    for k, dy in enumerate((0, -1, 1, 2)):
        cp.cross.arrived(hid.at[hslot(dy, 1 - c)], k)
    cp.edge.go(hid.at[7, pl.ds(112, 16)], r.edge, 0, next_dev)
    for k in range(1, 4):
        cp.ostage.arrived(r.ostage.at[(y + 4 - k) % 4], k - 1)
    r.ounit[...] = dot(pack(24), r.ostage[...].reshape(128, CH)).astype(BF)
    ring.pass_on(2)
    for k in range(4):
        ring.end(k)
    mine.wait()
    oring.first(r.ounit)
    mine = pltpu.make_async_copy(r.ounit, r.wo.at[g], local.at[1])
    mine.start()

    w, xs, bc, steps, sg = r.w, r.xs, r.bc, r.steps, r.sg

    def columns(a, z):
        return w[:, :, a:z].reshape(d, z - a)

    def project_bc(i, _):
        at = pl.multiple_of(i * 256, 256)
        got = dot(hid[pl.ds(i * 2, 2)].reshape(256, d), columns(2 * CH, UNIT)).astype(BF)
        bc[c, pl.ds(pl.multiple_of(at + 16, 16), 256), :] = got[:, :N]
        steps[pl.ds(at, 256), :] = got[:, N:]
        return 0

    lax.fori_loop(0, 4, project_bc, 0)
    mid = pl.ds(16, 1024)
    cp.bc.go(bc.at[c, mid], bc.at[c, mid], 0, mate)

    def project(i, _):
        at = pl.multiple_of(i * 256, 256)
        got = dot(hid[pl.ds(i * 2, 2)].reshape(256, d), columns(0, 2 * CH)).astype(BF)
        sg[pl.ds(at, 256), :] = got[:, :CH].astype(F32)
        xs[pl.ds(pl.multiple_of(at + 8, 8), 256), 0:CH] = got[:, CH:].astype(F32)
        return 0

    lax.fori_loop(0, 2, project, 0)
    cp.edge.arrived(r.edge, 0)
    bc[c, 0:16, :] = dot(r.edge[...], columns(2 * CH, 2 * CH + N)).astype(BF)
    cp.bc.go(bc.at[c, pl.ds(0, 16)], bc.at[c, pl.ds(0, 16)], 1, mate)
    xs[0:8, 0:CH] = dot(r.edge[...], columns(CH, 2 * CH))[8:16].astype(BF).astype(F32)
    lax.fori_loop(2, 4, project, 0)
    for k in (1, 3, 2):
        oring.turn(k)
    cp.bc.arrived(bc.at[1 - c, mid], 0)
    cp.bc.arrived(bc.at[1 - c, pl.ds(0, 16)], 1)
    for k in range(2):
        xs[0:8, CH + k * N : CH + k * N + N] = bc[k, 0:16, :].astype(F32)[8:16]
        xs[8:1032, CH + k * N : CH + k * N + N] = bc[k, 16:1040, :].astype(F32)

    hot = head_hot()
    starts = []
    total = jnp.int32(0)
    for k in range(8):
        starts.append(total)
        total = total + lens[k]
    row = lax.broadcasted_iota(jnp.int32, (128, 128), 0)
    col = lax.broadcasted_iota(jnp.int32, (128, 128), 1)
    head0 = c * 24 + y * MINE
    pick = jnp.where(col < MINE, (row == col + head0).astype(F32), 0.0).astype(BF)
    wrow = lax.broadcasted_iota(jnp.int32, (128, CH), 0)
    wcol = lax.broadcasted_iota(jnp.int32, (128, CH), 1)
    pickx = (wrow == wcol // HEAD + head0).astype(F32).astype(BF)

    def take(ref):
        at = jnp.where(col < MINE, (row == col + y * MINE).astype(F32), 0.0).astype(BF)[0:32]
        wide_v = jnp.concatenate([jnp.broadcast_to(ref[...], (8, 24)), jnp.zeros((8, 8), F32)], axis=1)
        return sum(dot(part, at) for part in three(wide_v))[0:1]

    def takex(ref):
        at = (wrow == wcol // HEAD + y * MINE).astype(F32).astype(BF)[0:32]
        wide_v = jnp.concatenate([jnp.broadcast_to(ref[...], (8, 24)), jnp.zeros((8, 8), F32)], axis=1)
        return sum(dot(part, at) for part in three(wide_v))[0:1]

    rate6 = jnp.where(col[0:1] < MINE, -jnp.exp(take(r.rates_log)), 0.0)
    bias6, biasx, skipx = take(r.dtb), takex(r.dtb), takex(r.skip)
    taps = cinner[...]
    biasc = r.binner[...]
    small, dps = r.small, r.dps
    small[0] = jnp.zeros((CH, N), BF)

    def find(pos):
        first = jnp.zeros(pos.shape, jnp.int32)
        for k in range(1, 8):
            first = jnp.where(pos >= starts[k], starts[k], first)
        return first

    def advance(i, held):
        old, dp, dprow = held
        at = pl.multiple_of(i * 256, 256)
        base = g * 1024 + i * 256
        first = find(base + lax.broadcasted_iota(jnp.int32, (256, 128), 0))
        off = base + lax.broadcasted_iota(jnp.int32, (256, 128), 0) - first
        xc = biasc + jnp.zeros((256, CH), F32)
        bv = r.bshared[:, :N] + jnp.zeros((256, N), F32)
        window = xs[pl.ds(at, 264), : CH + N]
        for lag in range(CONV):
            ok = (off >= lag).astype(F32)
            part = window[8 - lag : 264 - lag, :]
            xc = xc + taps[lag : lag + 1, :] * part[:, :CH] * wide(ok)
            bv = bv + cshared[lag : lag + 1, :N] * part[:, CH : CH + N] * ok
        xc = silu(xc)
        b_all = silu(bv).astype(BF)
        r.b[pl.ds(at, 256), :] = b_all
        step = steps[pl.ds(at, 256), :]
        dt6 = softplus(dot(step, pick) + bias6)
        log6 = rate6 * dt6
        dtx = softplus(dot(step, pickx) + biasx)
        xdt_all = xc * dtx
        r.xdt[pl.ds(at, 256), :] = xdt_all.astype(BF)
        r.y[pl.ds(at, 256), :] = skipx * xc
        for sub in range(2):
            k = i * 2 + sub
            p0 = base + sub * 128
            rows = slice(sub * 128, sub * 128 + 128)
            f0 = first[rows, :]
            mask = (row >= col) & (f0 == find(p0 + col))
            maskb = mask.astype(F32).astype(BF)
            cum = sum(dot(maskb, part) for part in three(log6[rows, :]))
            there = pl.ds(pl.multiple_of(at + sub * 128, 128), 128)
            r.cum[there, :] = cum
            cumt = cum.T
            flast = jnp.int32(0)
            glast = grps[0]
            for j in range(1, 8):
                got = p0 + 127 >= starts[j]
                flast = jnp.where(got, starts[j], flast)
                glast = jnp.where(got, grps[j], glast)
            w6 = jnp.exp(jnp.where(f0 == flast, cum[127:128, :] - cum, NEG))
            xw = (xdt_all[rows, :] * expand(w6, hot)).astype(BF)
            summary = dot_tn(xw, b_all[rows, :])
            keep = (flast < p0).astype(F32)
            ecum = jnp.exp(cum)
            r.fac[there, :] = jnp.where(f0 < p0, ecum, 0.0) * dprow
            scale = jnp.exp(jnp.broadcast_to(cumt[0:8, 127:128], (8, 128)))
            dp = dp * scale * keep
            dprow = dprow * jnp.exp(cum[127:128, :]) * keep
            dps[k] = dp
            start = r.initf[0]
            for j in range(1, 4):
                start = jnp.where(glast == j, r.initf[j], start)
            old = jnp.where(flast < p0, old, start)
            old = jnp.concatenate(
                [scale[h : h + 1, :] * old[h * HEAD : h * HEAD + HEAD, :] for h in range(MINE)], axis=0
            ) + summary
            small[k + 1] = old.astype(BF)
        return old, dp, dprow

    held = (jnp.zeros((CH, N), F32), jnp.ones((8, 128), F32), jnp.ones((1, 128), F32))
    last, dplast, _ = lax.fori_loop(0, 4, advance, held, unroll=2)

    state, parts, befores, carry = r.state, r.parts, r.befores, r.carry
    for j in range(3):
        state[:, j] = last[j * 128 : j * 128 + 128].reshape(16, 8, N)
    state[:, 3] = jnp.broadcast_to(dplast[None], (16, 8, N))
    for k in range(1, 16):
        cp.part.go(state.at[(g + k) % 16], parts.at[g], k - 1, peers[k - 1])
    parts[g] = state[g]
    for k in range(1, 4):
        t = (y + k) % 4
        cp.page.go(small.at[pl.ds(t * 2 + 1, 2)], r.pages.at[y], k - 1, near[k - 1])
        cp.decay.go(dps.at[pl.ds(t * 2, 2)], r.rates.at[y], k - 1, near[k - 1])
    for k in range(2):
        r.pages[y, k] = small[y * 2 + 1 + k]
        r.rates[y, k] = dps[y * 2 + k]

    def inside(i, _):
        first_at = pl.multiple_of(i * 256, 256)
        pos = g * 1024 + i * 256 + lax.broadcasted_iota(jnp.int32, (256, 128), 0)
        off = pos - find(pos)
        cv = r.bshared[:, N:] + jnp.zeros((256, N), F32)
        window = xs[pl.ds(first_at, 264), CH + N :]
        for lag in range(CONV):
            ok = (off >= lag).astype(F32)
            cv = cv + cshared[lag : lag + 1, N:] * window[8 - lag : 264 - lag, :] * ok
        c_all = silu(cv).astype(BF)
        r.c[pl.ds(first_at, 256), :] = c_all
        for sub in range(2):
            k = i * 2 + sub
            p0 = g * 1024 + k * 128
            at = pl.ds(pl.multiple_of(k * 128, 128), 128)
            f0 = find(p0 + row)
            mask = (row >= col) & (f0 == find(p0 + col))
            cum = r.cum[at, :]
            cumt = cum.T
            cb = c_all[sub * 128 : sub * 128 + 128, :]
            r.fx[at, :] = expand(r.fac[at, :], hot)
            cf = cb.astype(F32)
            scores = dot_nt(cb, r.b[at, :])
            gid = jnp.zeros((128, 128), jnp.int32) + grps[0]
            for j in range(1, 8):
                gid = jnp.where(p0 + row >= starts[j], grps[j], gid)
            gid = jnp.where(f0 < p0, 4, gid)
            chot = jnp.concatenate(
                [jnp.where(gid == j, cf, 0.0).astype(BF) for j in range(4)], axis=1
            )
            read = dot_nt(jnp.where(gid == 4, cf, 0.0).astype(BF), small[k])
            read = read + dot_nt(chot, r.initb[...])
            lane = col
            pieces = []
            for pair in range(3):
                xp = r.xdt[at, pair * 128 : pair * 128 + 128]
                got = []
                for h in (2 * pair, 2 * pair + 1):
                    diff = cum[:, h : h + 1] - cumt[h : h + 1, :]
                    mix = jnp.exp(jnp.where(mask, diff, NEG)) * scores
                    got.append(dot(mix.astype(BF), xp))
                pieces.append(jnp.where(lane < HEAD, got[0], got[1]))
            r.y[at, :] = (
                r.y[at, :] + expand(jnp.exp(cum), hot) * read + jnp.concatenate(pieces, axis=1)
            )
            sg[at, :] = silu(sg[at, :])
        return 0

    lax.fori_loop(0, 2, inside, 0)
    for k in range(1, 16):
        cp.part.arrived(parts.at[(g + 16 - k) % 16], k - 1)
    hb = g // 8
    run = [jnp.zeros((8, 128), F32) for _ in range(3)]
    for k in range(16):
        for j in range(3):
            befores[k, j] = run[j]
            run[j] = parts[k, 3, pl.ds(hb + 2 * j, 1), :] * run[j] + parts[k, j]
    for k in range(1, 16):
        cp.back.go(befores.at[(g + k) % 16], carry.at[g], k - 1, peers[k - 1])
    carry[g] = befores[g]
    lax.fori_loop(2, 4, inside, 0)
    for k in range(4):
        oring.pass_on(k)
        oring.end(k)
    mine.wait()
    for k in range(1, 16):
        cp.back.arrived(carry.at[(g + 16 - k) % 16], k - 1)

    carries = r.carries
    cs = jnp.concatenate([carry[:, j].reshape(128, N) for j in range(3)], axis=0).astype(BF)
    carries[y] = cs
    for k in range(1, 4):
        cp.state.go(carries.at[y], carries.at[y], k - 1, near[k - 1])
    ones = jnp.ones((8, CH), BF)
    gain = r.ngain[...]
    xs_out, xs_in, sq, sqr = r.xs_out, r.xs_in, r.sq, r.sqr

    def partial(dy, k, keep):
        t = (y + dy) % 4
        for part in range(2):
            core = c if part else 1 - c
            at = pl.ds(pl.multiple_of(t * 256 + core * 128, 128), 128)
            full = r.y[at, :] + r.fx[at, :] * dot_nt(r.c[at, :], cs)
            gv = full * sg[at, :]
            g2 = gv * gv
            top = g2.astype(BF)
            rest = (g2 - top.astype(F32)).astype(BF)
            sq[t * 2 + core] = dot_nt(ones, top) + dot_nt(ones, rest)
            gg = (gv * gain).astype(BF)
            for n in range(0, 1536, CH):
                got = dot_nt(gg, r.wo[n // 96 : n // 96 + 4].reshape(CH, CH)).astype(BF)
                if part:
                    keep[:, n : n + CH] = got
                else:
                    xs_out[k, :, n : n + CH] = got
            if not part:
                cp.mate.go(xs_out.at[k], xs_in.at[k], k, mate)

    def join(k, keep):
        cp.mate.arrived(xs_in.at[k], k)
        keep[...] = (keep[...].astype(F32) + xs_in[k].astype(F32)).astype(BF)

    opp, ahead, behind, own = r.opp, r.ahead, r.behind, r.own
    from_l, from_r = r.from_l, r.from_r
    partial(2, 0, opp)
    partial(1, 1, ahead)
    join(0, opp)
    cp.ring.go(opp.at[lo], r.low, 0, right)
    cp.ring.go(opp.at[hi], r.high, 1, left)
    partial(3, 2, behind)
    join(1, ahead)
    cp.ring.go(ahead.at[hi], from_l.at[hi], 2, right)
    join(2, behind)
    cp.ring.go(behind.at[lo], from_r.at[lo], 3, left)
    cp.ring.arrived(r.low, 0)
    ahead[0:64, :] = (ahead[0:64, :].astype(F32) + r.low[...].astype(F32)).astype(BF)
    cp.ring.go(ahead.at[lo], from_l.at[lo], 4, right)
    cp.ring.arrived(r.high, 1)
    behind[64:128, :] = (behind[64:128, :].astype(F32) + r.high[...].astype(F32)).astype(BF)
    cp.ring.go(behind.at[hi], from_r.at[hi], 5, left)
    partial(0, 3, own)
    for k in range(1, 8):
        cp.sum.go(sq.at[(q + k) % 8], sqr.at[q], k - 1, group[k - 1])
    sqr[q] = sq[q]
    join(3, own)

    swap = r.pt[0] != (g * 4 + y) * 2
    for k in range(4):
        t = (y + 4 - k) % 4
        if k:
            cp.state.arrived(carries.at[t], k - 1)
            cp.page.arrived(r.pages.at[t], k - 1)
            cp.decay.arrived(r.rates.at[t], k - 1)
        for h in range(MINE):
            at = slice(h * HEAD, h * HEAD + HEAD)
            into = carries[t, at, :].astype(F32)
            one, two = (
                r.pages[t, j, at, :].astype(F32) + r.rates[t, j, h : h + 1, :] * into
                for j in range(2)
            )
            r.snaps[0, t, at, :] = jnp.where(swap, two, one)
            r.snaps[1, t, at, :] = jnp.where(swap, one, two)

    snaps = pltpu.make_async_copy(r.snaps, page_o, local.at[0])
    snaps.start()

    for k in range(1, 8):
        cp.sum.arrived(sqr.at[(q + 8 - k) % 8], k - 1)
    total = sqr[0]
    for k in range(1, 8):
        total = total + sqr[k]
    scale = lax.rsqrt(total / DI + EPS)
    scale = jnp.broadcast_to(scale[0:1, :], (128, 128)).T
    cp.ring.arrived(from_l.at[hi], 2)
    cp.ring.arrived(from_r.at[lo], 3)
    cp.ring.arrived(from_l.at[lo], 4)
    cp.ring.arrived(from_r.at[hi], 5)
    for n in range(0, 1536, 128):
        cols = slice(n, n + 128)
        whole = sum(v[:, cols].astype(F32) for v in (own, from_l, from_r))
        r.res[:, cols] = (whole * scale).astype(BF)
    res = pltpu.make_async_copy(r.res, out_o, local.at[21])
    res.start()
    for part in vars(cp).values():
        part.close()
    for one in (snaps, res):
        one.wait()


def place_kernel(mixed, pages, mixed_o, pages_o, block, snaps, came, gone):
    moves = []
    for k in range(4):
        part = pl.ds(k * 32, 32)
        moves.append((mixed.at[part], block.at[part], mixed_o.at[part]))
    for k in range(8):
        part = (k // 4, k % 4)
        moves.append((pages.at[part], snaps.at[part], pages_o.at[part]))
    ins = [pltpu.make_async_copy(a, b, came.at[k]) for k, (a, b, _) in enumerate(moves)]
    outs = [pltpu.make_async_copy(b, o, gone.at[k]) for k, (_, b, o) in enumerate(moves)]
    for copy in ins:
        copy.start()
    for one, two in zip(ins, outs):
        one.wait()
        two.start()
    for copy in outs:
        copy.wait()


def on_device(
    hidden_in, gate_proj, inner_proj, small_proj, row_layout, conv_inner, conv_shared,
    bias_inner, bias_shared, dt_bias, decay_log, skip_gain, norm_gain, out_proj,
    prompt_lengths, group_map, init_states, page_table,
):
    d = hidden_in.shape[1]
    hbm = pl.BlockSpec(memory_space=pltpu.HBM)
    dma = pltpu.SemaphoreType.DMA
    scratch = list(buffers(d).values())
    for count in COPY.values():
        scratch += [dma((count,)), dma((count,))]
    mixed, pages = pl.pallas_call(
        layer_kernel,
        in_specs=[hbm] * 18,
        out_specs=[hbm, hbm],
        out_shape=[
            jax.ShapeDtypeStruct((128, d), BF),
            jax.ShapeDtypeStruct((2, 4, CH, N), F32),
        ],
        scratch_shapes=scratch + [dma((22,))],
        compiler_params=pltpu.CompilerParams(
            collective_id=0, has_side_effects=True, vmem_limit_bytes=60 << 20
        ),
        name="layer",
    )(
        hidden_in, gate_proj, inner_proj, small_proj, conv_inner, conv_shared, bias_inner, norm_gain, out_proj.T,
        dt_bias, decay_log, skip_gain, row_layout, bias_shared, prompt_lengths, group_map, page_table, init_states.reshape(4, 24 * HEAD, N),
    )
    mixed, pages = pl.pallas_call(
        place_kernel,
        in_specs=[hbm, hbm],
        out_specs=[hbm, hbm],
        out_shape=[
            jax.ShapeDtypeStruct((128, d), BF),
            jax.ShapeDtypeStruct((2, 4, CH, N), F32),
        ],
        scratch_shapes=[
            pltpu.VMEM((128, d), BF),
            pltpu.VMEM((2, 4, CH, N), F32),
            dma((12,)), dma((12,)),
        ],
        compiler_params=pltpu.CompilerParams(vmem_limit_bytes=60 << 20),
        name="place",
    )(mixed, pages)
    return (mixed, pages.reshape(2, 24, HEAD, N))


def solution(mesh):
    fine = Mesh(mesh.devices.reshape(4, 4, 4, 2), ("z", "x", "y", "tp"))
    seq = ("z", "x", "y")
    every = ("z", "x", "y", "tp")
    placed = (
        P(seq, None),
        P(every, None),
        P(every, None),
        P(every, None),
        P(),
        P(None, "tp"),
        P(),
        P("tp"),
        P(),
        P("tp"),
        P("tp"),
        P("tp"),
        P("tp"),
        P("tp", seq),
        P(),
        P(),
        P(None, "tp", None, None),
        P(seq),
    )
    return jax.shard_map(
        on_device,
        mesh=fine,
        in_specs=placed,
        out_specs=(P(every, None), P(seq, "tp", None, None)),
        check_vma=False,
    )
```
